128 devices in a mesh: gx: 8 (over y, core), gy: 4 (over z), gz: 4 (over x).
Axes of the slice: x: 4, y: 4, z: 4, core: 2. Of those that a mesh axis runs over, the one named last changes fastest.
Arguments:
- velocity: float32 [3, 64, 128, 512], P(None, 'gx', 'gz', 'gy'), may hold values from -4 to 4
- pressure: float32 [64, 128, 512], P('gx', 'gz', 'gy'), may hold values from -4 to 4
- viscosity: float32 [64, 128, 512], P('gx', 'gz', 'gy'), may hold values from 0.1 to 10
- body_force: float32 [3, 64, 128, 512], P(None, 'gx', 'gz', 'gy'), may hold values from -6 to 6
Outputs:
- velocity_out: float32 [3, 64, 128, 512], P(None, 'gx', 'gz', 'gy')
- pressure_out: float32 [64, 128, 512], P('gx', 'gz', 'gy')
The draws below stay inside these ranges and needn't reach their ends.
All inputs are finite; a program needn't handle non-finite values.
Results may differ from the reference program's by a relative error of at most 0.00002.
Values sent between devices are 32-bit elements; how exact they have to be, the bound alone decides.
A program may use at most 128 MiB of HBM per device.

```python
import math
import jax
import jax.numpy as jnp

PRE = 2
COARSE = 4
POST = 2
NX = 64
NY = 512
NZ = 128


def shard_levels(own_key, shape, split, least, largest):
    level, own = 1.0, jax.random.fold_in(own_key, 6)
    for dim, shards_of in split:
        steps = jnp.exp(jax.random.uniform(jax.random.fold_in(own, dim), (shards_of,), jnp.float32, least / len(split), largest / len(split)))
        level = level * jnp.repeat(steps, shape[dim] // shards_of).reshape([-1 if axis == dim else 1 for axis in range(len(shape))])
    return level


def bell_draw(key, shape, width, bound, cuts=(), held_as=jnp.bfloat16):
    factor_of = shard_levels(key, shape, cuts, -0.22, 0.18) if cuts else 1.0
    array = jax.random.normal(key, shape, jnp.float32) * width * factor_of
    return jnp.minimum(jnp.maximum(array, -bound), bound).astype(held_as)


def setup_inputs(seed: int = 0) -> dict:
    seeds = jax.random.split(jax.random.key(seed), 5)
    velocity = bell_draw(seeds[0], (3, NX, NZ, NY), 0.5, 4.0, ((1, 8), (2, 4), (3, 4)), jnp.float32)
    pressure = bell_draw(seeds[1], (NX, NZ, NY), 0.5, 4.0, ((0, 8), (1, 4), (2, 4)), jnp.float32)
    viscosity = jnp.clip(jnp.exp(math.log(10.0) - 4.6051702 * jax.random.uniform(seeds[2], (NX, NZ, NY), jnp.float32) ** shard_levels(seeds[2], (NX, NZ, NY), ((0, 8), (1, 4), (2, 4)), -0.2, 0.2)), 0.1, 10.0)
    body_force = bell_draw(seeds[3], (3, NX, NZ, NY), 1.0, 6.0, ((1, 8), (2, 4), (3, 4)), jnp.float32)
    return dict(velocity=velocity, pressure=pressure, viscosity=viscosity, body_force=body_force)


relax_weight = 0.6
uzawa_step = 0.5


def window(padded, spatial, offset):
    leading = padded.ndim - 3
    selection = [slice(None)] * leading
    for axis_id in range(3):
        extent = padded.shape[leading + axis_id]
        if axis_id == spatial:
            selection.append(slice(1 + offset, extent - 1 + offset))
        else:
            selection.append(slice(1, extent - 1))
    return padded[tuple(selection)]


def operator_terms(padded_fields, padded_visc, right_side, source, spacing):
    visc_cell = window(padded_visc, 0, 0)
    velocity = window(padded_fields[:3], 0, 0)
    inverse_sq = 1.0 / (spacing * spacing)
    half_inverse = 0.5 / spacing
    diagonal = jnp.zeros_like(visc_cell)
    viscous = jnp.zeros_like(velocity)
    divergence = jnp.zeros_like(visc_cell)
    gradients = []
    for spatial in range(3):
        for offset in (1, -1):
            face_visc = 0.5 * (visc_cell + window(padded_visc, spatial, offset))
            diagonal = diagonal + face_visc
            viscous = viscous + face_visc * (velocity - window(padded_fields[:3], spatial, offset))
        gradients.append((window(padded_fields[3], spatial, 1) - window(padded_fields[3], spatial, -1)) * half_inverse)
        divergence = divergence + (window(padded_fields[spatial], spatial, 1) - window(padded_fields[spatial], spatial, -1)) * half_inverse
    momentum = right_side - viscous * inverse_sq - jnp.stack(gradients)
    continuity = source - divergence
    return momentum, continuity, diagonal * inverse_sq, visc_cell


def relax_sweep(padded_fields, padded_visc, right_side, source, spacing):
    momentum, continuity, diagonal, visc_cell = operator_terms(padded_fields, padded_visc, right_side, source, spacing)
    velocity = window(padded_fields[:3], 0, 0)
    pressure = window(padded_fields[3], 0, 0)
    new_velocity = velocity + relax_weight * momentum / diagonal
    new_pressure = pressure + uzawa_step * visc_cell * continuity
    return jnp.concatenate([new_velocity, new_pressure[None]], axis=0)


def restrict(stacked):
    extents = stacked.shape
    blocks = stacked.reshape(extents[0], extents[1] // 2, 2, extents[2] // 2, 2, extents[3] // 2, 2)
    return blocks.mean(axis=(2, 4, 6))


def prolong(coarse_fields):
    return jnp.repeat(jnp.repeat(jnp.repeat(coarse_fields, 2, axis=1), 2, axis=2), 2, axis=3)


def pad_fields(fields):
    return jnp.pad(fields, ((0, 0), (1, 1), (1, 1), (1, 1)))


def reference(velocity, pressure, viscosity, body_force):
    padded_visc = jnp.pad(viscosity, 1)
    fields = jnp.concatenate([velocity, pressure[None]], axis=0)
    for repeat_index in range(PRE):
        fields = relax_sweep(pad_fields(fields), padded_visc, body_force, 0.0, 1.0)
    momentum, continuity, diagonal, visc_cell = operator_terms(pad_fields(fields), padded_visc, body_force, 0.0, 1.0)
    coarse = restrict(jnp.concatenate([momentum, continuity[None], viscosity[None]], axis=0))
    coarse_visc = jnp.pad(coarse[4], 1)
    correction = relax_sweep(pad_fields(jnp.zeros_like(coarse[:4])), coarse_visc, coarse[:3], coarse[3], 2.0)
    for repeat_index in range(COARSE - 1):
        correction = relax_sweep(pad_fields(correction), coarse_visc, coarse[:3], coarse[3], 2.0)
    fields = fields + prolong(correction)
    for repeat_index in range(POST):
        fields = relax_sweep(pad_fields(fields), padded_visc, body_force, 0.0, 1.0)
    return fields[:3], fields[3]
```

```python
import functools

import jax
import jax.numpy as jnp
from jax import lax
from jax.experimental import pallas as pl
from jax.experimental.pallas import tpu as pltpu
from jax.sharding import PartitionSpec as P

MESH = pl.DeviceIdType.MESH
F32 = jnp.float32
NX, NZ, NY = 8, 32, 128
CX, CZ = 4, 16
TOP = 8
AXES = ("gx", "gz", "gy")


def kernel(
    size, vel, prs, vis, frc, vout, pout,
    u0, u1, u2, u3, u4, visc, force, cvisc, c1, c2, c3,
    wts, scl, diag, rhs, cwts, cscl, crhs, tmp, out,
    ysend0, yrecv0, ysend, yrecv, csend, crecv,
    send_sem, recv_sem, load_sem, store_sem,
):
    where = {axis: lax.axis_index(axis) for axis in AXES}
    lane = lax.broadcasted_iota(jnp.int32, (8, NY), 1)
    even = lax.rem(lane, 2) == 0
    count = [0]
    pending = []

    def roll(value, shift):
        return pltpu.roll(value, shift, 1)

    def neighbours(axis):
        n = size[axis]
        me = where[axis]
        return lax.rem(me + 1, n), lax.rem(me + n - 1, n), me < n - 1, me > 0

    def pair(axis, high_face, low_halo, low_face, high_halo):
        upper, lower, has_upper, has_lower = neighbours(axis)
        slot = count[0]
        count[0] += 2

        def make(k, src, dst, device):
            return pltpu.make_async_remote_copy(
                src_ref=src, dst_ref=dst,
                send_sem=send_sem.at[slot + k], recv_sem=recv_sem.at[slot + k],
                device_id={axis: device}, device_id_type=MESH,
            )

        def up():
            return make(0, high_face, low_halo, upper)

        def down():
            return make(1, low_face, high_halo, lower)

        def start():
            @pl.when(has_upper)
            def _():
                up().start()

            @pl.when(has_lower)
            def _():
                down().start()

        def wait():
            @pl.when(has_lower)
            def _():
                up().wait_recv()

            @pl.when(has_upper)
            def _():
                down().wait_recv()

        def drain():
            @pl.when(has_upper)
            def _():
                up().wait_send()

            @pl.when(has_lower)
            def _():
                down().wait_send()

        pending.append(drain)
        return start, wait

    zs = pl.ds(TOP, NZ)

    def x_pair(u, source=None):
        if source is None:
            high, low = u.at[:, NX, zs, :], u.at[:, 1, zs, :]
        else:
            high, low = source
        return pair("gx", high, u.at[:, 0, zs, :], low, u.at[:, NX + 1, zs, :])

    def z_pair(u):
        xs = pl.ds(1, NX)
        return pair(
            "gz", u.at[:, xs, TOP + NZ - 1, :], u.at[:, xs, TOP - 1, :],
            u.at[:, xs, TOP, :], u.at[:, xs, TOP + NZ, :],
        )

    def y_pair(sent, received):
        return pair("gy", sent.at[1], received.at[0], sent.at[0], received.at[1])

    fine_planes = pl.ds(1, NX)
    loads = [
        pltpu.make_async_copy(vel, u0.at[0:3, fine_planes, zs, :], load_sem.at[0]),
        pltpu.make_async_copy(prs, u0.at[3, fine_planes, zs, :], load_sem.at[1]),
        pltpu.make_async_copy(vis, visc.at[fine_planes, zs, :], load_sem.at[2]),
        pltpu.make_async_copy(frc, force, load_sem.at[3]),
    ]
    for load in loads:
        load.start()

    barrier = pltpu.get_barrier_semaphore()
    total = jnp.int32(0)
    for axis in AXES:
        upper, lower, has_upper, has_lower = neighbours(axis)
        for device, has in ((upper, has_upper), (lower, has_lower)):
            @pl.when(has)
            def _():
                pl.semaphore_signal(barrier, inc=1, device_id={axis: device}, device_id_type=MESH)
            total = total + has.astype(jnp.int32)
    pl.semaphore_wait(barrier, total)

    first = [
        pair("gx", vel.at[:, NX - 1], u0.at[0:3, 0, zs, :], vel.at[:, 0], u0.at[0:3, NX + 1, zs, :]),
        pair("gx", prs.at[NX - 1], u0.at[3, 0, zs, :], prs.at[0], u0.at[3, NX + 1, zs, :]),
        pair("gx", vis.at[NX - 1], visc.at[0, zs, :], vis.at[0], visc.at[NX + 1, zs, :]),
    ]
    for start, _ in first:
        start()

    def zero(ref):
        ref[...] = jnp.zeros(ref.shape, F32)

    def edges(axis, low, high):
        @pl.when(where[axis] == 0)
        def _():
            for ref in low:
                zero(ref)

        @pl.when(where[axis] == size[axis] - 1)
        def _():
            for ref in high:
                zero(ref)

    fields = (u0, u1, u2, u3, u4)
    coarse = (c1, c2, c3)
    czs, cxs = pl.ds(TOP, CZ), pl.ds(1, CX)
    edges(
        "gx",
        [u.at[:, 0, zs, :] for u in fields] + [visc.at[0, zs, :], cvisc.at[0, czs, :]]
        + [c.at[:, 0, czs, :] for c in coarse],
        [u.at[:, NX + 1, zs, :] for u in fields] + [visc.at[NX + 1, zs, :], cvisc.at[CX + 1, czs, :]]
        + [c.at[:, CX + 1, czs, :] for c in coarse],
    )
    edges(
        "gz",
        [u.at[:, fine_planes, TOP - 1 : TOP, :] for u in fields]
        + [visc.at[fine_planes, TOP - 1 : TOP, :], cvisc.at[cxs, TOP - 1 : TOP, :]]
        + [c.at[:, cxs, TOP - 1 : TOP, :] for c in coarse],
        [u.at[:, fine_planes, TOP + NZ : TOP + NZ + 1, :] for u in fields]
        + [visc.at[fine_planes, TOP + NZ : TOP + NZ + 1, :], cvisc.at[cxs, TOP + CZ : TOP + CZ + 1, :]]
        + [c.at[:, cxs, TOP + CZ : TOP + CZ + 1, :] for c in coarse],
    )
    edges(
        "gy",
        [yrecv0.at[0]] + [yrecv.at[s, 0] for s in range(4)] + [crecv.at[s, 0] for s in range(3)],
        [yrecv0.at[1]] + [yrecv.at[s, 1] for s in range(4)] + [crecv.at[s, 1] for s in range(3)],
    )

    for load in loads[:3]:
        load.wait()
    more = [
        z_pair(u0),
        pair(
            "gz", visc.at[fine_planes, TOP + NZ - 1, :], visc.at[fine_planes, TOP - 1, :],
            visc.at[fine_planes, TOP, :], visc.at[fine_planes, TOP + NZ, :],
        ),
    ]
    for start, _ in more:
        start()
    first += more

    def slot_of(k, i, t):
        return t * 32 + k * 8 + i

    def put(packs, value, slot):
        low, high = packs
        here = lane == slot
        low = jnp.where(here, roll(value, slot), low)
        high = jnp.where(here, roll(value, lax.rem(slot + 1, NY)), high)
        return low, high

    def y_shifts(value, packs, slot):
        low, high = packs
        before = jnp.where(lane == 0, roll(low, lax.rem(NY - slot, NY)), roll(value, 1))
        after = jnp.where(lane == NY - 1, roll(high, NY - 1 - slot), roll(value, NY - 1))
        return before, after

    nil = jnp.zeros((8, NY), F32)

    def cslot(k, i, t):
        return 2 * (t * 16 + k * 4 + i)

    def put2(packs, value, slot):
        low, high = packs
        here = (lane == slot) | (lane == slot + 1)
        low = jnp.where(here, roll(value, slot), low)
        high = jnp.where(here, roll(value, (slot + 2) % NY), high)
        return low, high

    def y_shifts2(value, packs, slot):
        low, high = packs
        before = jnp.where(lane < 2, roll(low, (NY - slot) % NY), roll(value, 2))
        after = jnp.where(lane >= NY - 2, roll(high, NY - 2 - slot), roll(value, NY - 2))
        return before, after

    def halves(i, t, source):
        return source[i, pl.ds(TOP + 8 * t, 8), :]

    def first_pack(i, carry):
        fields_pack, visc_pack = (carry[0], carry[1]), (carry[2], carry[3])
        for t in range(4):
            rows = pl.ds(TOP + 8 * t, 8)
            for k in range(4):
                fields_pack = put(fields_pack, u0[k, i + 1, rows, :], slot_of(k, i, t))
            visc_pack = put(visc_pack, visc[i + 1, rows, :], t * 8 + i)
        return (*fields_pack, *visc_pack)

    fl, fh, vl, vh = lax.fori_loop(0, NX, first_pack, (nil, nil, nil, nil))

    def pair_sum(value):
        return value + jnp.where(even, roll(value, NY - 1), roll(value, 1))

    def z_pairs(ref, t):
        return ref[pl.ds(16 * t, 8, stride=2), :] + ref[pl.ds(16 * t + 1, 8, stride=2), :]

    cpack = (vl, vh)
    for i in range(CX):
        for t in range(4):
            rows = pl.ds(TOP + 8 * t, 8)
            tmp[0, i, pl.ds(8 * t, 8), :] = pair_sum(visc[2 * i + 1, rows, :] + visc[2 * i + 2, rows, :])
        for t in range(2):
            mean = 0.125 * z_pairs(tmp.at[0, i], t)
            cvisc[i + 1, pl.ds(TOP + 8 * t, 8), :] = mean
            cpack = put2(cpack, mean, 64 + 2 * (t * 4 + i))
    ysend0[0, 0], ysend0[1, 0] = fl, fh
    ysend0[0, 1], ysend0[1, 1] = cpack
    more = [
        y_pair(ysend0, yrecv0),
        pair("gx", cvisc.at[CX, czs, :], cvisc.at[0, czs, :], cvisc.at[1, czs, :], cvisc.at[CX + 1, czs, :]),
        pair(
            "gz", cvisc.at[cxs, TOP + CZ - 1, :], cvisc.at[cxs, TOP - 1, :],
            cvisc.at[cxs, TOP, :], cvisc.at[cxs, TOP + CZ, :],
        ),
    ]
    for start, _ in more:
        start()
    first += more
    loads[3].wait()
    for _, wait in first:
        wait()

    def stencil_weights(here, around):
        sums = [here + other for other in around]
        twice = sums[0] + sums[1] + sums[2] + sums[3] + sums[4] + sums[5]
        scale = 0.6 / twice
        return scale, [scale * s for s in sums], twice

    def weights(i, _):
        packs = (yrecv0[0, 1], yrecv0[1, 1])
        for t in range(4):
            r = TOP + 8 * t
            here = visc[i + 1, pl.ds(r, 8), :]
            before, after = y_shifts(here, packs, t * 8 + i)
            around = (
                visc[i, pl.ds(r, 8), :], visc[i + 2, pl.ds(r, 8), :],
                visc[i + 1, pl.ds(r - 1, 8), :], visc[i + 1, pl.ds(r + 1, 8), :],
                before, after,
            )
            scale, sides, twice = stencil_weights(here, around)
            rows = pl.ds(8 * t, 8)
            for j in range(6):
                wts[j, i, rows, :] = sides[j]
            scl[i, rows, :] = scale
            diag[i, rows, :] = twice * (0.5 / 0.6)
            for k in range(3):
                rhs[k, i, rows, :] = (2.0 * scale) * force[k, i, rows, :]
        return 0

    def coarse_weights():
        packs = (yrecv0[0, 1], yrecv0[1, 1])
        for i in range(CX):
            for t in range(2):
                r = TOP + 8 * t
                here = cvisc[i + 1, pl.ds(r, 8), :]
                before, after = y_shifts2(here, packs, 64 + 2 * (t * 4 + i))
                around = (
                    cvisc[i, pl.ds(r, 8), :], cvisc[i + 2, pl.ds(r, 8), :],
                    cvisc[i + 1, pl.ds(r - 1, 8), :], cvisc[i + 1, pl.ds(r + 1, 8), :],
                    before, after,
                )
                scale, sides, _ = stencil_weights(here, around)
                rows = pl.ds(8 * t, 8)
                for j in range(6):
                    cwts[j, i, rows, :] = sides[j]
                cscl[i, rows, :] = scale

    lax.fori_loop(0, NX, weights, 0)

    def terms(here, around, sides, grad_scale):
        moves, spread = [], None
        for k in range(3):
            total = sides[0] * around[0][k]
            for j in range(1, 6):
                total = total + sides[j] * around[j][k]
            moves.append(total - grad_scale * (around[2 * k + 1][3] - around[2 * k][3]))
            d = around[2 * k + 1][k] - around[2 * k][k]
            spread = d if spread is None else spread + d
        return moves, spread

    def fine_terms(u, packs, i, t):
        r = TOP + 8 * t
        rows = pl.ds(8 * t, 8)
        here = [u[k, i + 1, pl.ds(r, 8), :] for k in range(4)]
        ys = [y_shifts(here[k], packs, slot_of(k, i, t)) for k in range(4)]
        around = (
            [u[k, i, pl.ds(r, 8), :] for k in range(4)],
            [u[k, i + 2, pl.ds(r, 8), :] for k in range(4)],
            [u[k, i + 1, pl.ds(r - 1, 8), :] for k in range(4)],
            [u[k, i + 1, pl.ds(r + 1, 8), :] for k in range(4)],
            [y[0] for y in ys],
            [y[1] for y in ys],
        )
        sides = [wts[j, i, rows, :] for j in range(6)]
        moves, spread = terms(here, around, sides, scl[i, rows, :])
        moves = [m + rhs[k, i, rows, :] for k, m in enumerate(moves)]
        return here, moves, spread

    def fine_update(u, packs, i, t):
        here, moves, spread = fine_terms(u, packs, i, t)
        new = [0.4 * here[k] + moves[k] for k in range(3)]
        new.append(here[3] - 0.25 * (visc[i + 1, pl.ds(TOP + 8 * t, 8), :] * spread))
        return new

    def order(j):
        return jnp.where(j == 1, NX - 1, jnp.maximum(j - 1, 0))

    def exchange(u, make, sent, received):
        def body(j, packs):
            i = order(j)
            for t in range(4):
                new = make(i, t)
                for k in range(4):
                    u[k, i + 1, pl.ds(TOP + 8 * t, 8), :] = new[k]
                    packs = put(packs, new[k], slot_of(k, i, t))
            return packs

        packs = lax.fori_loop(0, 2, body, (nil, nil))
        x_start, x_wait = x_pair(u)
        x_start()
        packs = lax.fori_loop(2, NX, body, packs)
        sent[0], sent[1] = packs
        z_start, z_wait = z_pair(u)
        z_start()
        y_start, y_wait = y_pair(sent, received)
        y_start()

        def wait():
            x_wait()
            z_wait()
            y_wait()

        return wait

    packs = (yrecv0[0, 0], yrecv0[1, 0])
    wait = exchange(u1, lambda i, t: fine_update(u0, packs, i, t), ysend.at[0], yrecv.at[0])
    coarse_weights()
    wait()
    packs1 = (yrecv[0, 0], yrecv[0, 1])
    wait = exchange(u2, lambda i, t: fine_update(u1, packs1, i, t), ysend.at[1], yrecv.at[1])
    wait()

    packs2 = (yrecv[1, 0], yrecv[1, 1])

    def restrict(i, _):
        for t in range(4):
            sums = None
            for h in range(2):
                here, moves, spread = fine_terms(u2, packs2, 2 * i + h, t)
                d = diag[2 * i + h, pl.ds(8 * t, 8), :]
                parts = [d * (moves[k] - 0.6 * here[k]) for k in range(3)] + [spread]
                sums = parts if sums is None else [a + b for a, b in zip(sums, parts)]
            for k in range(4):
                tmp[k, i, pl.ds(8 * t, 8), :] = pair_sum(sums[k])
        return 0

    lax.fori_loop(0, CX, restrict, 0)

    def coarse_exchange(c, values, sent, received):
        packs = (nil, nil)
        for i in (0, CX - 1, 1, CX - 2):
            for t in range(2):
                new = values(i, t)
                for k in range(4):
                    c[k, i + 1, pl.ds(TOP + 8 * t, 8), :] = new[k]
                    packs = put2(packs, new[k], cslot(k, i, t))
        sent[0], sent[1] = packs
        copies = [
            pair(
                "gx", c.at[:, CX, czs, :], c.at[:, 0, czs, :], c.at[:, 1, czs, :], c.at[:, CX + 1, czs, :],
            ),
            pair(
                "gz", c.at[:, cxs, TOP + CZ - 1, :], c.at[:, cxs, TOP - 1, :],
                c.at[:, cxs, TOP, :], c.at[:, cxs, TOP + CZ, :],
            ),
            y_pair(sent, received),
        ]
        for start, _ in copies:
            start()

        def wait():
            for _, one in copies:
                one()

        return wait

    def start_values(i, t):
        rows = pl.ds(8 * t, 8)
        scale = cscl[i, rows, :]
        new = [scale * z_pairs(tmp.at[k, i], t) for k in range(3)]
        new.append(-0.03125 * (cvisc[i + 1, pl.ds(TOP + 8 * t, 8), :] * z_pairs(tmp.at[3, i], t)))
        for k in range(4):
            crhs[k, i, rows, :] = new[k]
        return new

    def coarse_update(c, packs, i, t):
        r = TOP + 8 * t
        rows = pl.ds(8 * t, 8)
        here = [c[k, i + 1, pl.ds(r, 8), :] for k in range(4)]
        ys = [y_shifts2(here[k], packs, cslot(k, i, t)) for k in range(4)]
        around = (
            [c[k, i, pl.ds(r, 8), :] for k in range(4)],
            [c[k, i + 2, pl.ds(r, 8), :] for k in range(4)],
            [c[k, i + 1, pl.ds(r - 1, 8), :] for k in range(4)],
            [c[k, i + 1, pl.ds(r + 1, 8), :] for k in range(4)],
            [y[0] for y in ys],
            [y[1] for y in ys],
        )
        sides = [cwts[j, i, rows, :] for j in range(6)]
        moves, spread = terms(here, around, sides, 2.0 * cscl[i, rows, :])
        new = [0.4 * here[k] + (moves[k] + crhs[k, i, rows, :]) for k in range(3)]
        new.append(here[3] + (crhs[3, i, rows, :] - 0.125 * (cvisc[i + 1, pl.ds(r, 8), :] * spread)))
        return new

    wait = coarse_exchange(c1, start_values, csend.at[0], crecv.at[0])
    wait()
    cp1 = (crecv[0, 0], crecv[0, 1])
    wait = coarse_exchange(c2, lambda i, t: coarse_update(c1, cp1, i, t), csend.at[1], crecv.at[1])
    wait()
    cp2 = (crecv[1, 0], crecv[1, 1])
    wait = coarse_exchange(c3, lambda i, t: coarse_update(c2, cp2, i, t), csend.at[2], crecv.at[2])
    wait()
    cp3 = (crecv[2, 0], crecv[2, 1])
    for i in range(CX):
        for t in range(2):
            new = coarse_update(c3, cp3, i, t)
            for k in range(4):
                tmp[k, i, pl.ds(16 * t, 8, stride=2), :] = new[k]
                tmp[k, i, pl.ds(16 * t + 1, 8, stride=2), :] = new[k]

    def corrected(i, t):
        half = lax.div(i, 2)
        return [
            u2[k, i + 1, pl.ds(TOP + 8 * t, 8), :] + tmp[k, half, pl.ds(8 * t, 8), :] for k in range(4)
        ]

    wait = exchange(u3, corrected, ysend.at[2], yrecv.at[2])
    wait()
    packs3 = (yrecv[2, 0], yrecv[2, 1])
    wait = exchange(u4, lambda i, t: fine_update(u3, packs3, i, t), ysend.at[3], yrecv.at[3])
    wait()
    packs4 = (yrecv[3, 0], yrecv[3, 1])

    def stores(i):
        return (
            pltpu.make_async_copy(out.at[0:3, i], vout.at[:, i], store_sem.at[0, i]),
            pltpu.make_async_copy(out.at[3, i], pout.at[i], store_sem.at[1, i]),
        )

    def last(i, _):
        for t in range(4):
            new = fine_update(u4, packs4, i, t)
            for k in range(4):
                out[k, i, pl.ds(8 * t, 8), :] = new[k]
        for store in stores(i):
            store.start()
        return 0

    lax.fori_loop(0, NX, last, 0)
    for i in range(NX):
        for store in stores(i):
            store.wait()
    for drain in pending:
        drain()


COPIES = 2 * (3 + 2 + 3 + 4 * 3 + 3 * 3)


def cycle(size, velocity, pressure, viscosity, body_force):
    field = pltpu.VMEM((4, NX + 2, NZ + 16, NY), F32)
    small = pltpu.VMEM((4, CX + 2, CZ + 16, NY), F32)
    anywhere = pl.BlockSpec(memory_space=pl.ANY)
    out = pl.pallas_call(
        functools.partial(kernel, size),
        out_shape=(
            jax.ShapeDtypeStruct((3, NX, NZ, NY), F32),
            jax.ShapeDtypeStruct((NX, NZ, NY), F32),
        ),
        in_specs=[anywhere] * 4,
        out_specs=(anywhere, anywhere),
        scratch_shapes=[
            field, field, field, field, field,
            pltpu.VMEM((NX + 2, NZ + 16, NY), F32),
            pltpu.VMEM((3, NX, NZ, NY), F32),
            pltpu.VMEM((CX + 2, CZ + 16, NY), F32),
            small, small, small,
            pltpu.VMEM((6, NX, NZ, NY), F32),
            pltpu.VMEM((NX, NZ, NY), F32),
            pltpu.VMEM((NX, NZ, NY), F32),
            pltpu.VMEM((3, NX, NZ, NY), F32),
            pltpu.VMEM((6, CX, CZ, NY), F32),
            pltpu.VMEM((CX, CZ, NY), F32),
            pltpu.VMEM((4, CX, CZ, NY), F32),
            pltpu.VMEM((4, CX, NZ, NY), F32),
            pltpu.VMEM((4, NX, NZ, NY), F32),
            pltpu.VMEM((2, 2, 8, NY), F32),
            pltpu.VMEM((2, 2, 8, NY), F32),
            pltpu.VMEM((4, 2, 8, NY), F32),
            pltpu.VMEM((4, 2, 8, NY), F32),
            pltpu.VMEM((3, 2, 8, NY), F32),
            pltpu.VMEM((3, 2, 8, NY), F32),
            pltpu.SemaphoreType.DMA((COPIES,)),
            pltpu.SemaphoreType.DMA((COPIES,)),
            pltpu.SemaphoreType.DMA((4,)),
            pltpu.SemaphoreType.DMA((2, NX)),
        ],
        compiler_params=pltpu.CompilerParams(collective_id=0, has_side_effects=True),
        name="cycle",
    )(velocity, pressure, viscosity, body_force)
    return out[0], out[1]


def solution(mesh):
    return jax.shard_map(
        functools.partial(cycle, dict(mesh.shape)),
        mesh=mesh,
        in_specs=(
            P(None, "gx", "gz", "gy"),
            P("gx", "gz", "gy"),
            P("gx", "gz", "gy"),
            P(None, "gx", "gz", "gy"),
        ),
        out_specs=(P(None, "gx", "gz", "gy"), P("gx", "gz", "gy")),
        check_vma=False,
    )
```

```python
import functools
import itertools

import jax
import jax.numpy as jnp
from jax import lax
from jax.experimental import pallas as pl
from jax.experimental.pallas import tpu as pltpu
from jax.sharding import PartitionSpec as P

MESH = pl.DeviceIdType.MESH
F32 = jnp.float32
NX, NZ, NY = 8, 32, 128
CX, CZ = 4, 16
DEEP = 4
HX, HZ = CX + 2 * DEEP, CZ + 2 * DEEP
TOP = 8
OWN = TOP + DEEP
AXES = ("gx", "gy", "gz")
AROUND = [d for d in itertools.product((-1, 0, 1), repeat=3) if any(d)]
FACES = 2 * (3 + 2 + 1 + 3 * 3)


def kernel(
    size, vel, prs, vis, frc, vout, pout,
    u0, u1, u2, u3, u4, visc, force, hvisc, c1, c2, c3, c4,
    wts, scl, diag, rhs, cwts, cscl, tmp, grown, edge, out,
    ysend0, yrecv0, ysend, yrecv,
    vx, vy, vxb, vzb, vyc, vyz, cx, cy, cxb, czb, cyc, cyz,
    send_sem, recv_sem, deep_send, deep_recv, load_sem, store_sem,
):
    at = {axis: lax.axis_index(axis) for axis in AXES}
    has = {}
    for axis in AXES:
        has[axis, 1] = at[axis] < size[axis] - 1
        has[axis, -1] = at[axis] > 0
    lane = lax.broadcasted_iota(jnp.int32, (8, NY), 1)
    row = lax.broadcasted_iota(jnp.int32, (8, NY), 0)
    even = lax.rem(lane, 2) == 0
    couple = lax.div(lane, 2)
    nil = jnp.zeros((8, NY), F32)
    count = [0]
    pending = []

    def roll(value, shift):
        return pltpu.roll(value, shift % NY if isinstance(shift, int) else lax.rem(shift + NY, NY), 1)

    def pick(value, index):
        return jnp.take_along_axis(value, index, axis=1, mode="promise_in_bounds")

    def beside(axis, sign):
        return lax.rem(at[axis] + size[axis] + sign, size[axis])

    def exists(offset, sign=1):
        found = None
        for axis, d in zip(AXES, offset):
            if d:
                one = has[axis, sign * d]
                found = one if found is None else found & one
        return found


    def pair(axis, high_face, low_halo, low_face, high_halo):
        slot = count[0]
        count[0] += 2

        def make(k):
            src, dst, sign = ((high_face, low_halo, 1), (low_face, high_halo, -1))[k]
            return pltpu.make_async_remote_copy(
                src_ref=src, dst_ref=dst,
                send_sem=send_sem.at[slot + k], recv_sem=recv_sem.at[slot + k],
                device_id={axis: beside(axis, sign)}, device_id_type=MESH,
            )

        def each(sign, act):
            @pl.when(has[axis, sign])
            def _():
                act(make(0))

            @pl.when(has[axis, -sign])
            def _():
                act(make(1))

        pending.append(lambda: each(1, lambda c: c.wait_send()))
        return (lambda: each(1, lambda c: c.start())), (lambda: each(-1, lambda c: c.wait_recv()))

    def deep_parts(d, xs, ys, xb, zb, yc, yz):
        dx, dy, dz = d
        if dy == 0 and dz == 0:
            return xs, xb.at[0 if dx > 0 else 1]
        if dy == 0:
            if dz > 0:
                return xs.at[:, :, CZ - DEEP : CZ, :], zb.at[1 - dx, :, :, 0:DEEP, :]
            return xs.at[:, :, 0:DEEP, :], zb.at[1 - dx, :, :, DEEP : 2 * DEEP, :]
        src, side = ys.at[1 if dy > 0 else 0], 0 if dy > 0 else 1
        if dz == 0:
            return src, yc.at[1 - dx, side]
        if dz > 0:
            return src.at[DEEP : 2 * DEEP, :], yz.at[1 - dx, side, 0:DEEP, :]
        return src.at[0:DEEP, :], yz.at[1 - dx, side, DEEP : 2 * DEEP, :]

    def deep_exchange(which, *refs):
        def make(k):
            d = AROUND[k]
            src, dst = deep_parts(d, *refs)
            return pltpu.make_async_remote_copy(
                src_ref=src, dst_ref=dst,
                send_sem=deep_send.at[which, k], recv_sem=deep_recv.at[which, k],
                device_id={axis: beside(axis, s) for axis, s in zip(AXES, d) if s}, device_id_type=MESH,
            )

        def each(sign, act):
            for k, d in enumerate(AROUND):
                @pl.when(exists(d, sign))
                def _():
                    act(make(k))

        pending.append(lambda: each(1, lambda c: c.wait_send()))
        return (lambda: each(1, lambda c: c.start())), (lambda: each(-1, lambda c: c.wait_recv()))

    zs = pl.ds(TOP, NZ)
    planes = pl.ds(1, NX)

    def x_pair(u):
        return pair("gx", u.at[:, NX, zs, :], u.at[:, 0, zs, :], u.at[:, 1, zs, :], u.at[:, NX + 1, zs, :])

    def z_pair(u):
        return pair(
            "gz", u.at[:, planes, TOP + NZ - 1, :], u.at[:, planes, TOP - 1, :],
            u.at[:, planes, TOP, :], u.at[:, planes, TOP + NZ, :],
        )

    def y_pair(sent, received):
        return pair("gy", sent, received.at[0], sent, received.at[1])


    loads = [
        pltpu.make_async_copy(vel, u0.at[0:3, planes, zs, :], load_sem.at[0]),
        pltpu.make_async_copy(prs, u0.at[3, planes, zs, :], load_sem.at[1]),
        pltpu.make_async_copy(vis, visc.at[planes, zs, :], load_sem.at[2]),
        pltpu.make_async_copy(frc, force, load_sem.at[3]),
    ]
    for load in loads:
        load.start()

    barrier = pltpu.get_barrier_semaphore()
    total = jnp.int32(0)
    for axis in AXES:
        for sign in (1, -1):
            @pl.when(has[axis, sign])
            def _():
                pl.semaphore_signal(barrier, inc=1, device_id={axis: beside(axis, sign)}, device_id_type=MESH)
            total = total + has[axis, sign].astype(jnp.int32)
    pl.semaphore_wait(barrier, total)

    first = [
        pair("gx", vel.at[:, NX - 1], u0.at[0:3, 0, zs, :], vel.at[:, 0], u0.at[0:3, NX + 1, zs, :]),
        pair("gx", prs.at[NX - 1], u0.at[3, 0, zs, :], prs.at[0], u0.at[3, NX + 1, zs, :]),
        pair("gx", vis.at[NX - 1], visc.at[0, zs, :], vis.at[0], visc.at[NX + 1, zs, :]),
    ]
    for start, _ in first:
        start()

    def zero(ref):
        ref[...] = jnp.zeros(ref.shape, F32)

    fields = (u0, u1, u2, u4)
    low, high = TOP - 1, TOP + NZ

    def edges(axis, sign, refs):
        @pl.when(jnp.logical_not(has[axis, sign]))
        def _():
            for ref in refs:
                zero(ref)

    edges("gx", -1, [u.at[:, 0, zs, :] for u in fields] + [visc.at[0, zs, :]])
    edges("gx", 1, [u.at[:, NX + 1, zs, :] for u in fields] + [visc.at[NX + 1, zs, :]])
    edges("gz", -1, [u.at[:, planes, low : low + 1, :] for u in fields] + [visc.at[planes, low : low + 1, :]])
    edges("gz", 1, [u.at[:, planes, high : high + 1, :] for u in fields] + [visc.at[planes, high : high + 1, :]])
    edges("gy", -1, [yrecv0.at[0]] + [yrecv.at[s, 0] for s in range(3)])
    edges("gy", 1, [yrecv0.at[1]] + [yrecv.at[s, 1] for s in range(3)])

    for load in loads[:3]:
        load.wait()
    more = [
        z_pair(u0),
        pair(
            "gz", visc.at[planes, TOP + NZ - 1, :], visc.at[planes, TOP - 1, :],
            visc.at[planes, TOP, :], visc.at[planes, TOP + NZ, :],
        ),
    ]
    for start, _ in more:
        start()
    first += more


    def slot_of(k, i, t):
        return (k % 2) * 32 + t * 8 + i

    def put(pack, value, slot):
        return jnp.where(couple == slot, roll(value, 2 * slot + 1), pack)

    def join(from_low, from_high):
        return jnp.where(even, roll(from_high, NY - 1), roll(from_low, 1))

    def ends(joined, slot):
        return roll(joined, NY - 1 - 2 * slot)

    def y_shifts(value, end):
        return jnp.where(lane == 0, end, roll(value, 1)), jnp.where(lane == NY - 1, end, roll(value, NY - 1))

    def first_pack(i, packs):
        a, b, c = packs
        for t in range(4):
            rows = pl.ds(TOP + 8 * t, 8)
            a = put(put(a, u0[0, i + 1, rows, :], slot_of(0, i, t)), u0[1, i + 1, rows, :], slot_of(1, i, t))
            b = put(put(b, u0[2, i + 1, rows, :], slot_of(2, i, t)), u0[3, i + 1, rows, :], slot_of(3, i, t))
            c = put(c, visc[i + 1, rows, :], slot_of(0, i, t))
        return a, b, c

    packs = lax.fori_loop(0, NX, first_pack, (nil, nil, nil), unroll=2)
    for n in range(3):
        ysend0[n] = packs[n]
    more = [y_pair(ysend0, yrecv0)]
    more[0][0]()
    first += more


    doubled = jnp.bitwise_and(2 * lane, NY - 1)
    first_half = lane < NY // 2

    def z_pairs(ref, t):
        return ref[pl.ds(16 * t, 8, stride=2), :] + ref[pl.ds(16 * t + 1, 8, stride=2), :]

    def squeeze(a, b):
        a = a + roll(a, NY - 1)
        b = b + roll(b, NY - 1)
        return jnp.where(first_half, pick(a, doubled), pick(b, doubled))

    group = lax.rem(lax.div(lane, DEEP), 16)

    def deep_slot(f, pp, t):
        return t * 8 + f * 2 + pp

    def deep_pack(xs, ys, nf):
        low_pack, high_pack = nil, nil
        for f in range(nf):
            for pp in range(2):
                for t in range(2):
                    value = xs[f, pp, pl.ds(8 * t, 8), :]
                    s = deep_slot(f, pp, t)
                    low_pack = jnp.where(group == s, roll(value, DEEP * s), low_pack)
                    high_pack = jnp.where(group == s, roll(value, DEEP * s - (NY // 2 - DEEP)), high_pack)
        ys[0], ys[1] = low_pack, high_pack

    def deep_unpack(h, nf, xs, ys, xb, zb, yc, yz):
        for dx in range(3):
            corner = []
            for side in range(2):
                value = yz[dx, side]
                corner.append(jnp.where(row < DEEP, roll(value, -8 * DEEP), value))
            middle = [yc[dx, side] for side in range(2)]
            block = xs if dx == 1 else xb.at[0 if dx == 0 else 1]

            def lay(value, odd, s, sides):
                own = roll(value, DEEP - NY // 2 if odd else DEEP)
                s = s + 16 * odd
                before = roll(sides[0], -DEEP * s)
                after = roll(sides[1], NY // 2 + DEEP - DEEP * s)
                return jnp.where(lane < DEEP, before, jnp.where(lane < NY // 2 + DEEP, own, after))

            for f in range(nf):
                for i in range(CX):
                    pp, odd, x = i // 2, i % 2, dx * CX + i
                    for t in range(2):
                        h[f, x, pl.ds(OWN + 8 * t, 8), :] = lay(
                            block[f, pp, pl.ds(8 * t, 8), :], odd, deep_slot(f, pp, t), middle
                        )
                    both = lay(zb[dx, f, pp], odd, deep_slot(f, pp, 0), corner)
                    h[f, x, pl.ds(TOP, DEEP), :] = both[0:DEEP]
                    h[f, x, pl.ds(OWN + CZ, DEEP), :] = both[DEEP : 2 * DEEP]

    def average(i, _):
        for t in range(4):
            rows = pl.ds(TOP + 8 * t, 8)
            tmp[0, i, pl.ds(8 * t, 8), :] = visc[2 * i + 1, rows, :] + visc[2 * i + 2, rows, :]
        return 0

    lax.fori_loop(0, CX, average, 0, unroll=True)
    for pp in range(2):
        for t in range(2):
            vx[0, pp, pl.ds(8 * t, 8), :] = 0.125 * squeeze(
                z_pairs(tmp.at[0, 2 * pp], t), z_pairs(tmp.at[0, 2 * pp + 1], t)
            )
    deep_pack(vx, vy, 1)
    visc_refs = (vx, vy, vxb, vzb, vyc, vyz)
    flow_refs = (cx, cy, cxb, czb, cyc, cyz)
    for refs in (visc_refs, flow_refs):
        for d in AROUND:
            @pl.when(jnp.logical_not(exists(d, -1)))
            def _():
                zero(deep_parts(d, *refs)[1])

    loads[3].wait()
    for _, wait in first:
        wait()


    def weights(i, _):
        joined = join(yrecv0[0, 2], yrecv0[1, 2])
        for t in range(4):
            r = TOP + 8 * t
            here = visc[i + 1, pl.ds(r, 8), :]
            before, after = y_shifts(here, ends(joined, slot_of(0, i, t)))
            sums = [here + other for other in (
                visc[i, pl.ds(r, 8), :], visc[i + 2, pl.ds(r, 8), :],
                visc[i + 1, pl.ds(r - 1, 8), :], visc[i + 1, pl.ds(r + 1, 8), :],
                before, after,
            )]
            twice = (sums[0] + sums[1]) + (sums[2] + sums[3]) + (sums[4] + sums[5])
            scale = 0.6 / twice
            rows = pl.ds(8 * t, 8)
            for j in range(6):
                wts[j, i, rows, :] = scale * sums[j]
            scl[i, rows, :] = scale
            diag[i, rows, :] = twice * (0.5 / 0.6)
            for k in range(3):
                rhs[k, i, rows, :] = (2.0 * scale) * force[k, i, rows, :]
        return 0

    lax.fori_loop(0, NX, weights, 0, unroll=2)

    def coarse_weights(x, _):
        for t in range(3):
            r = TOP + 8 * t
            here = hvisc[0, x, pl.ds(r, 8), :]
            sums = [here + other for other in (
                hvisc[0, x - 1, pl.ds(r, 8), :], hvisc[0, x + 1, pl.ds(r, 8), :],
                hvisc[0, x, pl.ds(r - 1, 8), :], hvisc[0, x, pl.ds(r + 1, 8), :],
                roll(here, 1), roll(here, NY - 1),
            )]
            twice = (sums[0] + sums[1]) + (sums[2] + sums[3]) + (sums[4] + sums[5])
            scale = jnp.where(here > 0.0, 0.6 / twice, 0.0)
            rows = pl.ds(8 * t, 8)
            for j in range(6):
                cwts[j, x - 1, rows, :] = scale * sums[j]
            cscl[x - 1, rows, :] = scale
        return 0


    def terms(here, around, sides, grad_scale):
        moves, spread = [], None
        for k in range(3):
            parts = [sides[j] * around[j][k] for j in range(6)]
            total = (parts[0] + parts[1]) + (parts[2] + parts[3]) + (parts[4] + parts[5])
            moves.append(total - grad_scale * (around[2 * k + 1][3] - around[2 * k][3]))
            d = around[2 * k + 1][k] - around[2 * k][k]
            spread = d if spread is None else spread + d
        return moves, spread

    def fine_terms(u, end_of, i, t):
        r = TOP + 8 * t
        rows = pl.ds(8 * t, 8)
        here = [u[k, i + 1, pl.ds(r, 8), :] for k in range(4)]
        ys = [y_shifts(here[k], end_of(k, i, t)) for k in range(4)]
        around = (
            [u[k, i, pl.ds(r, 8), :] for k in range(4)],
            [u[k, i + 2, pl.ds(r, 8), :] for k in range(4)],
            [u[k, i + 1, pl.ds(r - 1, 8), :] for k in range(4)],
            [u[k, i + 1, pl.ds(r + 1, 8), :] for k in range(4)],
            [y[0] for y in ys],
            [y[1] for y in ys],
        )
        sides = [wts[j, i, rows, :] for j in range(6)]
        moves, spread = terms(here, around, sides, scl[i, rows, :])
        moves = [m + rhs[k, i, rows, :] for k, m in enumerate(moves)]
        return here, moves, spread

    def fine_update(u, end_of, i, t):
        here, moves, spread = fine_terms(u, end_of, i, t)
        new = [0.4 * here[k] + moves[k] for k in range(3)]
        new.append(here[3] - 0.25 * (visc[i + 1, pl.ds(TOP + 8 * t, 8), :] * spread))
        return new

    def joined_ends(low_pack, high_pack):
        joined = [join(low_pack[n], high_pack[n]) for n in range(2)]
        return lambda k, i, t: ends(joined[k // 2], slot_of(k, i, t))

    def exchange(u, make, sent, received):
        def plane(i, packs):
            packs = list(packs)
            for t in range(4):
                new = make(i, t)
                for k in range(4):
                    u[k, i + 1, pl.ds(TOP + 8 * t, 8), :] = new[k]
                    packs[k // 2] = put(packs[k // 2], new[k], slot_of(k, i, t))
            return tuple(packs)

        packs = plane(NX - 1, plane(0, (nil, nil)))
        x_start, x_wait = x_pair(u)
        x_start()
        packs = lax.fori_loop(1, NX - 1, plane, packs, unroll=2)
        sent[0], sent[1] = packs
        z_start, z_wait = z_pair(u)
        z_start()
        y_start, y_wait = y_pair(sent, received)
        y_start()

        def wait():
            x_wait()
            z_wait()
            y_wait()

        return wait

    ends0 = joined_ends(yrecv0.at[0], yrecv0.at[1])
    wait = exchange(u1, lambda i, t: fine_update(u0, ends0, i, t), ysend.at[0], yrecv.at[0])
    wait()
    visc_start, visc_wait = deep_exchange(0, *visc_refs)
    visc_start()
    ends1 = joined_ends(yrecv.at[0, 0], yrecv.at[0, 1])
    wait = exchange(u2, lambda i, t: fine_update(u1, ends1, i, t), ysend.at[1], yrecv.at[1])
    visc_wait()
    deep_unpack(hvisc, 1, *visc_refs)
    lax.fori_loop(1, HX - 1, coarse_weights, 0, unroll=2)

    def flat(ref, pp, t):
        rows = pl.ds(DEEP + 8 * t, 8)
        a, b = ref[CX + 2 * pp - 1, rows, :], ref[CX + 2 * pp, rows, :]
        return jnp.where(first_half, roll(a, -DEEP), roll(b, NY // 2 - DEEP))

    scales = [[flat(cscl, pp, t) for t in range(2)] for pp in range(2)]
    wait()


    ends2 = joined_ends(yrecv.at[1, 0], yrecv.at[1, 1])

    def restrict(i, _):
        for t in range(4):
            sums = None
            for h in range(2):
                here, moves, spread = fine_terms(u2, ends2, 2 * i + h, t)
                d = diag[2 * i + h, pl.ds(8 * t, 8), :]
                parts = [d * (moves[k] - 0.6 * here[k]) for k in range(3)] + [spread]
                sums = parts if sums is None else [a + b for a, b in zip(sums, parts)]
            for k in range(4):
                tmp[k, i, pl.ds(8 * t, 8), :] = sums[k]
        return 0

    lax.fori_loop(0, CX, restrict, 0)
    for k in range(4):
        for pp in range(2):
            for t in range(2):
                factor = scales[pp][t] if k < 3 else -0.03125 * vx[0, pp, pl.ds(8 * t, 8), :]
                cx[k, pp, pl.ds(8 * t, 8), :] = factor * squeeze(
                    z_pairs(tmp.at[k, 2 * pp], t), z_pairs(tmp.at[k, 2 * pp + 1], t)
                )
    deep_pack(cx, cy, 4)
    flow_start, flow_wait = deep_exchange(1, *flow_refs)
    flow_start()
    flow_wait()
    deep_unpack(c1, 4, *flow_refs)

    def coarse_sweep(old, new, start, stop):
        def plane(x, _):
            for t in range(3):
                r = TOP + 8 * t
                rows = pl.ds(8 * t, 8)
                here = [old[k, x, pl.ds(r, 8), :] for k in range(4)]
                around = (
                    [old[k, x - 1, pl.ds(r, 8), :] for k in range(4)],
                    [old[k, x + 1, pl.ds(r, 8), :] for k in range(4)],
                    [old[k, x, pl.ds(r - 1, 8), :] for k in range(4)],
                    [old[k, x, pl.ds(r + 1, 8), :] for k in range(4)],
                    [roll(h, 1) for h in here],
                    [roll(h, NY - 1) for h in here],
                )
                sides = [cwts[j, x - 1, rows, :] for j in range(6)]
                moves, spread = terms(here, around, sides, 2.0 * cscl[x - 1, rows, :])
                source = [c1[k, x, pl.ds(r, 8), :] for k in range(4)]
                for k in range(3):
                    new[k, x, pl.ds(r, 8), :] = 0.4 * here[k] + (moves[k] + source[k])
                new[3, x, pl.ds(r, 8), :] = here[3] + (
                    source[3] - 0.125 * (hvisc[0, x, pl.ds(r, 8), :] * spread)
                )
            return 0

        lax.fori_loop(start, stop, plane, 0, unroll=2)

    coarse_sweep(c1, c2, 1, HX - 1)
    coarse_sweep(c2, c3, 2, HX - 2)
    coarse_sweep(c3, c4, 3, HX - 3)


    spread_out = DEEP + couple
    past_ends = jnp.where(lane < NY // 2, DEEP - 1, NY // 2 + DEEP)

    def prolong(x, _):
        for k in range(4):
            for t in range(2):
                value = pick(c4[k, x + 3, pl.ds(OWN + 8 * t, 8), :], spread_out)
                grown[k, x, pl.ds(TOP + 16 * t, 8, stride=2), :] = value
                grown[k, x, pl.ds(TOP + 16 * t + 1, 8, stride=2), :] = value
        return 0

    def prolong_sides(x, _):
        for k in range(4):
            above = pick(c4[k, x + 3, pl.ds(TOP, 8), :], spread_out)
            grown[k, x, TOP - 1 : TOP, :] = above[DEEP - 1 : DEEP]
            below = pick(c4[k, x + 3, pl.ds(OWN + CZ - DEEP, 8), :], spread_out)
            grown[k, x, TOP + NZ : TOP + NZ + 1, :] = below[DEEP : DEEP + 1]
            for t in range(2):
                value = pick(c4[k, x + 3, pl.ds(OWN + 8 * t, 8), :], past_ends)
                edge[k, x - 1, pl.ds(16 * t, 8, stride=2), :] = value
                edge[k, x - 1, pl.ds(16 * t + 1, 8, stride=2), :] = value
        return 0

    lax.fori_loop(0, CX + 2, prolong, 0, unroll=2)
    lax.fori_loop(1, CX + 1, prolong_sides, 0, unroll=2)

    def correct(i, _):
        half = lax.div(i + 1, 2)
        for k in range(4):
            for t in range(4):
                rows = pl.ds(TOP + 8 * t, 8)
                u3[k, i, rows, :] = u2[k, i, rows, :] + grown[k, half, rows, :]
            for r in (TOP - 1, TOP + NZ):
                u3[k, i, r : r + 1, :] = u2[k, i, r : r + 1, :] + grown[k, half, r : r + 1, :]
        return 0

    lax.fori_loop(1, NX + 1, correct, 0, unroll=2)
    for i, x in ((0, 0), (NX + 1, CX + 1)):
        for k in range(4):
            for t in range(4):
                rows = pl.ds(TOP + 8 * t, 8)
                u3[k, i, rows, :] = u2[k, i, rows, :] + grown[k, x, rows, :]

    def ends3(k, i, t):
        return ends2(k, i, t) + edge[k, lax.div(i, 2) if not isinstance(i, int) else i // 2, pl.ds(8 * t, 8), :]


    wait = exchange(u4, lambda i, t: fine_update(u3, ends3, i, t), ysend.at[2], yrecv.at[2])
    wait()
    ends4 = joined_ends(yrecv.at[2, 0], yrecv.at[2, 1])

    def stores(i):
        return (
            pltpu.make_async_copy(out.at[0:3, i], vout.at[:, i], store_sem.at[0, i]),
            pltpu.make_async_copy(out.at[3, i], pout.at[i], store_sem.at[1, i]),
        )

    def last(i, _):
        for t in range(4):
            new = fine_update(u4, ends4, i, t)
            for k in range(4):
                out[k, i, pl.ds(8 * t, 8), :] = new[k]
        for store in stores(i):
            store.start()
        return 0

    lax.fori_loop(0, NX, last, 0, unroll=2)
    for i in range(NX):
        for store in stores(i):
            store.wait()
    for drain in pending:
        drain()


def cycle(size, velocity, pressure, viscosity, body_force):
    field = pltpu.VMEM((4, NX + 2, NZ + 16, NY), F32)
    small = pltpu.VMEM((4, HX, HZ + 16, NY), F32)
    anywhere = pl.BlockSpec(memory_space=pl.ANY)

    def deep_buffers(nf):
        return [
            pltpu.VMEM((nf, 2, CZ, NY), F32),
            pltpu.VMEM((2, 8, NY), F32),
            pltpu.VMEM((2, nf, 2, CZ, NY), F32),
            pltpu.VMEM((3, nf, 2, 8, NY), F32),
            pltpu.VMEM((3, 2, 8, NY), F32),
            pltpu.VMEM((3, 2, 8, NY), F32),
        ]

    out = pl.pallas_call(
        functools.partial(kernel, size),
        out_shape=(
            jax.ShapeDtypeStruct((3, NX, NZ, NY), F32),
            jax.ShapeDtypeStruct((NX, NZ, NY), F32),
        ),
        in_specs=[anywhere] * 4,
        out_specs=(anywhere, anywhere),
        scratch_shapes=[
            field, field, field, field, field,
            pltpu.VMEM((NX + 2, NZ + 16, NY), F32),
            pltpu.VMEM((3, NX, NZ, NY), F32),
            pltpu.VMEM((1, HX, HZ + 16, NY), F32),
            small, small, small, small,
            pltpu.VMEM((6, NX, NZ, NY), F32),
            pltpu.VMEM((NX, NZ, NY), F32),
            pltpu.VMEM((NX, NZ, NY), F32),
            pltpu.VMEM((3, NX, NZ, NY), F32),
            pltpu.VMEM((6, HX - 2, HZ, NY), F32),
            pltpu.VMEM((HX - 2, HZ, NY), F32),
            pltpu.VMEM((4, CX, NZ, NY), F32),
            pltpu.VMEM((4, CX + 2, NZ + 16, NY), F32),
            pltpu.VMEM((4, CX, NZ, NY), F32),
            pltpu.VMEM((4, NX, NZ, NY), F32),
            pltpu.VMEM((3, 8, NY), F32),
            pltpu.VMEM((2, 3, 8, NY), F32),
            pltpu.VMEM((3, 2, 8, NY), F32),
            pltpu.VMEM((3, 2, 2, 8, NY), F32),
            *deep_buffers(1),
            *deep_buffers(4),
            pltpu.SemaphoreType.DMA((FACES,)),
            pltpu.SemaphoreType.DMA((FACES,)),
            pltpu.SemaphoreType.DMA((2, len(AROUND))),
            pltpu.SemaphoreType.DMA((2, len(AROUND))),
            pltpu.SemaphoreType.DMA((4,)),
            pltpu.SemaphoreType.DMA((2, NX)),
        ],
        compiler_params=pltpu.CompilerParams(collective_id=0, has_side_effects=True),
        name="cycle",
    )(velocity, pressure, viscosity, body_force)
    return out[0], out[1]


def solution(mesh):
    return jax.shard_map(
        functools.partial(cycle, dict(mesh.shape)),
        mesh=mesh,
        in_specs=(
            P(None, "gx", "gz", "gy"),
            P("gx", "gz", "gy"),
            P("gx", "gz", "gy"),
            P(None, "gx", "gz", "gy"),
        ),
        out_specs=(P(None, "gx", "gz", "gy"), P("gx", "gz", "gy")),
        check_vma=False,
    )
```

```python
import functools
import itertools

import jax
import jax.numpy as jnp
from jax import lax
from jax.experimental import pallas as pl
from jax.experimental.pallas import tpu as pltpu
from jax.sharding import PartitionSpec as P

MESH = pl.DeviceIdType.MESH
F32 = jnp.float32
NX, NZ, NY = 8, 32, 128
CX, CZ = 4, 16
DEEP = 4
HX, HZ = CX + 2 * DEEP, CZ + 2 * DEEP
TOP = 8
OWN = TOP + DEEP
AXES = ("gx", "gy", "gz")
AROUND = sorted(
    (d for d in itertools.product((-1, 0, 1), repeat=3) if any(d)),
    key=lambda d: (d[1:] != (0, 0), -sum(map(abs, d))),
)
FACES = 2 * (3 + 2 + 1 + 3 * 3)


def kernel(
    size, vel, prs, vis, frc, vout, pout,
    u0, u1, u2, u3, u4, visc, force, hvisc, c1, c2, c3, c4,
    wts, scl, diag, rhs, cwts, cscl, tmp, grown, gprev, gnext, yprev, ynext, out,
    ysend0, yrecv0, ysend, yrecv,
    vx, vy, vxb, vzb, vyc, vyz, cx, cy, cxb, czb, cyc, cyz,
    send_sem, recv_sem, deep_send, deep_recv, load_sem, store_sem,
):
    at = {axis: lax.axis_index(axis) for axis in AXES}
    has = {}
    for axis in AXES:
        has[axis, 1] = at[axis] < size[axis] - 1
        has[axis, -1] = at[axis] > 0
    lane = lax.broadcasted_iota(jnp.int32, (8, NY), 1)
    row = lax.broadcasted_iota(jnp.int32, (8, NY), 0)
    even = lax.rem(lane, 2) == 0
    couple = lax.div(lane, 2)
    nil = jnp.zeros((8, NY), F32)
    count = [0]
    pending = []

    def drain(keep=0):
        while len(pending) > keep:
            pending.pop(0)()

    def roll(value, shift):
        return pltpu.roll(value, shift % NY if isinstance(shift, int) else lax.rem(shift + NY, NY), 1)

    def pick(value, index):
        return jnp.take_along_axis(value, index, axis=1, mode="promise_in_bounds")

    def beside(axis, sign):
        return lax.rem(at[axis] + size[axis] + sign, size[axis])

    def exists(offset, sign=1):
        found = None
        for axis, d in zip(AXES, offset):
            if d:
                one = has[axis, sign * d]
                found = one if found is None else found & one
        return found


    def pair(axis, high_face, low_halo, low_face, high_halo):
        slot = count[0]
        count[0] += 2

        def make(k):
            src, dst, sign = ((high_face, low_halo, 1), (low_face, high_halo, -1))[k]
            return pltpu.make_async_remote_copy(
                src_ref=src, dst_ref=dst,
                send_sem=send_sem.at[slot + k], recv_sem=recv_sem.at[slot + k],
                device_id={axis: beside(axis, sign)}, device_id_type=MESH,
            )

        def each(sign, act):
            @pl.when(has[axis, sign])
            def _():
                act(make(0))

            @pl.when(has[axis, -sign])
            def _():
                act(make(1))

        pending.append(lambda: each(1, lambda c: c.wait_send()))
        return (lambda: each(1, lambda c: c.start())), (lambda: each(-1, lambda c: c.wait_recv()))

    def deep_parts(d, xs, ys, xb, zb, yc, yz):
        dx, dy, dz = d
        if dy == 0 and dz == 0:
            return xs, xb.at[0 if dx > 0 else 1]
        if dy == 0:
            if dz > 0:
                return xs.at[:, :, CZ - DEEP : CZ, :], zb.at[1 - dx, :, :, 0:DEEP, :]
            return xs.at[:, :, 0:DEEP, :], zb.at[1 - dx, :, :, DEEP : 2 * DEEP, :]
        side = 0 if dy > 0 else 1
        if dz == 0:
            return ys, yc.at[1 - dx, side]
        if dz > 0:
            return ys.at[:, DEEP : 2 * DEEP, :], yz.at[1 - dx, side, :, 0:DEEP, :]
        return ys.at[:, 0:DEEP, :], yz.at[1 - dx, side, :, DEEP : 2 * DEEP, :]

    def deep_exchange(which, *refs):
        def make(k):
            d = AROUND[k]
            src, dst = deep_parts(d, *refs)
            return pltpu.make_async_remote_copy(
                src_ref=src, dst_ref=dst,
                send_sem=deep_send.at[which, k], recv_sem=deep_recv.at[which, k],
                device_id={axis: beside(axis, s) for axis, s in zip(AXES, d) if s}, device_id_type=MESH,
            )

        def each(sign, act):
            for k, d in enumerate(AROUND):
                @pl.when(exists(d, sign))
                def _():
                    act(make(k))

        pending.append(lambda: each(1, lambda c: c.wait_send()))
        return (lambda: each(1, lambda c: c.start())), (lambda: each(-1, lambda c: c.wait_recv()))

    zs = pl.ds(TOP, NZ)
    planes = pl.ds(1, NX)

    def x_pair(u):
        return pair("gx", u.at[:, NX, zs, :], u.at[:, 0, zs, :], u.at[:, 1, zs, :], u.at[:, NX + 1, zs, :])

    def z_pair(u):
        return pair(
            "gz", u.at[:, planes, TOP + NZ - 1, :], u.at[:, planes, TOP - 1, :],
            u.at[:, planes, TOP, :], u.at[:, planes, TOP + NZ, :],
        )

    def y_pair(sent, received):
        return pair("gy", sent, received.at[0], sent, received.at[1])


    loads = [
        pltpu.make_async_copy(vel, u0.at[0:3, planes, zs, :], load_sem.at[0]),
        pltpu.make_async_copy(prs, u0.at[3, planes, zs, :], load_sem.at[1]),
        pltpu.make_async_copy(vis, visc.at[planes, zs, :], load_sem.at[2]),
        pltpu.make_async_copy(frc, force, load_sem.at[3]),
    ]
    for load in loads:
        load.start()

    barrier = pltpu.get_barrier_semaphore()
    total = jnp.int32(0)
    for axis in AXES:
        for sign in (1, -1):
            @pl.when(has[axis, sign])
            def _():
                pl.semaphore_signal(barrier, inc=1, device_id={axis: beside(axis, sign)}, device_id_type=MESH)
            total = total + has[axis, sign].astype(jnp.int32)
    pl.semaphore_wait(barrier, total)

    first = [
        pair("gx", vel.at[:, NX - 1], u0.at[0:3, 0, zs, :], vel.at[:, 0], u0.at[0:3, NX + 1, zs, :]),
        pair("gx", prs.at[NX - 1], u0.at[3, 0, zs, :], prs.at[0], u0.at[3, NX + 1, zs, :]),
        pair("gx", vis.at[NX - 1], visc.at[0, zs, :], vis.at[0], visc.at[NX + 1, zs, :]),
    ]
    for start, _ in first:
        start()

    def zero(ref):
        ref[...] = jnp.zeros(ref.shape, F32)

    fields = (u0, u1, u2, u4)
    low, high = TOP - 1, TOP + NZ

    def edges(axis, sign, refs):
        @pl.when(jnp.logical_not(has[axis, sign]))
        def _():
            for ref in refs:
                zero(ref)

    edges("gx", -1, [u.at[:, 0, zs, :] for u in fields] + [visc.at[0, zs, :]])
    edges("gx", 1, [u.at[:, NX + 1, zs, :] for u in fields] + [visc.at[NX + 1, zs, :]])
    edges("gz", -1, [u.at[:, planes, low : low + 1, :] for u in fields] + [visc.at[planes, low : low + 1, :]])
    edges("gz", 1, [u.at[:, planes, high : high + 1, :] for u in fields] + [visc.at[planes, high : high + 1, :]])
    edges("gy", -1, [yrecv0.at[0]] + [yrecv.at[s, 0] for s in range(3)])
    edges("gy", 1, [yrecv0.at[1]] + [yrecv.at[s, 1] for s in range(3)])

    for load in loads[:3]:
        load.wait()
    more = [
        z_pair(u0),
        pair(
            "gz", visc.at[planes, TOP + NZ - 1, :], visc.at[planes, TOP - 1, :],
            visc.at[planes, TOP, :], visc.at[planes, TOP + NZ, :],
        ),
    ]
    for start, _ in more:
        start()
    first += more


    def slot_of(k, i, t):
        return (k % 2) * 32 + t * 8 + i

    def put(pack, value, slot):
        return jnp.where(couple == slot, roll(value, 2 * slot + 1), pack)

    def join(from_low, from_high):
        return jnp.where(even, roll(from_high, NY - 1), roll(from_low, 1))

    def ends(joined, slot):
        return roll(joined, NY - 1 - 2 * slot)

    def y_shifts(k, i, t, end):
        rows = pl.ds(8 * t, 8)
        return jnp.where(lane == 0, end, yprev[k, i, rows, :]), jnp.where(lane == NY - 1, end, ynext[k, i, rows, :])

    def rotate(u, more=None):
        def plane(i, _):
            for t in range(4):
                for k in range(4 if more is None else 5):
                    rows = pl.ds(TOP + 8 * t, 8)
                    value = u[k, i + 1, rows, :] if k < 4 else more[i + 1, rows, :]
                    yprev[k, i, pl.ds(8 * t, 8), :] = roll(value, 1)
                    ynext[k, i, pl.ds(8 * t, 8), :] = roll(value, NY - 1)
            return 0

        lax.fori_loop(0, NX, plane, 0, unroll=2)

    def first_pack(i, packs):
        a, b, c = packs
        for t in range(4):
            rows = pl.ds(TOP + 8 * t, 8)
            a = put(put(a, u0[0, i + 1, rows, :], slot_of(0, i, t)), u0[1, i + 1, rows, :], slot_of(1, i, t))
            b = put(put(b, u0[2, i + 1, rows, :], slot_of(2, i, t)), u0[3, i + 1, rows, :], slot_of(3, i, t))
            c = put(c, visc[i + 1, rows, :], slot_of(0, i, t))
        return a, b, c

    packs = lax.fori_loop(0, NX, first_pack, (nil, nil, nil), unroll=2)
    for n in range(3):
        ysend0[n] = packs[n]
    more = [y_pair(ysend0, yrecv0)]
    more[0][0]()
    first += more


    doubled = jnp.bitwise_and(2 * lane, NY - 1)
    first_half = lane < NY // 2

    def z_pairs(ref, t):
        return ref[pl.ds(16 * t, 8, stride=2), :] + ref[pl.ds(16 * t + 1, 8, stride=2), :]

    def squeeze(a, b):
        a = a + roll(a, NY - 1)
        b = b + roll(b, NY - 1)
        return jnp.where(first_half, pick(a, doubled), pick(b, doubled))

    octet, fore = lax.div(lane, 2 * DEEP), lax.rem(lane, 2 * DEEP) < DEEP

    def deep_slot(f, pp, t):
        return (f % 2) * 4 + t * 2 + pp

    def deep_pack(xs, ys, nf):
        for n in range((nf + 1) // 2):
            pack = nil
            for f in range(2 * n, min(2 * n + 2, nf)):
                for pp in range(2):
                    for t in range(2):
                        s = deep_slot(f, pp, t)
                        first = fore & (lax.rem(octet, 8) == s)
                        last = jnp.logical_not(fore) & (lax.rem(octet + 1, 8) == s)
                        pack = jnp.where(first | last, roll(xs[f, pp, pl.ds(8 * t, 8), :], 8 * s), pack)
            ys[n] = pack

    def deep_unpack(h, nf, xs, ys, xb, zb, yc, yz):
        for dx in range(3):
            middle, corner = [], []
            for n in range((nf + 1) // 2):
                middle.append(jnp.where(fore, yc[dx, 1, n], yc[dx, 0, n]))
                value = jnp.where(fore, yz[dx, 1, n], yz[dx, 0, n])
                corner.append(jnp.where(row < DEEP, roll(value, -4 * DEEP), value))
            block = xs if dx == 1 else xb.at[0 if dx == 0 else 1]

            def lay(value, odd, s, sides):
                own = roll(value, NY // 2) if odd else value
                return jnp.where(first_half, own, roll(sides, NY // 2 - 8 * (s + 8 * odd)))

            for f in range(nf):
                for i in range(CX):
                    pp, odd, x = i // 2, i % 2, dx * CX + i
                    for t in range(2):
                        h[f, x, pl.ds(OWN + 8 * t, 8), :] = lay(
                            block[f, pp, pl.ds(8 * t, 8), :], odd, deep_slot(f, pp, t), middle[f // 2]
                        )
                    both = lay(zb[dx, f, pp], odd, deep_slot(f, pp, 0), corner[f // 2])
                    h[f, x, pl.ds(TOP, DEEP), :] = both[0:DEEP]
                    h[f, x, pl.ds(OWN + CZ, DEEP), :] = both[DEEP : 2 * DEEP]

    def average(i, _):
        for t in range(4):
            rows = pl.ds(TOP + 8 * t, 8)
            tmp[0, i, pl.ds(8 * t, 8), :] = visc[2 * i + 1, rows, :] + visc[2 * i + 2, rows, :]
        return 0

    lax.fori_loop(0, CX, average, 0, unroll=True)
    for pp in range(2):
        for t in range(2):
            vx[0, pp, pl.ds(8 * t, 8), :] = 0.125 * squeeze(
                z_pairs(tmp.at[0, 2 * pp], t), z_pairs(tmp.at[0, 2 * pp + 1], t)
            )
    deep_pack(vx, vy, 1)
    visc_refs = (vx, vy, vxb, vzb, vyc, vyz)
    flow_refs = (cx, cy, cxb, czb, cyc, cyz)
    for refs in (visc_refs, flow_refs):
        for d in AROUND:
            @pl.when(jnp.logical_not(exists(d, -1)))
            def _():
                zero(deep_parts(d, *refs)[1])

    rotate(u0, visc)
    loads[3].wait()
    for _, wait in first:
        wait()


    def weights(i, _):
        joined = join(yrecv0[0, 2], yrecv0[1, 2])
        for t in range(4):
            r = TOP + 8 * t
            here = visc[i + 1, pl.ds(r, 8), :]
            before, after = y_shifts(4, i, t, ends(joined, slot_of(0, i, t)))
            sums = [here + other for other in (
                visc[i, pl.ds(r, 8), :], visc[i + 2, pl.ds(r, 8), :],
                visc[i + 1, pl.ds(r - 1, 8), :], visc[i + 1, pl.ds(r + 1, 8), :],
                before, after,
            )]
            twice = (sums[0] + sums[1]) + (sums[2] + sums[3]) + (sums[4] + sums[5])
            scale = 0.6 / twice
            rows = pl.ds(8 * t, 8)
            for j in range(6):
                wts[j, i, rows, :] = scale * sums[j]
            scl[i, rows, :] = scale
            diag[i, rows, :] = twice * (0.5 / 0.6)
            for k in range(3):
                rhs[k, i, rows, :] = (2.0 * scale) * force[k, i, rows, :]
        return 0

    lax.fori_loop(0, NX, weights, 0, unroll=2)

    def coarse_weights(x, _):
        for t in range(3):
            r = TOP + 8 * t
            here = hvisc[0, x, pl.ds(r, 8), :]
            sums = [here + other for other in (
                hvisc[0, x - 1, pl.ds(r, 8), :], hvisc[0, x + 1, pl.ds(r, 8), :],
                hvisc[0, x, pl.ds(r - 1, 8), :], hvisc[0, x, pl.ds(r + 1, 8), :],
                roll(here, 1), roll(here, NY - 1),
            )]
            twice = (sums[0] + sums[1]) + (sums[2] + sums[3]) + (sums[4] + sums[5])
            scale = jnp.where(here > 0.0, 0.6 / twice, 0.0)
            rows = pl.ds(8 * t, 8)
            for j in range(6):
                cwts[j, x - 1, rows, :] = scale * sums[j]
            cscl[x - 1, rows, :] = scale
        return 0


    def terms(here, around, sides, grad_scale):
        moves, spread = [], None
        for k in range(3):
            parts = [sides[j] * around[j][k] for j in range(6)]
            total = (parts[0] + parts[1]) + (parts[2] + parts[3]) + (parts[4] + parts[5])
            moves.append(total - grad_scale * (around[2 * k + 1][3] - around[2 * k][3]))
            d = around[2 * k + 1][k] - around[2 * k][k]
            spread = d if spread is None else spread + d
        return moves, spread

    def fine_terms(u, y_of, i, t):
        r = TOP + 8 * t
        rows = pl.ds(8 * t, 8)
        here = [u[k, i + 1, pl.ds(r, 8), :] for k in range(4)]
        ys = [y_of(k, i, t) for k in range(4)]
        around = (
            [u[k, i, pl.ds(r, 8), :] for k in range(4)],
            [u[k, i + 2, pl.ds(r, 8), :] for k in range(4)],
            [u[k, i + 1, pl.ds(r - 1, 8), :] for k in range(4)],
            [u[k, i + 1, pl.ds(r + 1, 8), :] for k in range(4)],
            [y[0] for y in ys],
            [y[1] for y in ys],
        )
        sides = [wts[j, i, rows, :] for j in range(6)]
        moves, spread = terms(here, around, sides, scl[i, rows, :])
        moves = [m + rhs[k, i, rows, :] for k, m in enumerate(moves)]
        return here, moves, spread

    def fine_update(u, y_of, i, t):
        here, moves, spread = fine_terms(u, y_of, i, t)
        new = [0.4 * here[k] + moves[k] for k in range(3)]
        new.append(here[3] - 0.25 * (visc[i + 1, pl.ds(TOP + 8 * t, 8), :] * spread))
        return new

    def joined_ends(low_pack, high_pack):
        joined = [join(low_pack[n], high_pack[n]) for n in range(2)]
        return lambda k, i, t: y_shifts(k, i, t, ends(joined[k // 2], slot_of(k, i, t)))

    def exchange(u, make, sent, received):
        def plane(i, packs):
            packs = list(packs)
            for t in range(4):
                new = make(i, t)
                for k in range(4):
                    u[k, i + 1, pl.ds(TOP + 8 * t, 8), :] = new[k]
                    packs[k // 2] = put(packs[k // 2], new[k], slot_of(k, i, t))
            return tuple(packs)

        packs = plane(NX - 1, plane(0, (nil, nil)))
        x_start, x_wait = x_pair(u)
        x_start()
        packs = lax.fori_loop(1, NX - 1, plane, packs, unroll=2)
        sent[0], sent[1] = packs
        z_start, z_wait = z_pair(u)
        z_start()
        y_start, y_wait = y_pair(sent, received)
        y_start()

        def wait():
            x_wait()
            z_wait()
            y_wait()

        return wait

    ends0 = joined_ends(yrecv0.at[0], yrecv0.at[1])
    wait = exchange(u1, lambda i, t: fine_update(u0, ends0, i, t), ysend.at[0], yrecv.at[0])
    rotate(u1)
    drain(3)
    wait()
    visc_start, visc_wait = deep_exchange(0, *visc_refs)
    visc_start()
    ends1 = joined_ends(yrecv.at[0, 0], yrecv.at[0, 1])
    wait = exchange(u2, lambda i, t: fine_update(u1, ends1, i, t), ysend.at[1], yrecv.at[1])
    rotate(u2)
    visc_wait()
    deep_unpack(hvisc, 1, *visc_refs)
    lax.fori_loop(1, HX - 1, coarse_weights, 0, unroll=2)

    def flat(ref, pp, t):
        rows = pl.ds(DEEP + 8 * t, 8)
        a, b = ref[CX + 2 * pp - 1, rows, :], ref[CX + 2 * pp, rows, :]
        return jnp.where(first_half, a, roll(b, NY // 2))

    scales = [[flat(cscl, pp, t) for t in range(2)] for pp in range(2)]
    wait()


    ends2 = joined_ends(yrecv.at[1, 0], yrecv.at[1, 1])

    def restrict(i, _):
        for t in range(4):
            sums = None
            for h in range(2):
                here, moves, spread = fine_terms(u2, ends2, 2 * i + h, t)
                d = diag[2 * i + h, pl.ds(8 * t, 8), :]
                parts = [d * (moves[k] - 0.6 * here[k]) for k in range(3)] + [spread]
                sums = parts if sums is None else [a + b for a, b in zip(sums, parts)]
            for k in range(4):
                tmp[k, i, pl.ds(8 * t, 8), :] = sums[k]
        return 0

    lax.fori_loop(0, CX, restrict, 0)
    for k in range(4):
        for pp in range(2):
            for t in range(2):
                factor = scales[pp][t] if k < 3 else -0.03125 * vx[0, pp, pl.ds(8 * t, 8), :]
                cx[k, pp, pl.ds(8 * t, 8), :] = factor * squeeze(
                    z_pairs(tmp.at[k, 2 * pp], t), z_pairs(tmp.at[k, 2 * pp + 1], t)
                )
    deep_pack(cx, cy, 4)
    flow_start, flow_wait = deep_exchange(1, *flow_refs)
    flow_start()

    def insert_ends(i, _):
        for t in range(4):
            rows = pl.ds(8 * t, 8)
            for k in range(4):
                yprev[k, i, rows, :], ynext[k, i, rows, :] = ends2(k, i, t)
        return 0

    lax.fori_loop(0, NX, insert_ends, 0, unroll=2)
    drain(1)
    flow_wait()
    deep_unpack(c1, 4, *flow_refs)

    def coarse_sweep(old, new, start, stop):
        def plane(x, _):
            for t in range(3):
                r = TOP + 8 * t
                rows = pl.ds(8 * t, 8)
                here = [old[k, x, pl.ds(r, 8), :] for k in range(4)]
                around = (
                    [old[k, x - 1, pl.ds(r, 8), :] for k in range(4)],
                    [old[k, x + 1, pl.ds(r, 8), :] for k in range(4)],
                    [old[k, x, pl.ds(r - 1, 8), :] for k in range(4)],
                    [old[k, x, pl.ds(r + 1, 8), :] for k in range(4)],
                    [roll(h, 1) for h in here],
                    [roll(h, NY - 1) for h in here],
                )
                sides = [cwts[j, x - 1, rows, :] for j in range(6)]
                moves, spread = terms(here, around, sides, 2.0 * cscl[x - 1, rows, :])
                source = [c1[k, x, pl.ds(r, 8), :] for k in range(4)]
                for k in range(3):
                    new[k, x, pl.ds(r, 8), :] = 0.4 * here[k] + (moves[k] + source[k])
                new[3, x, pl.ds(r, 8), :] = here[3] + (
                    source[3] - 0.125 * (hvisc[0, x, pl.ds(r, 8), :] * spread)
                )
            return 0

        lax.fori_loop(start, stop, plane, 0, unroll=2)

    coarse_sweep(c1, c2, 1, HX - 1)
    coarse_sweep(c2, c3, 2, HX - 2)
    coarse_sweep(c3, c4, 3, HX - 3)


    parents = (couple, jnp.where(lane == 0, NY - 1, lax.div(lane + 1, 2) - 1), lax.div(lane + 1, 2))

    def widen(ref, start, value):
        ref[pl.ds(start, 8, stride=2), :] = value
        ref[pl.ds(start + 1, 8, stride=2), :] = value

    def prolong(x, _):
        for k in range(4):
            for t in range(2):
                widen(grown.at[k, x], TOP + 16 * t, pick(c4[k, x + 3, pl.ds(OWN + 8 * t, 8), :], parents[0]))
        return 0

    def prolong_sides(x, _):
        for k in range(4):
            above = pick(c4[k, x + 3, pl.ds(TOP, 8), :], parents[0])
            grown[k, x, TOP - 1 : TOP, :] = above[DEEP - 1 : DEEP]
            below = pick(c4[k, x + 3, pl.ds(OWN + CZ - DEEP, 8), :], parents[0])
            grown[k, x, TOP + NZ : TOP + NZ + 1, :] = below[DEEP : DEEP + 1]
            for t in range(2):
                value = c4[k, x + 3, pl.ds(OWN + 8 * t, 8), :]
                widen(gprev.at[k, x - 1], 16 * t, pick(value, parents[1]))
                widen(gnext.at[k, x - 1], 16 * t, pick(value, parents[2]))
        return 0

    lax.fori_loop(0, CX + 2, prolong, 0, unroll=2)
    lax.fori_loop(1, CX + 1, prolong_sides, 0, unroll=2)

    def correct(i, _):
        half = lax.div(i + 1, 2)
        for k in range(4):
            for t in range(4):
                rows = pl.ds(TOP + 8 * t, 8)
                u3[k, i, rows, :] = u2[k, i, rows, :] + grown[k, half, rows, :]
            for r in (TOP - 1, TOP + NZ):
                u3[k, i, r : r + 1, :] = u2[k, i, r : r + 1, :] + grown[k, half, r : r + 1, :]
        return 0

    lax.fori_loop(1, NX + 1, correct, 0, unroll=2)
    for i, x in ((0, 0), (NX + 1, CX + 1)):
        for k in range(4):
            for t in range(4):
                rows = pl.ds(TOP + 8 * t, 8)
                u3[k, i, rows, :] = u2[k, i, rows, :] + grown[k, x, rows, :]

    def ends3(k, i, t):
        rows = pl.ds(8 * t, 8)
        half = i // 2 if isinstance(i, int) else lax.div(i, 2)
        return yprev[k, i, rows, :] + gprev[k, half, rows, :], ynext[k, i, rows, :] + gnext[k, half, rows, :]


    wait = exchange(u4, lambda i, t: fine_update(u3, ends3, i, t), ysend.at[2], yrecv.at[2])
    rotate(u4)
    drain(3)
    wait()
    ends4 = joined_ends(yrecv.at[2, 0], yrecv.at[2, 1])

    def stores(i):
        return (
            pltpu.make_async_copy(out.at[0:3, i], vout.at[:, i], store_sem.at[0, i]),
            pltpu.make_async_copy(out.at[3, i], pout.at[i], store_sem.at[1, i]),
        )

    def last(i, _):
        for t in range(4):
            new = fine_update(u4, ends4, i, t)
            for k in range(4):
                out[k, i, pl.ds(8 * t, 8), :] = new[k]
        for store in stores(i):
            store.start()
        return 0

    lax.fori_loop(0, NX, last, 0, unroll=2)
    for i in range(NX):
        for store in stores(i):
            store.wait()
    drain()


def cycle(size, velocity, pressure, viscosity, body_force):
    field = pltpu.VMEM((4, NX + 2, NZ + 16, NY), F32)
    small = pltpu.VMEM((4, HX, HZ + 16, NY), F32)
    anywhere = pl.BlockSpec(memory_space=pl.ANY)

    def deep_buffers(nf):
        return [
            pltpu.VMEM((nf, 2, CZ, NY), F32),
            pltpu.VMEM(((nf + 1) // 2, 8, NY), F32),
            pltpu.VMEM((2, nf, 2, CZ, NY), F32),
            pltpu.VMEM((3, nf, 2, 8, NY), F32),
            pltpu.VMEM((3, 2, (nf + 1) // 2, 8, NY), F32),
            pltpu.VMEM((3, 2, (nf + 1) // 2, 8, NY), F32),
        ]

    out = pl.pallas_call(
        functools.partial(kernel, size),
        out_shape=(
            jax.ShapeDtypeStruct((3, NX, NZ, NY), F32),
            jax.ShapeDtypeStruct((NX, NZ, NY), F32),
        ),
        in_specs=[anywhere] * 4,
        out_specs=(anywhere, anywhere),
        scratch_shapes=[
            field, field, field, field, field,
            pltpu.VMEM((NX + 2, NZ + 16, NY), F32),
            pltpu.VMEM((3, NX, NZ, NY), F32),
            pltpu.VMEM((1, HX, HZ + 16, NY), F32),
            small, small, small, small,
            pltpu.VMEM((6, NX, NZ, NY), F32),
            pltpu.VMEM((NX, NZ, NY), F32),
            pltpu.VMEM((NX, NZ, NY), F32),
            pltpu.VMEM((3, NX, NZ, NY), F32),
            pltpu.VMEM((6, HX - 2, HZ, NY), F32),
            pltpu.VMEM((HX - 2, HZ, NY), F32),
            pltpu.VMEM((4, CX, NZ, NY), F32),
            pltpu.VMEM((4, CX + 2, NZ + 16, NY), F32),
            pltpu.VMEM((4, CX, NZ, NY), F32),
            pltpu.VMEM((4, CX, NZ, NY), F32),
            pltpu.VMEM((5, NX, NZ, NY), F32),
            pltpu.VMEM((5, NX, NZ, NY), F32),
            pltpu.VMEM((4, NX, NZ, NY), F32),
            pltpu.VMEM((3, 8, NY), F32),
            pltpu.VMEM((2, 3, 8, NY), F32),
            pltpu.VMEM((3, 2, 8, NY), F32),
            pltpu.VMEM((3, 2, 2, 8, NY), F32),
            *deep_buffers(1),
            *deep_buffers(4),
            pltpu.SemaphoreType.DMA((FACES,)),
            pltpu.SemaphoreType.DMA((FACES,)),
            pltpu.SemaphoreType.DMA((2, len(AROUND))),
            pltpu.SemaphoreType.DMA((2, len(AROUND))),
            pltpu.SemaphoreType.DMA((4,)),
            pltpu.SemaphoreType.DMA((2, NX)),
        ],
        compiler_params=pltpu.CompilerParams(collective_id=0, has_side_effects=True),
        name="cycle",
    )(velocity, pressure, viscosity, body_force)
    return out[0], out[1]


def solution(mesh):
    return jax.shard_map(
        functools.partial(cycle, dict(mesh.shape)),
        mesh=mesh,
        in_specs=(
            P(None, "gx", "gz", "gy"),
            P("gx", "gz", "gy"),
            P("gx", "gz", "gy"),
            P(None, "gx", "gz", "gy"),
        ),
        out_specs=(P(None, "gx", "gz", "gy"), P("gx", "gz", "gy")),
        check_vma=False,
    )
```

```python
import functools
import itertools

import jax
import jax.numpy as jnp
from jax import lax
from jax.experimental import pallas as pl
from jax.experimental.pallas import tpu as pltpu
from jax.sharding import PartitionSpec as P

MESH = pl.DeviceIdType.MESH
F32 = jnp.float32
NX, NZ, NY = 8, 32, 128
CX, CZ = 4, 16
DEEP = 4
HX, HZ = CX + 2 * DEEP, CZ + 2 * DEEP
TOP = 8
OWN = TOP + DEEP
AXES = ("gx", "gy", "gz")
AROUND = sorted(
    (d for d in itertools.product((-1, 0, 1), repeat=3) if any(d)),
    key=lambda d: (d[1:] != (0, 0), -sum(map(abs, d))),
)
FACES = 2 * (2 + 2 + 1 + 3 * 3)


def kernel(
    size, vel, prs, vis, frc, vout, pout,
    u0, u1, u2, u3, u4, visc, force, hvisc, c1, c2, c3, c4,
    wts, scl, diag, rhs, cwts, cscl, tmp, grown, gprev, gnext, yprev, ynext, out,
    ysend0, yrecv0, ysend, yrecv,
    vx, vy, vxb, vzb, vyc, vyz, cx, cy, cxb, czb, cyc, cyz,
    send_sem, recv_sem, deep_send, deep_recv, load_sem, store_sem,
):
    at = {axis: lax.axis_index(axis) for axis in AXES}
    has = {}
    for axis in AXES:
        has[axis, 1] = at[axis] < size[axis] - 1
        has[axis, -1] = at[axis] > 0
    lane = lax.broadcasted_iota(jnp.int32, (8, NY), 1)
    row = lax.broadcasted_iota(jnp.int32, (8, NY), 0)
    even = lax.rem(lane, 2) == 0
    couple = lax.div(lane, 2)
    nil = jnp.zeros((8, NY), F32)
    count = [0]
    pending = []

    def drain(keep=0):
        while len(pending) > keep:
            pending.pop(0)()

    def roll(value, shift):
        return pltpu.roll(value, shift % NY if isinstance(shift, int) else shift, 1)

    def pick(value, index):
        return jnp.take_along_axis(value, index, axis=1, mode="promise_in_bounds")

    def beside(axis, sign):
        return lax.rem(at[axis] + size[axis] + sign, size[axis])

    def exists(offset, sign=1):
        found = None
        for axis, d in zip(AXES, offset):
            if d:
                one = has[axis, sign * d]
                found = one if found is None else found & one
        return found


    def pair(axis, high_face, low_halo, low_face, high_halo):
        slot = count[0]
        count[0] += 2

        def make(k):
            src, dst, sign = ((high_face, low_halo, 1), (low_face, high_halo, -1))[k]
            return pltpu.make_async_remote_copy(
                src_ref=src, dst_ref=dst,
                send_sem=send_sem.at[slot + k], recv_sem=recv_sem.at[slot + k],
                device_id={axis: beside(axis, sign)}, device_id_type=MESH,
            )

        def each(sign, act):
            @pl.when(has[axis, sign])
            def _():
                act(make(0))

            @pl.when(has[axis, -sign])
            def _():
                act(make(1))

        pending.append(lambda: each(1, lambda c: c.wait_send()))
        return (lambda: each(1, lambda c: c.start())), (lambda: each(-1, lambda c: c.wait_recv()))

    def deep_parts(d, xs, ys, xb, zb, yc, yz):
        dx, dy, dz = d
        if dy == 0 and dz == 0:
            return xs, xb.at[0 if dx > 0 else 1]
        if dy == 0:
            if dz > 0:
                return xs.at[:, :, CZ - DEEP : CZ, :], zb.at[1 - dx, :, :, 0:DEEP, :]
            return xs.at[:, :, 0:DEEP, :], zb.at[1 - dx, :, :, DEEP : 2 * DEEP, :]
        side = 0 if dy > 0 else 1
        if dz == 0:
            return ys, yc.at[1 - dx, side]
        if dz > 0:
            return ys.at[:, DEEP : 2 * DEEP, :], yz.at[1 - dx, side, :, 0:DEEP, :]
        return ys.at[:, 0:DEEP, :], yz.at[1 - dx, side, :, DEEP : 2 * DEEP, :]

    def deep_exchange(which, *refs):
        def make(k):
            d = AROUND[k]
            src, dst = deep_parts(d, *refs)
            return pltpu.make_async_remote_copy(
                src_ref=src, dst_ref=dst,
                send_sem=deep_send.at[which, k], recv_sem=deep_recv.at[which, k],
                device_id={axis: beside(axis, s) for axis, s in zip(AXES, d) if s}, device_id_type=MESH,
            )

        def each(sign, act, hops=(1, 2, 3)):
            for k, d in enumerate(AROUND):
                if sum(map(abs, d)) in hops:
                    @pl.when(exists(d, sign))
                    def _():
                        act(make(k))

        def start(*hops):
            each(1, lambda c: c.start(), hops)

        pending.append(lambda: each(1, lambda c: c.wait_send()))
        return start, (lambda: each(-1, lambda c: c.wait_recv()))

    zs = pl.ds(TOP, NZ)
    planes = pl.ds(1, NX)

    def x_pair(u):
        return pair("gx", u.at[:, NX, zs, :], u.at[:, 0, zs, :], u.at[:, 1, zs, :], u.at[:, NX + 1, zs, :])

    def z_pair(u):
        return pair(
            "gz", u.at[:, planes, TOP + NZ - 1, :], u.at[:, planes, TOP - 1, :],
            u.at[:, planes, TOP, :], u.at[:, planes, TOP + NZ, :],
        )

    def y_pair(sent, received):
        return pair("gy", sent, received.at[0], sent, received.at[1])


    loads = [
        pltpu.make_async_copy(vel, u0.at[0:3, planes, zs, :], load_sem.at[0]),
        pltpu.make_async_copy(prs, u0.at[3, planes, zs, :], load_sem.at[1]),
        pltpu.make_async_copy(vis, visc.at[planes, zs, :], load_sem.at[2]),
        pltpu.make_async_copy(frc, force, load_sem.at[3]),
    ]
    for load in loads:
        load.start()

    barrier = pltpu.get_barrier_semaphore()
    total = jnp.int32(0)
    for axis in AXES:
        for sign in (1, -1):
            @pl.when(has[axis, sign])
            def _():
                pl.semaphore_signal(barrier, inc=1, device_id={axis: beside(axis, sign)}, device_id_type=MESH)
            total = total + has[axis, sign].astype(jnp.int32)

    def zero(ref):
        ref[...] = jnp.zeros(ref.shape, F32)

    fields = (u0, u1, u2, u4)
    low, high = TOP - 1, TOP + NZ

    def edges(axis, sign, refs):
        @pl.when(jnp.logical_not(has[axis, sign]))
        def _():
            for ref in refs:
                zero(ref)

    edges("gx", -1, [u.at[:, 0, zs, :] for u in fields] + [visc.at[0, zs, :]])
    edges("gx", 1, [u.at[:, NX + 1, zs, :] for u in fields] + [visc.at[NX + 1, zs, :]])
    edges("gz", -1, [u.at[:, planes, low : low + 1, :] for u in fields] + [visc.at[planes, low : low + 1, :]])
    edges("gz", 1, [u.at[:, planes, high : high + 1, :] for u in fields] + [visc.at[planes, high : high + 1, :]])
    edges("gy", -1, [yrecv0.at[0]] + [yrecv.at[s, 0] for s in range(3)])
    edges("gy", 1, [yrecv0.at[1]] + [yrecv.at[s, 1] for s in range(3)])

    for load in loads[:3]:
        load.wait()


    def slot_of(k, i, t):
        return (k % 2) * 32 + t * 8 + i

    def put(pack, value, slot):
        return jnp.where(couple == slot, roll(value, 2 * slot + 1), pack)

    def join(from_low, from_high):
        return jnp.where(even, roll(from_high, NY - 1), roll(from_low, 1))

    def ends(joined, slot):
        return roll(joined, NY - 1 - 2 * slot)

    def y_shifts(k, i, t, end):
        rows = pl.ds(8 * t, 8)
        return jnp.where(lane == 0, end, yprev[k, i, rows, :]), jnp.where(lane == NY - 1, end, ynext[k, i, rows, :])

    def rotate(u, more=None):
        def plane(i, _):
            for t in range(4):
                for k in range(4 if more is None else 5):
                    rows = pl.ds(TOP + 8 * t, 8)
                    value = u[k, i + 1, rows, :] if k < 4 else more[i + 1, rows, :]
                    yprev[k, i, pl.ds(8 * t, 8), :] = roll(value, 1)
                    ynext[k, i, pl.ds(8 * t, 8), :] = roll(value, NY - 1)
            return 0

        lax.fori_loop(0, NX, plane, 0, unroll=2)

    def first_pack(i, packs):
        a, b, c = packs
        for t in range(4):
            rows = pl.ds(TOP + 8 * t, 8)
            a = put(put(a, u0[0, i + 1, rows, :], slot_of(0, i, t)), u0[1, i + 1, rows, :], slot_of(1, i, t))
            b = put(put(b, u0[2, i + 1, rows, :], slot_of(2, i, t)), u0[3, i + 1, rows, :], slot_of(3, i, t))
            c = put(c, visc[i + 1, rows, :], slot_of(0, i, t))
        return a, b, c

    packs = lax.fori_loop(0, NX, first_pack, (nil, nil, nil), unroll=2)
    for n in range(3):
        ysend0[n] = packs[n]

    pl.semaphore_wait(barrier, total)
    first = [
        x_pair(u0),
        pair("gx", visc.at[NX, zs, :], visc.at[0, zs, :], visc.at[1, zs, :], visc.at[NX + 1, zs, :]),
        y_pair(ysend0, yrecv0),
        z_pair(u0),
        pair(
            "gz", visc.at[planes, TOP + NZ - 1, :], visc.at[planes, TOP - 1, :],
            visc.at[planes, TOP, :], visc.at[planes, TOP + NZ, :],
        ),
    ]
    for start, _ in first:
        start()


    doubled = jnp.bitwise_and(2 * lane, NY - 1)
    first_half = lane < NY // 2

    def z_pairs(ref, t):
        return ref[pl.ds(16 * t, 8, stride=2), :] + ref[pl.ds(16 * t + 1, 8, stride=2), :]

    def squeeze(a, b):
        a = a + roll(a, NY - 1)
        b = b + roll(b, NY - 1)
        return jnp.where(first_half, pick(a, doubled), pick(b, doubled))

    octet, fore = lax.div(lane, 2 * DEEP), lax.rem(lane, 2 * DEEP) < DEEP

    def deep_slot(f, pp, t):
        return (f % 2) * 4 + t * 2 + pp

    def deep_pack(xs, ys, nf):
        for n in range((nf + 1) // 2):
            pack = nil
            for f in range(2 * n, min(2 * n + 2, nf)):
                for pp in range(2):
                    for t in range(2):
                        s = deep_slot(f, pp, t)
                        first = fore & (lax.rem(octet, 8) == s)
                        last = jnp.logical_not(fore) & (lax.rem(octet + 1, 8) == s)
                        pack = jnp.where(first | last, roll(xs[f, pp, pl.ds(8 * t, 8), :], 8 * s), pack)
            ys[n] = pack

    def deep_unpack(h, nf, xs, ys, xb, zb, yc, yz):
        for dx in range(3):
            middle, corner = [], []
            for n in range((nf + 1) // 2):
                middle.append(jnp.where(fore, yc[dx, 1, n], yc[dx, 0, n]))
                value = jnp.where(fore, yz[dx, 1, n], yz[dx, 0, n])
                corner.append(jnp.where(row < DEEP, roll(value, -4 * DEEP), value))
            block = xs if dx == 1 else xb.at[0 if dx == 0 else 1]

            def lay(value, odd, s, sides):
                own = roll(value, NY // 2) if odd else value
                return jnp.where(first_half, own, roll(sides, NY // 2 - 8 * (s + 8 * odd)))

            for f in range(nf):
                for i in range(CX):
                    pp, odd, x = i // 2, i % 2, dx * CX + i
                    for t in range(2):
                        h[f, x, pl.ds(OWN + 8 * t, 8), :] = lay(
                            block[f, pp, pl.ds(8 * t, 8), :], odd, deep_slot(f, pp, t), middle[f // 2]
                        )
                    both = lay(zb[dx, f, pp], odd, deep_slot(f, pp, 0), corner[f // 2])
                    h[f, x, pl.ds(TOP, DEEP), :] = both[0:DEEP]
                    h[f, x, pl.ds(OWN + CZ, DEEP), :] = both[DEEP : 2 * DEEP]

    def average(i, _):
        for t in range(4):
            rows = pl.ds(TOP + 8 * t, 8)
            tmp[0, i, pl.ds(8 * t, 8), :] = visc[2 * i + 1, rows, :] + visc[2 * i + 2, rows, :]
        return 0

    lax.fori_loop(0, CX, average, 0, unroll=True)
    for pp in range(2):
        for t in range(2):
            vx[0, pp, pl.ds(8 * t, 8), :] = 0.125 * squeeze(
                z_pairs(tmp.at[0, 2 * pp], t), z_pairs(tmp.at[0, 2 * pp + 1], t)
            )
    deep_pack(vx, vy, 1)
    visc_refs = (vx, vy, vxb, vzb, vyc, vyz)
    flow_refs = (cx, cy, cxb, czb, cyc, cyz)
    for refs in (visc_refs, flow_refs):
        for d in AROUND:
            @pl.when(jnp.logical_not(exists(d, -1)))
            def _():
                zero(deep_parts(d, *refs)[1])

    rotate(u0, visc)
    loads[3].wait()
    for _, wait in first:
        wait()


    def weights(i, _):
        joined = join(yrecv0[0, 2], yrecv0[1, 2])
        for t in range(4):
            r = TOP + 8 * t
            here = visc[i + 1, pl.ds(r, 8), :]
            before, after = y_shifts(4, i, t, ends(joined, slot_of(0, i, t)))
            sums = [here + other for other in (
                visc[i, pl.ds(r, 8), :], visc[i + 2, pl.ds(r, 8), :],
                visc[i + 1, pl.ds(r - 1, 8), :], visc[i + 1, pl.ds(r + 1, 8), :],
                before, after,
            )]
            twice = (sums[0] + sums[1]) + (sums[2] + sums[3]) + (sums[4] + sums[5])
            scale = 0.6 / twice
            rows = pl.ds(8 * t, 8)
            for j in range(6):
                wts[j, i, rows, :] = scale * sums[j]
            scl[i, rows, :] = scale
            diag[i, rows, :] = twice * (0.5 / 0.6)
            for k in range(3):
                rhs[k, i, rows, :] = (2.0 * scale) * force[k, i, rows, :]
        return 0

    lax.fori_loop(0, NX, weights, 0, unroll=2)

    def coarse_weights(x, _):
        for t in range(3):
            r = TOP + 8 * t
            here = hvisc[0, x, pl.ds(r, 8), :]
            sums = [here + other for other in (
                hvisc[0, x - 1, pl.ds(r, 8), :], hvisc[0, x + 1, pl.ds(r, 8), :],
                hvisc[0, x, pl.ds(r - 1, 8), :], hvisc[0, x, pl.ds(r + 1, 8), :],
                roll(here, 1), roll(here, NY - 1),
            )]
            twice = (sums[0] + sums[1]) + (sums[2] + sums[3]) + (sums[4] + sums[5])
            scale = jnp.where(here > 0.0, 0.6 / twice, 0.0)
            rows = pl.ds(8 * t, 8)
            for j in range(6):
                cwts[j, x - 1, rows, :] = scale * sums[j]
            cscl[x - 1, rows, :] = scale
        return 0


    def terms(here, around, sides, grad_scale):
        moves, spread = [], None
        for k in range(3):
            parts = [sides[j] * around[j][k] for j in range(6)]
            total = (parts[0] + parts[1]) + (parts[2] + parts[3]) + (parts[4] + parts[5])
            moves.append(total - grad_scale * (around[2 * k + 1][3] - around[2 * k][3]))
            d = around[2 * k + 1][k] - around[2 * k][k]
            spread = d if spread is None else spread + d
        return moves, spread

    def fine_terms(u, y_of, i, t):
        r = TOP + 8 * t
        rows = pl.ds(8 * t, 8)
        here = [u[k, i + 1, pl.ds(r, 8), :] for k in range(4)]
        ys = [y_of(k, i, t) for k in range(4)]
        around = (
            [u[k, i, pl.ds(r, 8), :] for k in range(4)],
            [u[k, i + 2, pl.ds(r, 8), :] for k in range(4)],
            [u[k, i + 1, pl.ds(r - 1, 8), :] for k in range(4)],
            [u[k, i + 1, pl.ds(r + 1, 8), :] for k in range(4)],
            [y[0] for y in ys],
            [y[1] for y in ys],
        )
        sides = [wts[j, i, rows, :] for j in range(6)]
        moves, spread = terms(here, around, sides, scl[i, rows, :])
        moves = [m + rhs[k, i, rows, :] for k, m in enumerate(moves)]
        return here, moves, spread

    def fine_update(u, y_of, i, t):
        here, moves, spread = fine_terms(u, y_of, i, t)
        new = [0.4 * here[k] + moves[k] for k in range(3)]
        new.append(here[3] - 0.25 * (visc[i + 1, pl.ds(TOP + 8 * t, 8), :] * spread))
        return new

    def joined_ends(low_pack, high_pack):
        joined = [join(low_pack[n], high_pack[n]) for n in range(2)]
        return lambda k, i, t: y_shifts(k, i, t, ends(joined[k // 2], slot_of(k, i, t)))

    def exchange(u, make, sent, received):
        def plane(i, packs):
            packs = list(packs)
            for t in range(4):
                new = make(i, t)
                for k in range(4):
                    u[k, i + 1, pl.ds(TOP + 8 * t, 8), :] = new[k]
                    packs[k // 2] = put(packs[k // 2], new[k], slot_of(k, i, t))
            return tuple(packs)

        packs = plane(NX - 1, plane(0, (nil, nil)))
        x_start, x_wait = x_pair(u)
        x_start()
        packs = lax.fori_loop(1, NX - 1, plane, packs, unroll=2)
        sent[0], sent[1] = packs
        z_start, z_wait = z_pair(u)
        z_start()
        y_start, y_wait = y_pair(sent, received)
        y_start()

        def wait():
            x_wait()
            z_wait()
            y_wait()

        return wait

    ends0 = joined_ends(yrecv0.at[0], yrecv0.at[1])
    wait = exchange(u1, lambda i, t: fine_update(u0, ends0, i, t), ysend.at[0], yrecv.at[0])
    rotate(u1)
    drain(3)
    visc_start, visc_wait = deep_exchange(0, *visc_refs)
    visc_start(1, 2)
    wait()
    visc_start(3)
    ends1 = joined_ends(yrecv.at[0, 0], yrecv.at[0, 1])
    wait = exchange(u2, lambda i, t: fine_update(u1, ends1, i, t), ysend.at[1], yrecv.at[1])
    rotate(u2)
    visc_wait()
    deep_unpack(hvisc, 1, *visc_refs)
    lax.fori_loop(1, HX - 1, coarse_weights, 0, unroll=2)

    def flat(ref, pp, t):
        rows = pl.ds(DEEP + 8 * t, 8)
        a, b = ref[CX + 2 * pp - 1, rows, :], ref[CX + 2 * pp, rows, :]
        return jnp.where(first_half, a, roll(b, NY // 2))

    scales = [[flat(cscl, pp, t) for t in range(2)] for pp in range(2)]
    wait()


    ends2 = joined_ends(yrecv.at[1, 0], yrecv.at[1, 1])

    def restrict(i, _):
        for t in range(4):
            sums = None
            for h in range(2):
                here, moves, spread = fine_terms(u2, ends2, 2 * i + h, t)
                d = diag[2 * i + h, pl.ds(8 * t, 8), :]
                parts = [d * (moves[k] - 0.6 * here[k]) for k in range(3)] + [spread]
                sums = parts if sums is None else [a + b for a, b in zip(sums, parts)]
            for k in range(4):
                tmp[k, i, pl.ds(8 * t, 8), :] = sums[k]
        return 0

    lax.fori_loop(0, CX, restrict, 0)
    for k in range(4):
        for pp in range(2):
            for t in range(2):
                factor = scales[pp][t] if k < 3 else -0.03125 * vx[0, pp, pl.ds(8 * t, 8), :]
                cx[k, pp, pl.ds(8 * t, 8), :] = factor * squeeze(
                    z_pairs(tmp.at[k, 2 * pp], t), z_pairs(tmp.at[k, 2 * pp + 1], t)
                )
    deep_pack(cx, cy, 4)
    flow_start, flow_wait = deep_exchange(1, *flow_refs)
    flow_start(1, 2, 3)

    def insert_ends(i, _):
        for t in range(4):
            rows = pl.ds(8 * t, 8)
            for k in range(4):
                yprev[k, i, rows, :], ynext[k, i, rows, :] = ends2(k, i, t)
        return 0

    lax.fori_loop(0, NX, insert_ends, 0, unroll=2)
    drain(1)
    flow_wait()
    deep_unpack(c1, 4, *flow_refs)

    def coarse_sweep(old, new, start, stop):
        def plane(x, _):
            for t in range(3):
                r = TOP + 8 * t
                rows = pl.ds(8 * t, 8)
                here = [old[k, x, pl.ds(r, 8), :] for k in range(4)]
                around = (
                    [old[k, x - 1, pl.ds(r, 8), :] for k in range(4)],
                    [old[k, x + 1, pl.ds(r, 8), :] for k in range(4)],
                    [old[k, x, pl.ds(r - 1, 8), :] for k in range(4)],
                    [old[k, x, pl.ds(r + 1, 8), :] for k in range(4)],
                    [roll(h, 1) for h in here],
                    [roll(h, NY - 1) for h in here],
                )
                sides = [cwts[j, x - 1, rows, :] for j in range(6)]
                moves, spread = terms(here, around, sides, 2.0 * cscl[x - 1, rows, :])
                source = [c1[k, x, pl.ds(r, 8), :] for k in range(4)]
                for k in range(3):
                    new[k, x, pl.ds(r, 8), :] = 0.4 * here[k] + (moves[k] + source[k])
                new[3, x, pl.ds(r, 8), :] = here[3] + (
                    source[3] - 0.125 * (hvisc[0, x, pl.ds(r, 8), :] * spread)
                )
            return 0

        lax.fori_loop(start, stop, plane, 0, unroll=2)

    coarse_sweep(c1, c2, 1, HX - 1)
    coarse_sweep(c2, c3, 2, HX - 2)
    coarse_sweep(c3, c4, 3, HX - 3)


    parents = (couple, jnp.where(lane == 0, NY - 1, lax.div(lane + 1, 2) - 1), lax.div(lane + 1, 2))

    def widen(ref, start, value):
        ref[pl.ds(start, 8, stride=2), :] = value
        ref[pl.ds(start + 1, 8, stride=2), :] = value

    def prolong(x, _):
        for k in range(4):
            for t in range(2):
                widen(grown.at[k, x], TOP + 16 * t, pick(c4[k, x + 3, pl.ds(OWN + 8 * t, 8), :], parents[0]))
        return 0

    def prolong_sides(x, _):
        for k in range(4):
            above = pick(c4[k, x + 3, pl.ds(TOP, 8), :], parents[0])
            grown[k, x, TOP - 1 : TOP, :] = above[DEEP - 1 : DEEP]
            below = pick(c4[k, x + 3, pl.ds(OWN + CZ - DEEP, 8), :], parents[0])
            grown[k, x, TOP + NZ : TOP + NZ + 1, :] = below[DEEP : DEEP + 1]
            for t in range(2):
                value = c4[k, x + 3, pl.ds(OWN + 8 * t, 8), :]
                widen(gprev.at[k, x - 1], 16 * t, pick(value, parents[1]))
                widen(gnext.at[k, x - 1], 16 * t, pick(value, parents[2]))
        return 0

    lax.fori_loop(0, CX + 2, prolong, 0, unroll=2)
    lax.fori_loop(1, CX + 1, prolong_sides, 0, unroll=2)

    def correct(i, _):
        half = lax.div(i + 1, 2)
        for k in range(4):
            for t in range(4):
                rows = pl.ds(TOP + 8 * t, 8)
                u3[k, i, rows, :] = u2[k, i, rows, :] + grown[k, half, rows, :]
            for r in (TOP - 1, TOP + NZ):
                u3[k, i, r : r + 1, :] = u2[k, i, r : r + 1, :] + grown[k, half, r : r + 1, :]
        return 0

    lax.fori_loop(1, NX + 1, correct, 0, unroll=2)
    for i, x in ((0, 0), (NX + 1, CX + 1)):
        for k in range(4):
            for t in range(4):
                rows = pl.ds(TOP + 8 * t, 8)
                u3[k, i, rows, :] = u2[k, i, rows, :] + grown[k, x, rows, :]

    def ends3(k, i, t):
        rows = pl.ds(8 * t, 8)
        half = i // 2 if isinstance(i, int) else lax.div(i, 2)
        return yprev[k, i, rows, :] + gprev[k, half, rows, :], ynext[k, i, rows, :] + gnext[k, half, rows, :]


    wait = exchange(u4, lambda i, t: fine_update(u3, ends3, i, t), ysend.at[2], yrecv.at[2])
    rotate(u4)
    drain()
    wait()
    ends4 = joined_ends(yrecv.at[2, 0], yrecv.at[2, 1])

    def stores(half):
        some = pl.ds(half * (NX // 2), NX // 2)
        return (
            pltpu.make_async_copy(out.at[0:3, some], vout.at[:, some], store_sem.at[0, half]),
            pltpu.make_async_copy(out.at[3, some], pout.at[some], store_sem.at[1, half]),
        )

    def last(i, _):
        for t in range(4):
            new = fine_update(u4, ends4, i, t)
            for k in range(4):
                out[k, i, pl.ds(8 * t, 8), :] = new[k]
        return 0

    for half in range(2):
        lax.fori_loop(half * (NX // 2), (half + 1) * (NX // 2), last, 0, unroll=2)
        for store in stores(half):
            store.start()
    for half in range(2):
        for store in stores(half):
            store.wait()


def cycle(size, velocity, pressure, viscosity, body_force):
    field = pltpu.VMEM((4, NX + 2, NZ + 16, NY), F32)
    small = pltpu.VMEM((4, HX, HZ + 16, NY), F32)
    anywhere = pl.BlockSpec(memory_space=pl.ANY)

    def deep_buffers(nf):
        return [
            pltpu.VMEM((nf, 2, CZ, NY), F32),
            pltpu.VMEM(((nf + 1) // 2, 8, NY), F32),
            pltpu.VMEM((2, nf, 2, CZ, NY), F32),
            pltpu.VMEM((3, nf, 2, 8, NY), F32),
            pltpu.VMEM((3, 2, (nf + 1) // 2, 8, NY), F32),
            pltpu.VMEM((3, 2, (nf + 1) // 2, 8, NY), F32),
        ]

    out = pl.pallas_call(
        functools.partial(kernel, size),
        out_shape=(
            jax.ShapeDtypeStruct((3, NX, NZ, NY), F32),
            jax.ShapeDtypeStruct((NX, NZ, NY), F32),
        ),
        in_specs=[anywhere] * 4,
        out_specs=(anywhere, anywhere),
        scratch_shapes=[
            field, field, field, field, field,
            pltpu.VMEM((NX + 2, NZ + 16, NY), F32),
            pltpu.VMEM((3, NX, NZ, NY), F32),
            pltpu.VMEM((1, HX, HZ + 16, NY), F32),
            small, small, small, small,
            pltpu.VMEM((6, NX, NZ, NY), F32),
            pltpu.VMEM((NX, NZ, NY), F32),
            pltpu.VMEM((NX, NZ, NY), F32),
            pltpu.VMEM((3, NX, NZ, NY), F32),
            pltpu.VMEM((6, HX - 2, HZ, NY), F32),
            pltpu.VMEM((HX - 2, HZ, NY), F32),
            pltpu.VMEM((4, CX, NZ, NY), F32),
            pltpu.VMEM((4, CX + 2, NZ + 16, NY), F32),
            pltpu.VMEM((4, CX, NZ, NY), F32),
            pltpu.VMEM((4, CX, NZ, NY), F32),
            pltpu.VMEM((5, NX, NZ, NY), F32),
            pltpu.VMEM((5, NX, NZ, NY), F32),
            pltpu.VMEM((4, NX, NZ, NY), F32),
            pltpu.VMEM((3, 8, NY), F32),
            pltpu.VMEM((2, 3, 8, NY), F32),
            pltpu.VMEM((3, 2, 8, NY), F32),
            pltpu.VMEM((3, 2, 2, 8, NY), F32),
            *deep_buffers(1),
            *deep_buffers(4),
            pltpu.SemaphoreType.DMA((FACES,)),
            pltpu.SemaphoreType.DMA((FACES,)),
            pltpu.SemaphoreType.DMA((2, len(AROUND))),
            pltpu.SemaphoreType.DMA((2, len(AROUND))),
            pltpu.SemaphoreType.DMA((4,)),
            pltpu.SemaphoreType.DMA((2, 2)),
        ],
        compiler_params=pltpu.CompilerParams(collective_id=0, has_side_effects=True),
        name="cycle",
    )(velocity, pressure, viscosity, body_force)
    return out[0], out[1]


def solution(mesh):
    return jax.shard_map(
        functools.partial(cycle, dict(mesh.shape)),
        mesh=mesh,
        in_specs=(
            P(None, "gx", "gz", "gy"),
            P("gx", "gz", "gy"),
            P("gx", "gz", "gy"),
            P(None, "gx", "gz", "gy"),
        ),
        out_specs=(P(None, "gx", "gz", "gy"), P("gx", "gz", "gy")),
        check_vma=False,
    )
```

```python
import functools
import itertools

import jax
import jax.numpy as jnp
from jax import lax
from jax.experimental import pallas as pl
from jax.experimental.pallas import tpu as pltpu
from jax.sharding import PartitionSpec as P

MESH = pl.DeviceIdType.MESH
F32 = jnp.float32
NX, NZ, NY = 8, 32, 128
CX, CZ = 4, 16
DEEP = 4
HX, HZ = CX + 2 * DEEP, CZ + 2 * DEEP
TOP = 8
OWN = TOP + DEEP
AXES = ("gx", "gy", "gz")
AROUND = sorted(
    (d for d in itertools.product((-1, 0, 1), repeat=3) if any(d)),
    key=lambda d: (d[1:] != (0, 0), -sum(map(abs, d))),
)
FACES = 2 * (2 + 2 + 1 + 3 * 3)


def kernel(
    size, vel, prs, vis, frc, vout, pout,
    u0, u1, u2, u3, u4, visc, force, hvisc, c1, c2, c3, c4,
    wts, scl, diag, rhs, cwts, cscl, tmp, grown, gprev, gnext, yprev, ynext,
    ysend0, yrecv0, ysend, yrecv,
    vx, vy, vxb, vzb, vyc, vyz, cx, cy, cxb, czb, cyc, cyz,
    send_sem, recv_sem, deep_send, deep_recv, load_sem,
):
    at = {axis: lax.axis_index(axis) for axis in AXES}
    has = {}
    for axis in AXES:
        has[axis, 1] = at[axis] < size[axis] - 1
        has[axis, -1] = at[axis] > 0
    lane = lax.broadcasted_iota(jnp.int32, (8, NY), 1)
    row = lax.broadcasted_iota(jnp.int32, (8, NY), 0)
    even = lax.rem(lane, 2) == 0
    couple = lax.div(lane, 2)
    nil = jnp.zeros((8, NY), F32)
    count = [0]
    pending = []

    def drain(keep=0):
        while len(pending) > keep:
            pending.pop(0)()

    def roll(value, shift):
        return pltpu.roll(value, shift % NY if isinstance(shift, int) else shift, 1)

    def pick(value, index):
        return jnp.take_along_axis(value, index, axis=1, mode="promise_in_bounds")

    def beside(axis, sign):
        return lax.rem(at[axis] + size[axis] + sign, size[axis])

    def exists(offset, sign=1):
        found = None
        for axis, d in zip(AXES, offset):
            if d:
                one = has[axis, sign * d]
                found = one if found is None else found & one
        return found


    def pair(axis, high_face, low_halo, low_face, high_halo):
        slot = count[0]
        count[0] += 2

        def make(k):
            src, dst, sign = ((high_face, low_halo, 1), (low_face, high_halo, -1))[k]
            return pltpu.make_async_remote_copy(
                src_ref=src, dst_ref=dst,
                send_sem=send_sem.at[slot + k], recv_sem=recv_sem.at[slot + k],
                device_id={axis: beside(axis, sign)}, device_id_type=MESH,
            )

        def each(sign, act):
            @pl.when(has[axis, sign])
            def _():
                act(make(0))

            @pl.when(has[axis, -sign])
            def _():
                act(make(1))

        pending.append(lambda: each(1, lambda c: c.wait_send()))
        return (lambda: each(1, lambda c: c.start())), (lambda: each(-1, lambda c: c.wait_recv()))

    def deep_parts(d, xs, ys, xb, zb, yc, yz):
        dx, dy, dz = d
        if dy == 0 and dz == 0:
            return xs, xb.at[0 if dx > 0 else 1]
        if dy == 0:
            if dz > 0:
                return xs.at[:, :, CZ - DEEP : CZ, :], zb.at[1 - dx, :, :, 0:DEEP, :]
            return xs.at[:, :, 0:DEEP, :], zb.at[1 - dx, :, :, DEEP : 2 * DEEP, :]
        side = 0 if dy > 0 else 1
        if dz == 0:
            return ys, yc.at[1 - dx, side]
        if dz > 0:
            return ys.at[:, DEEP : 2 * DEEP, :], yz.at[1 - dx, side, :, 0:DEEP, :]
        return ys.at[:, 0:DEEP, :], yz.at[1 - dx, side, :, DEEP : 2 * DEEP, :]

    def deep_exchange(which, *refs):
        def make(k):
            d = AROUND[k]
            src, dst = deep_parts(d, *refs)
            return pltpu.make_async_remote_copy(
                src_ref=src, dst_ref=dst,
                send_sem=deep_send.at[which, k], recv_sem=deep_recv.at[which, k],
                device_id={axis: beside(axis, s) for axis, s in zip(AXES, d) if s}, device_id_type=MESH,
            )

        def each(sign, act, hops=(1, 2, 3)):
            for k, d in enumerate(AROUND):
                if sum(map(abs, d)) in hops:
                    @pl.when(exists(d, sign))
                    def _():
                        act(make(k))

        def start(*hops):
            each(1, lambda c: c.start(), hops)

        pending.append(lambda: each(1, lambda c: c.wait_send()))
        return start, (lambda *hops: each(-1, lambda c: c.wait_recv(), hops))

    zs = pl.ds(TOP, NZ)
    planes = pl.ds(1, NX)

    def x_pair(u):
        return pair("gx", u.at[:, NX, zs, :], u.at[:, 0, zs, :], u.at[:, 1, zs, :], u.at[:, NX + 1, zs, :])

    def z_pair(u):
        return pair(
            "gz", u.at[:, planes, TOP + NZ - 1, :], u.at[:, planes, TOP - 1, :],
            u.at[:, planes, TOP, :], u.at[:, planes, TOP + NZ, :],
        )

    def y_pair(sent, received):
        return pair("gy", sent, received.at[0], sent, received.at[1])


    loads = [
        pltpu.make_async_copy(vel, u0.at[0:3, planes, zs, :], load_sem.at[0]),
        pltpu.make_async_copy(prs, u0.at[3, planes, zs, :], load_sem.at[1]),
        pltpu.make_async_copy(vis, visc.at[planes, zs, :], load_sem.at[2]),
        pltpu.make_async_copy(frc, force, load_sem.at[3]),
    ]
    for load in loads:
        load.start()

    barrier = pltpu.get_barrier_semaphore()
    total = jnp.int32(0)
    for axis in AXES:
        for sign in (1, -1):
            @pl.when(has[axis, sign])
            def _():
                pl.semaphore_signal(barrier, inc=1, device_id={axis: beside(axis, sign)}, device_id_type=MESH)
            total = total + has[axis, sign].astype(jnp.int32)

    def zero(ref):
        ref[...] = jnp.zeros(ref.shape, F32)

    fields = (u0, u1, u2, u4)
    low, high = TOP - 1, TOP + NZ

    def edges(axis, sign, refs):
        @pl.when(jnp.logical_not(has[axis, sign]))
        def _():
            for ref in refs:
                zero(ref)

    edges("gx", -1, [u.at[:, 0, zs, :] for u in fields] + [visc.at[0, zs, :]])
    edges("gx", 1, [u.at[:, NX + 1, zs, :] for u in fields] + [visc.at[NX + 1, zs, :]])
    edges("gz", -1, [u.at[:, planes, low : low + 1, :] for u in fields] + [visc.at[planes, low : low + 1, :]])
    edges("gz", 1, [u.at[:, planes, high : high + 1, :] for u in fields] + [visc.at[planes, high : high + 1, :]])
    edges("gy", -1, [yrecv0.at[0]] + [yrecv.at[s, 0] for s in range(3)])
    edges("gy", 1, [yrecv0.at[1]] + [yrecv.at[s, 1] for s in range(3)])

    for load in loads[:3]:
        load.wait()


    def slot_of(k, i, t):
        return (k % 2) * 32 + t * 8 + i

    def put(pack, value, slot):
        return jnp.where(couple == slot, roll(value, 2 * slot + 1), pack)

    def join(from_low, from_high):
        return jnp.where(even, roll(from_high, NY - 1), roll(from_low, 1))

    def ends(joined, slot):
        return roll(joined, NY - 1 - 2 * slot)

    def y_shifts(k, i, t, end):
        rows = pl.ds(8 * t, 8)
        return jnp.where(lane == 0, end, yprev[k, i, rows, :]), jnp.where(lane == NY - 1, end, ynext[k, i, rows, :])

    def rotate(u, more=None):
        def plane(i, _):
            for t in range(4):
                for k in range(4 if more is None else 5):
                    rows = pl.ds(TOP + 8 * t, 8)
                    value = u[k, i + 1, rows, :] if k < 4 else more[i + 1, rows, :]
                    yprev[k, i, pl.ds(8 * t, 8), :] = roll(value, 1)
                    ynext[k, i, pl.ds(8 * t, 8), :] = roll(value, NY - 1)
            return 0

        lax.fori_loop(0, NX, plane, 0, unroll=2)

    def first_pack(i, packs):
        a, b, c = packs
        for t in range(4):
            rows = pl.ds(TOP + 8 * t, 8)
            a = put(put(a, u0[0, i + 1, rows, :], slot_of(0, i, t)), u0[1, i + 1, rows, :], slot_of(1, i, t))
            b = put(put(b, u0[2, i + 1, rows, :], slot_of(2, i, t)), u0[3, i + 1, rows, :], slot_of(3, i, t))
            c = put(c, visc[i + 1, rows, :], slot_of(0, i, t))
        return a, b, c

    packs = lax.fori_loop(0, NX, first_pack, (nil, nil, nil), unroll=2)
    for n in range(3):
        ysend0[n] = packs[n]

    pl.semaphore_wait(barrier, total)
    first = [
        x_pair(u0),
        pair("gx", visc.at[NX, zs, :], visc.at[0, zs, :], visc.at[1, zs, :], visc.at[NX + 1, zs, :]),
        y_pair(ysend0, yrecv0),
        z_pair(u0),
        pair(
            "gz", visc.at[planes, TOP + NZ - 1, :], visc.at[planes, TOP - 1, :],
            visc.at[planes, TOP, :], visc.at[planes, TOP + NZ, :],
        ),
    ]
    for start, _ in first:
        start()


    doubled = jnp.bitwise_and(2 * lane, NY - 1)
    first_half = lane < NY // 2

    def z_pairs(ref, t):
        return ref[pl.ds(16 * t, 8, stride=2), :] + ref[pl.ds(16 * t + 1, 8, stride=2), :]

    def squeeze(a, b):
        a = a + roll(a, NY - 1)
        b = b + roll(b, NY - 1)
        return jnp.where(first_half, pick(a, doubled), pick(b, doubled))

    octet, fore = lax.div(lane, 2 * DEEP), lax.rem(lane, 2 * DEEP) < DEEP

    def deep_slot(f, pp, t):
        return (f % 2) * 4 + t * 2 + pp

    def deep_pack(xs, ys, nf):
        for n in range((nf + 1) // 2):
            pack = nil
            for f in range(2 * n, min(2 * n + 2, nf)):
                for pp in range(2):
                    for t in range(2):
                        s = deep_slot(f, pp, t)
                        first = fore & (lax.rem(octet, 8) == s)
                        last = jnp.logical_not(fore) & (lax.rem(octet + 1, 8) == s)
                        pack = jnp.where(first | last, roll(xs[f, pp, pl.ds(8 * t, 8), :], 8 * s), pack)
            ys[n] = pack

    def lay_own(value, odd):
        return roll(value, NY // 2) if odd else value

    def near_unpack(h, xs, ys, xb, zb, yc, yz):
        sides = jnp.where(fore, yc[1, 1, 0], yc[1, 0, 0])
        for i in range(CX):
            pp, odd = i // 2, i % 2
            for t in range(2):
                own = lay_own(xs[0, pp, pl.ds(8 * t, 8), :], odd)
                ends_here = roll(sides, NY // 2 - 8 * (deep_slot(0, pp, t) + 8 * odd))
                h[0, CX + i, pl.ds(OWN + 8 * t, 8), :] = jnp.where(first_half, own, ends_here)
            both = lay_own(zb[1, 0, pp], odd)
            h[0, CX + i, pl.ds(TOP, DEEP), :] = both[0:DEEP]
            h[0, CX + i, pl.ds(OWN + CZ, DEEP), :] = both[DEEP : 2 * DEEP]
        for t in range(2):
            rows = pl.ds(8 * t, 8)
            h[0, CX - 1, pl.ds(OWN + 8 * t, 8), :] = lay_own(xb[0, 0, 1, rows, :], 1)
            h[0, 2 * CX, pl.ds(OWN + 8 * t, 8), :] = lay_own(xb[1, 0, 0, rows, :], 0)

    def deep_unpack(h, nf, xs, ys, xb, zb, yc, yz):
        for dx in range(3):
            middle, corner = [], []
            for n in range((nf + 1) // 2):
                middle.append(jnp.where(fore, yc[dx, 1, n], yc[dx, 0, n]))
                value = jnp.where(fore, yz[dx, 1, n], yz[dx, 0, n])
                corner.append(jnp.where(row < DEEP, roll(value, -4 * DEEP), value))
            block = xs if dx == 1 else xb.at[0 if dx == 0 else 1]

            def lay(value, odd, s, sides):
                return jnp.where(first_half, lay_own(value, odd), roll(sides, NY // 2 - 8 * (s + 8 * odd)))

            for f in range(nf):
                for i in range(CX):
                    pp, odd, x = i // 2, i % 2, dx * CX + i
                    for t in range(2):
                        h[f, x, pl.ds(OWN + 8 * t, 8), :] = lay(
                            block[f, pp, pl.ds(8 * t, 8), :], odd, deep_slot(f, pp, t), middle[f // 2]
                        )
                    both = lay(zb[dx, f, pp], odd, deep_slot(f, pp, 0), corner[f // 2])
                    h[f, x, pl.ds(TOP, DEEP), :] = both[0:DEEP]
                    h[f, x, pl.ds(OWN + CZ, DEEP), :] = both[DEEP : 2 * DEEP]

    def average(i, _):
        for t in range(4):
            rows = pl.ds(TOP + 8 * t, 8)
            tmp[0, i, pl.ds(8 * t, 8), :] = visc[2 * i + 1, rows, :] + visc[2 * i + 2, rows, :]
        return 0

    lax.fori_loop(0, CX, average, 0, unroll=True)
    for pp in range(2):
        for t in range(2):
            vx[0, pp, pl.ds(8 * t, 8), :] = 0.125 * squeeze(
                z_pairs(tmp.at[0, 2 * pp], t), z_pairs(tmp.at[0, 2 * pp + 1], t)
            )
    deep_pack(vx, vy, 1)
    visc_refs = (vx, vy, vxb, vzb, vyc, vyz)
    flow_refs = (cx, cy, cxb, czb, cyc, cyz)
    for refs in (visc_refs, flow_refs):
        for d in AROUND:
            @pl.when(jnp.logical_not(exists(d, -1)))
            def _():
                zero(deep_parts(d, *refs)[1])

    rotate(u0, visc)
    loads[3].wait()
    for _, wait in first:
        wait()


    def weights(i, _):
        joined = join(yrecv0[0, 2], yrecv0[1, 2])
        for t in range(4):
            r = TOP + 8 * t
            here = visc[i + 1, pl.ds(r, 8), :]
            before, after = y_shifts(4, i, t, ends(joined, slot_of(0, i, t)))
            sums = [here + other for other in (
                visc[i, pl.ds(r, 8), :], visc[i + 2, pl.ds(r, 8), :],
                visc[i + 1, pl.ds(r - 1, 8), :], visc[i + 1, pl.ds(r + 1, 8), :],
                before, after,
            )]
            twice = (sums[0] + sums[1]) + (sums[2] + sums[3]) + (sums[4] + sums[5])
            scale = 0.6 / twice
            rows = pl.ds(8 * t, 8)
            for j in range(6):
                wts[j, i, rows, :] = scale * sums[j]
            scl[i, rows, :] = scale
            diag[i, rows, :] = twice * (0.5 / 0.6)
            for k in range(3):
                rhs[k, i, rows, :] = (2.0 * scale) * force[k, i, rows, :]
        return 0

    lax.fori_loop(0, NX, weights, 0, unroll=2)

    def coarse_weights(x, _):
        for t in range(3):
            r = TOP + 8 * t
            here = hvisc[0, x, pl.ds(r, 8), :]
            sums = [here + other for other in (
                hvisc[0, x - 1, pl.ds(r, 8), :], hvisc[0, x + 1, pl.ds(r, 8), :],
                hvisc[0, x, pl.ds(r - 1, 8), :], hvisc[0, x, pl.ds(r + 1, 8), :],
                roll(here, 1), roll(here, NY - 1),
            )]
            twice = (sums[0] + sums[1]) + (sums[2] + sums[3]) + (sums[4] + sums[5])
            scale = jnp.where(here > 0.0, 0.6 / twice, 0.0)
            rows = pl.ds(8 * t, 8)
            for j in range(6):
                cwts[j, x - 1, rows, :] = scale * sums[j]
            cscl[x - 1, rows, :] = scale
        return 0


    def terms(here, around, sides, grad_scale):
        moves, spread = [], None
        for k in range(3):
            parts = [sides[j] * around[j][k] for j in range(6)]
            total = (parts[0] + parts[1]) + (parts[2] + parts[3]) + (parts[4] + parts[5])
            moves.append(total - grad_scale * (around[2 * k + 1][3] - around[2 * k][3]))
            d = around[2 * k + 1][k] - around[2 * k][k]
            spread = d if spread is None else spread + d
        return moves, spread

    def fine_terms(u, y_of, i, t):
        r = TOP + 8 * t
        rows = pl.ds(8 * t, 8)
        here = [u[k, i + 1, pl.ds(r, 8), :] for k in range(4)]
        ys = [y_of(k, i, t) for k in range(4)]
        around = (
            [u[k, i, pl.ds(r, 8), :] for k in range(4)],
            [u[k, i + 2, pl.ds(r, 8), :] for k in range(4)],
            [u[k, i + 1, pl.ds(r - 1, 8), :] for k in range(4)],
            [u[k, i + 1, pl.ds(r + 1, 8), :] for k in range(4)],
            [y[0] for y in ys],
            [y[1] for y in ys],
        )
        sides = [wts[j, i, rows, :] for j in range(6)]
        moves, spread = terms(here, around, sides, scl[i, rows, :])
        moves = [m + rhs[k, i, rows, :] for k, m in enumerate(moves)]
        return here, moves, spread

    def fine_update(u, y_of, i, t):
        here, moves, spread = fine_terms(u, y_of, i, t)
        new = [0.4 * here[k] + moves[k] for k in range(3)]
        new.append(here[3] - 0.25 * (visc[i + 1, pl.ds(TOP + 8 * t, 8), :] * spread))
        return new

    def joined_ends(low_pack, high_pack):
        joined = [join(low_pack[n], high_pack[n]) for n in range(2)]
        return lambda k, i, t: y_shifts(k, i, t, ends(joined[k // 2], slot_of(k, i, t)))

    def exchange(u, make, sent, received):
        def plane(i, packs):
            packs = list(packs)
            for t in range(4):
                new = make(i, t)
                for k in range(4):
                    u[k, i + 1, pl.ds(TOP + 8 * t, 8), :] = new[k]
                    packs[k // 2] = put(packs[k // 2], new[k], slot_of(k, i, t))
            return tuple(packs)

        packs = plane(NX - 1, plane(0, (nil, nil)))
        x_start, x_wait = x_pair(u)
        x_start()
        packs = lax.fori_loop(1, NX - 1, plane, packs, unroll=2)
        sent[0], sent[1] = packs
        z_start, z_wait = z_pair(u)
        z_start()
        y_start, y_wait = y_pair(sent, received)
        y_start()

        def wait():
            x_wait()
            z_wait()
            y_wait()

        return wait

    ends0 = joined_ends(yrecv0.at[0], yrecv0.at[1])
    wait = exchange(u1, lambda i, t: fine_update(u0, ends0, i, t), ysend.at[0], yrecv.at[0])
    rotate(u1)
    drain(3)
    visc_start, visc_wait = deep_exchange(0, *visc_refs)
    visc_start(1, 2)
    wait()
    visc_start(3)
    ends1 = joined_ends(yrecv.at[0, 0], yrecv.at[0, 1])
    wait = exchange(u2, lambda i, t: fine_update(u1, ends1, i, t), ysend.at[1], yrecv.at[1])
    rotate(u2)
    visc_wait(1)
    near_unpack(hvisc, *visc_refs)
    lax.fori_loop(CX, 2 * CX, coarse_weights, 0, unroll=2)

    def flat(ref, pp, t):
        rows = pl.ds(DEEP + 8 * t, 8)
        a, b = ref[CX + 2 * pp - 1, rows, :], ref[CX + 2 * pp, rows, :]
        return jnp.where(first_half, a, roll(b, NY // 2))

    scales = [[flat(cscl, pp, t) for t in range(2)] for pp in range(2)]
    wait()


    ends2 = joined_ends(yrecv.at[1, 0], yrecv.at[1, 1])

    def restrict(i, _):
        for t in range(4):
            sums = None
            for h in range(2):
                here, moves, spread = fine_terms(u2, ends2, 2 * i + h, t)
                d = diag[2 * i + h, pl.ds(8 * t, 8), :]
                parts = [d * (moves[k] - 0.6 * here[k]) for k in range(3)] + [spread]
                sums = parts if sums is None else [a + b for a, b in zip(sums, parts)]
            for k in range(4):
                tmp[k, i, pl.ds(8 * t, 8), :] = sums[k]
        return 0

    lax.fori_loop(0, CX, restrict, 0)
    for k in range(4):
        for pp in range(2):
            for t in range(2):
                factor = scales[pp][t] if k < 3 else -0.03125 * vx[0, pp, pl.ds(8 * t, 8), :]
                cx[k, pp, pl.ds(8 * t, 8), :] = factor * squeeze(
                    z_pairs(tmp.at[k, 2 * pp], t), z_pairs(tmp.at[k, 2 * pp + 1], t)
                )
    deep_pack(cx, cy, 4)
    flow_start, flow_wait = deep_exchange(1, *flow_refs)
    flow_start(1, 2, 3)

    def insert_ends(i, _):
        for t in range(4):
            rows = pl.ds(8 * t, 8)
            for k in range(4):
                yprev[k, i, rows, :], ynext[k, i, rows, :] = ends2(k, i, t)
        return 0

    lax.fori_loop(0, NX, insert_ends, 0, unroll=2)
    visc_wait(2, 3)
    deep_unpack(hvisc, 1, *visc_refs)
    lax.fori_loop(1, HX - 1, coarse_weights, 0, unroll=2)
    drain(1)
    flow_wait(1, 2, 3)
    deep_unpack(c1, 4, *flow_refs)

    def coarse_sweep(old, new, start, stop):
        def plane(x, _):
            for t in range(3):
                r = TOP + 8 * t
                rows = pl.ds(8 * t, 8)
                here = [old[k, x, pl.ds(r, 8), :] for k in range(4)]
                around = (
                    [old[k, x - 1, pl.ds(r, 8), :] for k in range(4)],
                    [old[k, x + 1, pl.ds(r, 8), :] for k in range(4)],
                    [old[k, x, pl.ds(r - 1, 8), :] for k in range(4)],
                    [old[k, x, pl.ds(r + 1, 8), :] for k in range(4)],
                    [roll(h, 1) for h in here],
                    [roll(h, NY - 1) for h in here],
                )
                sides = [cwts[j, x - 1, rows, :] for j in range(6)]
                moves, spread = terms(here, around, sides, 2.0 * cscl[x - 1, rows, :])
                source = [c1[k, x, pl.ds(r, 8), :] for k in range(4)]
                for k in range(3):
                    new[k, x, pl.ds(r, 8), :] = 0.4 * here[k] + (moves[k] + source[k])
                new[3, x, pl.ds(r, 8), :] = here[3] + (
                    source[3] - 0.125 * (hvisc[0, x, pl.ds(r, 8), :] * spread)
                )
            return 0

        lax.fori_loop(start, stop, plane, 0, unroll=2)

    coarse_sweep(c1, c2, 1, HX - 1)
    coarse_sweep(c2, c3, 2, HX - 2)
    coarse_sweep(c3, c4, 3, HX - 3)


    parents = (couple, jnp.where(lane == 0, NY - 1, lax.div(lane + 1, 2) - 1), lax.div(lane + 1, 2))

    def widen(ref, start, value):
        ref[pl.ds(start, 8, stride=2), :] = value
        ref[pl.ds(start + 1, 8, stride=2), :] = value

    def prolong(x, _):
        for k in range(4):
            for t in range(2):
                widen(grown.at[k, x], TOP + 16 * t, pick(c4[k, x + 3, pl.ds(OWN + 8 * t, 8), :], parents[0]))
        return 0

    def prolong_sides(x, _):
        for k in range(4):
            above = pick(c4[k, x + 3, pl.ds(TOP, 8), :], parents[0])
            grown[k, x, TOP - 1 : TOP, :] = above[DEEP - 1 : DEEP]
            below = pick(c4[k, x + 3, pl.ds(OWN + CZ - DEEP, 8), :], parents[0])
            grown[k, x, TOP + NZ : TOP + NZ + 1, :] = below[DEEP : DEEP + 1]
            for t in range(2):
                value = c4[k, x + 3, pl.ds(OWN + 8 * t, 8), :]
                widen(gprev.at[k, x - 1], 16 * t, pick(value, parents[1]))
                widen(gnext.at[k, x - 1], 16 * t, pick(value, parents[2]))
        return 0

    lax.fori_loop(0, CX + 2, prolong, 0, unroll=2)
    lax.fori_loop(1, CX + 1, prolong_sides, 0, unroll=2)

    def correct(i, _):
        half = lax.div(i + 1, 2)
        for k in range(4):
            for t in range(4):
                rows = pl.ds(TOP + 8 * t, 8)
                u3[k, i, rows, :] = u2[k, i, rows, :] + grown[k, half, rows, :]
            for r in (TOP - 1, TOP + NZ):
                u3[k, i, r : r + 1, :] = u2[k, i, r : r + 1, :] + grown[k, half, r : r + 1, :]
        return 0

    lax.fori_loop(1, NX + 1, correct, 0, unroll=2)
    for i, x in ((0, 0), (NX + 1, CX + 1)):
        for k in range(4):
            for t in range(4):
                rows = pl.ds(TOP + 8 * t, 8)
                u3[k, i, rows, :] = u2[k, i, rows, :] + grown[k, x, rows, :]

    def ends3(k, i, t):
        rows = pl.ds(8 * t, 8)
        half = i // 2 if isinstance(i, int) else lax.div(i, 2)
        return yprev[k, i, rows, :] + gprev[k, half, rows, :], ynext[k, i, rows, :] + gnext[k, half, rows, :]


    wait = exchange(u4, lambda i, t: fine_update(u3, ends3, i, t), ysend.at[2], yrecv.at[2])
    rotate(u4)
    drain()
    wait()
    ends4 = joined_ends(yrecv.at[2, 0], yrecv.at[2, 1])

    def last(i, _):
        for t in range(4):
            new = fine_update(u4, ends4, i, t)
            for k in range(4):
                if k < 3:
                    vout[k, i, pl.ds(8 * t, 8), :] = new[k]
                else:
                    pout[i, pl.ds(8 * t, 8), :] = new[k]
        return 0

    lax.fori_loop(0, NX, last, 0, unroll=2)


def cycle(size, velocity, pressure, viscosity, body_force):
    field = pltpu.VMEM((4, NX + 2, NZ + 16, NY), F32)
    small = pltpu.VMEM((4, HX, HZ + 16, NY), F32)
    anywhere = pl.BlockSpec(memory_space=pl.ANY)

    def deep_buffers(nf):
        return [
            pltpu.VMEM((nf, 2, CZ, NY), F32),
            pltpu.VMEM(((nf + 1) // 2, 8, NY), F32),
            pltpu.VMEM((2, nf, 2, CZ, NY), F32),
            pltpu.VMEM((3, nf, 2, 8, NY), F32),
            pltpu.VMEM((3, 2, (nf + 1) // 2, 8, NY), F32),
            pltpu.VMEM((3, 2, (nf + 1) // 2, 8, NY), F32),
        ]

    out = pl.pallas_call(
        functools.partial(kernel, size),
        out_shape=(
            jax.ShapeDtypeStruct((3, NX, NZ, NY), F32),
            jax.ShapeDtypeStruct((NX, NZ, NY), F32),
        ),
        in_specs=[anywhere] * 4,
        out_specs=(pl.BlockSpec(memory_space=pltpu.VMEM),) * 2,
        scratch_shapes=[
            field, field, field, field, field,
            pltpu.VMEM((NX + 2, NZ + 16, NY), F32),
            pltpu.VMEM((3, NX, NZ, NY), F32),
            pltpu.VMEM((1, HX, HZ + 16, NY), F32),
            small, small, small, small,
            pltpu.VMEM((6, NX, NZ, NY), F32),
            pltpu.VMEM((NX, NZ, NY), F32),
            pltpu.VMEM((NX, NZ, NY), F32),
            pltpu.VMEM((3, NX, NZ, NY), F32),
            pltpu.VMEM((6, HX - 2, HZ, NY), F32),
            pltpu.VMEM((HX - 2, HZ, NY), F32),
            pltpu.VMEM((4, CX, NZ, NY), F32),
            pltpu.VMEM((4, CX + 2, NZ + 16, NY), F32),
            pltpu.VMEM((4, CX, NZ, NY), F32),
            pltpu.VMEM((4, CX, NZ, NY), F32),
            pltpu.VMEM((5, NX, NZ, NY), F32),
            pltpu.VMEM((5, NX, NZ, NY), F32),
            pltpu.VMEM((3, 8, NY), F32),
            pltpu.VMEM((2, 3, 8, NY), F32),
            pltpu.VMEM((3, 2, 8, NY), F32),
            pltpu.VMEM((3, 2, 2, 8, NY), F32),
            *deep_buffers(1),
            *deep_buffers(4),
            pltpu.SemaphoreType.DMA((FACES,)),
            pltpu.SemaphoreType.DMA((FACES,)),
            pltpu.SemaphoreType.DMA((2, len(AROUND))),
            pltpu.SemaphoreType.DMA((2, len(AROUND))),
            pltpu.SemaphoreType.DMA((4,)),
        ],
        compiler_params=pltpu.CompilerParams(collective_id=0, has_side_effects=True, vmem_limit_bytes=25165824),
        name="cycle",
    )(*[pltpu.with_memory_space_constraint(x, pltpu.HBM) for x in (velocity, pressure, viscosity, body_force)])
    return out[0], out[1]


def solution(mesh):
    return jax.shard_map(
        functools.partial(cycle, dict(mesh.shape)),
        mesh=mesh,
        in_specs=(
            P(None, "gx", "gz", "gy"),
            P("gx", "gz", "gy"),
            P("gx", "gz", "gy"),
            P(None, "gx", "gz", "gy"),
        ),
        out_specs=(P(None, "gx", "gz", "gy"), P("gx", "gz", "gy")),
        check_vma=False,
    )
```

```python
import functools
import itertools

import jax
import jax.numpy as jnp
from jax import lax
from jax.experimental import pallas as pl
from jax.experimental.pallas import tpu as pltpu
from jax.sharding import PartitionSpec as P

MESH = pl.DeviceIdType.MESH
F32 = jnp.float32
NX, NZ, NY = 8, 32, 128
CX, CZ = 4, 16
DEEP = 4
HX, HZ = CX + 2 * DEEP, CZ + 2 * DEEP
TOP = 8
OWN = TOP + DEEP
AXES = ("gx", "gy", "gz")
AROUND = sorted(
    (d for d in itertools.product((-1, 0, 1), repeat=3) if any(d)),
    key=lambda d: (d[1:] != (0, 0), -sum(map(abs, d))),
)
FACES = 2 * (2 + 2 + 1 + 3 * 3)


def kernel(
    size, vel, prs, vis, frc, vout, pout,
    u0, u1, u2, u3, u4, visc, force, hvisc, c1, c2, c3, c4,
    wts, scl, diag, rhs, cwts, cscl, tmp, grown, gprev, gnext, yprev, ynext,
    ysend0, yrecv0, ysend, yrecv,
    vx, vy, vxb, vzb, vyc, vyz, cx, cy, cxb, czb, cyc, cyz,
    send_sem, recv_sem, deep_send, deep_recv, load_sem,
):
    at = {axis: lax.axis_index(axis) for axis in AXES}
    has = {}
    for axis in AXES:
        has[axis, 1] = at[axis] < size[axis] - 1
        has[axis, -1] = at[axis] > 0
    lane = lax.broadcasted_iota(jnp.int32, (8, NY), 1)
    row = lax.broadcasted_iota(jnp.int32, (8, NY), 0)
    even = lax.rem(lane, 2) == 0
    couple = lax.div(lane, 2)
    nil = jnp.zeros((8, NY), F32)
    count = [0]
    pending = []

    def drain(keep=0):
        while len(pending) > keep:
            pending.pop(0)()

    def roll(value, shift):
        return pltpu.roll(value, shift % NY if isinstance(shift, int) else shift, 1)

    def pick(value, index):
        return jnp.take_along_axis(value, index, axis=1, mode="promise_in_bounds")

    def beside(axis, sign):
        return lax.rem(at[axis] + size[axis] + sign, size[axis])

    def exists(offset, sign=1):
        found = None
        for axis, d in zip(AXES, offset):
            if d:
                one = has[axis, sign * d]
                found = one if found is None else found & one
        return found


    def pair(axis, high_face, low_halo, low_face, high_halo):
        slot = count[0]
        count[0] += 2

        def make(k):
            src, dst, sign = ((high_face, low_halo, 1), (low_face, high_halo, -1))[k]
            return pltpu.make_async_remote_copy(
                src_ref=src, dst_ref=dst,
                send_sem=send_sem.at[slot + k], recv_sem=recv_sem.at[slot + k],
                device_id={axis: beside(axis, sign)}, device_id_type=MESH,
            )

        def each(sign, act):
            @pl.when(has[axis, sign])
            def _():
                act(make(0))

            @pl.when(has[axis, -sign])
            def _():
                act(make(1))

        pending.append(lambda: each(1, lambda c: c.wait_send()))
        return (lambda: each(1, lambda c: c.start())), (lambda: each(-1, lambda c: c.wait_recv()))

    def deep_parts(d, xs, ys, xb, zb, yc, yz):
        dx, dy, dz = d
        if dy == 0 and dz == 0:
            return xs, xb.at[0 if dx > 0 else 1]
        if dy == 0:
            if dz > 0:
                return xs.at[:, :, CZ - DEEP : CZ, :], zb.at[1 - dx, :, :, 0:DEEP, :]
            return xs.at[:, :, 0:DEEP, :], zb.at[1 - dx, :, :, DEEP : 2 * DEEP, :]
        side = 0 if dy > 0 else 1
        if dz == 0:
            return ys, yc.at[1 - dx, side]
        if dz > 0:
            return ys.at[:, DEEP : 2 * DEEP, :], yz.at[1 - dx, side, :, 0:DEEP, :]
        return ys.at[:, 0:DEEP, :], yz.at[1 - dx, side, :, DEEP : 2 * DEEP, :]

    def deep_exchange(which, *refs):
        def make(k):
            d = AROUND[k]
            src, dst = deep_parts(d, *refs)
            return pltpu.make_async_remote_copy(
                src_ref=src, dst_ref=dst,
                send_sem=deep_send.at[which, k], recv_sem=deep_recv.at[which, k],
                device_id={axis: beside(axis, s) for axis, s in zip(AXES, d) if s}, device_id_type=MESH,
            )

        def each(sign, act, hops=(1, 2, 3)):
            for k, d in enumerate(AROUND):
                if sum(map(abs, d)) in hops:
                    @pl.when(exists(d, sign))
                    def _():
                        act(make(k))

        def start(*hops):
            each(1, lambda c: c.start(), hops)

        pending.append(lambda: each(1, lambda c: c.wait_send()))
        return start, (lambda *hops: each(-1, lambda c: c.wait_recv(), hops))

    zs = pl.ds(TOP, NZ)
    planes = pl.ds(1, NX)

    def x_pair(u):
        return pair("gx", u.at[:, NX, zs, :], u.at[:, 0, zs, :], u.at[:, 1, zs, :], u.at[:, NX + 1, zs, :])

    def z_pair(u):
        return pair(
            "gz", u.at[:, planes, TOP + NZ - 1, :], u.at[:, planes, TOP - 1, :],
            u.at[:, planes, TOP, :], u.at[:, planes, TOP + NZ, :],
        )

    def y_pair(sent, received):
        return pair("gy", sent, received.at[0], sent, received.at[1])


    loads = [
        pltpu.make_async_copy(vel, u0.at[0:3, planes, zs, :], load_sem.at[0]),
        pltpu.make_async_copy(prs, u0.at[3, planes, zs, :], load_sem.at[1]),
        pltpu.make_async_copy(vis, visc.at[planes, zs, :], load_sem.at[2]),
        pltpu.make_async_copy(frc, force, load_sem.at[3]),
    ]
    for load in loads:
        load.start()

    barrier = pltpu.get_barrier_semaphore()
    total = jnp.int32(0)
    for axis in AXES:
        for sign in (1, -1):
            @pl.when(has[axis, sign])
            def _():
                pl.semaphore_signal(barrier, inc=1, device_id={axis: beside(axis, sign)}, device_id_type=MESH)
            total = total + has[axis, sign].astype(jnp.int32)

    def zero(ref):
        ref[...] = jnp.zeros(ref.shape, F32)

    fields = (u0, u1, u2, u4)
    low, high = TOP - 1, TOP + NZ

    def edges(axis, sign, refs):
        @pl.when(jnp.logical_not(has[axis, sign]))
        def _():
            for ref in refs:
                zero(ref)

    edges("gx", -1, [u.at[:, 0, zs, :] for u in fields] + [visc.at[0, zs, :]])
    edges("gx", 1, [u.at[:, NX + 1, zs, :] for u in fields] + [visc.at[NX + 1, zs, :]])
    edges("gz", -1, [u.at[:, planes, low : low + 1, :] for u in fields] + [visc.at[planes, low : low + 1, :]])
    edges("gz", 1, [u.at[:, planes, high : high + 1, :] for u in fields] + [visc.at[planes, high : high + 1, :]])
    edges("gy", -1, [yrecv0.at[0]] + [yrecv.at[s, 0] for s in range(3)])
    edges("gy", 1, [yrecv0.at[1]] + [yrecv.at[s, 1] for s in range(3)])

    for load in loads[:3]:
        load.wait()


    def slot_of(k, i, t):
        return (k % 2) * 32 + t * 8 + i

    def put(pack, value, slot):
        return jnp.where(couple == slot, roll(value, 2 * slot + 1), pack)

    def join(from_low, from_high):
        return jnp.where(even, roll(from_high, NY - 1), roll(from_low, 1))

    def ends(joined, slot):
        return roll(joined, NY - 1 - 2 * slot)

    def y_shifts(k, i, t, end):
        rows = pl.ds(8 * t, 8)
        return jnp.where(lane == 0, end, yprev[k, i, rows, :]), jnp.where(lane == NY - 1, end, ynext[k, i, rows, :])

    def rotate(u, more=None):
        def plane(i, _):
            for t in range(4):
                for k in range(4 if more is None else 5):
                    rows = pl.ds(TOP + 8 * t, 8)
                    value = u[k, i + 1, rows, :] if k < 4 else more[i + 1, rows, :]
                    yprev[k, i, pl.ds(8 * t, 8), :] = roll(value, 1)
                    ynext[k, i, pl.ds(8 * t, 8), :] = roll(value, NY - 1)
            return 0

        lax.fori_loop(0, NX, plane, 0, unroll=2)

    def first_pack(i, packs):
        a, b, c = packs
        for t in range(4):
            rows = pl.ds(TOP + 8 * t, 8)
            a = put(put(a, u0[0, i + 1, rows, :], slot_of(0, i, t)), u0[1, i + 1, rows, :], slot_of(1, i, t))
            b = put(put(b, u0[2, i + 1, rows, :], slot_of(2, i, t)), u0[3, i + 1, rows, :], slot_of(3, i, t))
            c = put(c, visc[i + 1, rows, :], slot_of(0, i, t))
        return a, b, c

    packs = lax.fori_loop(0, NX, first_pack, (nil, nil, nil), unroll=True)
    for n in range(3):
        ysend0[n] = packs[n]

    pl.semaphore_wait(barrier, total)
    first = [
        x_pair(u0),
        pair("gx", visc.at[NX, zs, :], visc.at[0, zs, :], visc.at[1, zs, :], visc.at[NX + 1, zs, :]),
        y_pair(ysend0, yrecv0),
        z_pair(u0),
        pair(
            "gz", visc.at[planes, TOP + NZ - 1, :], visc.at[planes, TOP - 1, :],
            visc.at[planes, TOP, :], visc.at[planes, TOP + NZ, :],
        ),
    ]
    for start, _ in first:
        start()


    doubled = jnp.bitwise_and(2 * lane, NY - 1)
    first_half = lane < NY // 2

    def z_pairs(ref, t):
        return ref[pl.ds(16 * t, 8, stride=2), :] + ref[pl.ds(16 * t + 1, 8, stride=2), :]

    def squeeze(a, b):
        a = a + roll(a, NY - 1)
        b = b + roll(b, NY - 1)
        return jnp.where(first_half, pick(a, doubled), pick(b, doubled))

    octet, fore = lax.div(lane, 2 * DEEP), lax.rem(lane, 2 * DEEP) < DEEP

    def deep_slot(f, pp, t):
        return (f % 2) * 4 + t * 2 + pp

    def deep_pack(xs, ys, nf):
        for n in range((nf + 1) // 2):
            pack = nil
            for f in range(2 * n, min(2 * n + 2, nf)):
                for pp in range(2):
                    for t in range(2):
                        s = deep_slot(f, pp, t)
                        first = fore & (lax.rem(octet, 8) == s)
                        last = jnp.logical_not(fore) & (lax.rem(octet + 1, 8) == s)
                        pack = jnp.where(first | last, roll(xs[f, pp, pl.ds(8 * t, 8), :], 8 * s), pack)
            ys[n] = pack

    def lay_own(value, odd):
        return roll(value, NY // 2) if odd else value

    def near_unpack(h, xs, ys, xb, zb, yc, yz):
        sides = jnp.where(fore, yc[1, 1, 0], yc[1, 0, 0])
        for i in range(CX):
            pp, odd = i // 2, i % 2
            for t in range(2):
                own = lay_own(xs[0, pp, pl.ds(8 * t, 8), :], odd)
                ends_here = roll(sides, NY // 2 - 8 * (deep_slot(0, pp, t) + 8 * odd))
                h[0, CX + i, pl.ds(OWN + 8 * t, 8), :] = jnp.where(first_half, own, ends_here)
            both = lay_own(zb[1, 0, pp], odd)
            h[0, CX + i, pl.ds(TOP, DEEP), :] = both[0:DEEP]
            h[0, CX + i, pl.ds(OWN + CZ, DEEP), :] = both[DEEP : 2 * DEEP]
        for t in range(2):
            rows = pl.ds(8 * t, 8)
            h[0, CX - 1, pl.ds(OWN + 8 * t, 8), :] = lay_own(xb[0, 0, 1, rows, :], 1)
            h[0, 2 * CX, pl.ds(OWN + 8 * t, 8), :] = lay_own(xb[1, 0, 0, rows, :], 0)

    def deep_unpack(h, nf, xs, ys, xb, zb, yc, yz):
        for dx in range(3):
            middle, corner = [], []
            for n in range((nf + 1) // 2):
                middle.append(jnp.where(fore, yc[dx, 1, n], yc[dx, 0, n]))
                value = jnp.where(fore, yz[dx, 1, n], yz[dx, 0, n])
                corner.append(jnp.where(row < DEEP, roll(value, -4 * DEEP), value))
            block = xs if dx == 1 else xb.at[0 if dx == 0 else 1]

            def lay(value, odd, s, sides):
                return jnp.where(first_half, lay_own(value, odd), roll(sides, NY // 2 - 8 * (s + 8 * odd)))

            for f in range(nf):
                for i in range(CX):
                    pp, odd, x = i // 2, i % 2, dx * CX + i
                    for t in range(2):
                        h[f, x, pl.ds(OWN + 8 * t, 8), :] = lay(
                            block[f, pp, pl.ds(8 * t, 8), :], odd, deep_slot(f, pp, t), middle[f // 2]
                        )
                    both = lay(zb[dx, f, pp], odd, deep_slot(f, pp, 0), corner[f // 2])
                    h[f, x, pl.ds(TOP, DEEP), :] = both[0:DEEP]
                    h[f, x, pl.ds(OWN + CZ, DEEP), :] = both[DEEP : 2 * DEEP]

    def average(i, _):
        for t in range(4):
            rows = pl.ds(TOP + 8 * t, 8)
            tmp[0, i, pl.ds(8 * t, 8), :] = visc[2 * i + 1, rows, :] + visc[2 * i + 2, rows, :]
        return 0

    lax.fori_loop(0, CX, average, 0, unroll=True)
    for pp in range(2):
        for t in range(2):
            vx[0, pp, pl.ds(8 * t, 8), :] = 0.125 * squeeze(
                z_pairs(tmp.at[0, 2 * pp], t), z_pairs(tmp.at[0, 2 * pp + 1], t)
            )
    deep_pack(vx, vy, 1)
    visc_refs = (vx, vy, vxb, vzb, vyc, vyz)
    flow_refs = (cx, cy, cxb, czb, cyc, cyz)
    for refs in (visc_refs, flow_refs):
        for d in AROUND:
            @pl.when(jnp.logical_not(exists(d, -1)))
            def _():
                zero(deep_parts(d, *refs)[1])

    rotate(u0, visc)
    loads[3].wait()
    for _, wait in first:
        wait()


    def weights(i, _):
        joined = join(yrecv0[0, 2], yrecv0[1, 2])
        for t in range(4):
            r = TOP + 8 * t
            here = visc[i + 1, pl.ds(r, 8), :]
            before, after = y_shifts(4, i, t, ends(joined, slot_of(0, i, t)))
            sums = [here + other for other in (
                visc[i, pl.ds(r, 8), :], visc[i + 2, pl.ds(r, 8), :],
                visc[i + 1, pl.ds(r - 1, 8), :], visc[i + 1, pl.ds(r + 1, 8), :],
                before, after,
            )]
            twice = (sums[0] + sums[1]) + (sums[2] + sums[3]) + (sums[4] + sums[5])
            scale = 0.6 / twice
            rows = pl.ds(8 * t, 8)
            for j in range(6):
                wts[j, i, rows, :] = scale * sums[j]
            scl[i, rows, :] = scale
            diag[i, rows, :] = twice * (0.5 / 0.6)
            for k in range(3):
                rhs[k, i, rows, :] = (2.0 * scale) * force[k, i, rows, :]
        return 0

    lax.fori_loop(0, NX, weights, 0, unroll=True)

    def coarse_weights(x, _):
        for t in range(3):
            r = TOP + 8 * t
            here = hvisc[0, x, pl.ds(r, 8), :]
            sums = [here + other for other in (
                hvisc[0, x - 1, pl.ds(r, 8), :], hvisc[0, x + 1, pl.ds(r, 8), :],
                hvisc[0, x, pl.ds(r - 1, 8), :], hvisc[0, x, pl.ds(r + 1, 8), :],
                roll(here, 1), roll(here, NY - 1),
            )]
            twice = (sums[0] + sums[1]) + (sums[2] + sums[3]) + (sums[4] + sums[5])
            scale = jnp.where(here > 0.0, 0.6 / twice, 0.0)
            rows = pl.ds(8 * t, 8)
            for j in range(6):
                cwts[j, x - 1, rows, :] = scale * sums[j]
            cscl[x - 1, rows, :] = scale
        return 0


    def terms(here, around, sides, grad_scale):
        moves, spread = [], None
        for k in range(3):
            parts = [sides[j] * around[j][k] for j in range(6)]
            total = (parts[0] + parts[1]) + (parts[2] + parts[3]) + (parts[4] + parts[5])
            moves.append(total - grad_scale * (around[2 * k + 1][3] - around[2 * k][3]))
            d = around[2 * k + 1][k] - around[2 * k][k]
            spread = d if spread is None else spread + d
        return moves, spread

    def fine_terms(u, y_of, i, t):
        r = TOP + 8 * t
        rows = pl.ds(8 * t, 8)
        here = [u[k, i + 1, pl.ds(r, 8), :] for k in range(4)]
        ys = [y_of(k, i, t) for k in range(4)]
        around = (
            [u[k, i, pl.ds(r, 8), :] for k in range(4)],
            [u[k, i + 2, pl.ds(r, 8), :] for k in range(4)],
            [u[k, i + 1, pl.ds(r - 1, 8), :] for k in range(4)],
            [u[k, i + 1, pl.ds(r + 1, 8), :] for k in range(4)],
            [y[0] for y in ys],
            [y[1] for y in ys],
        )
        sides = [wts[j, i, rows, :] for j in range(6)]
        moves, spread = terms(here, around, sides, scl[i, rows, :])
        moves = [m + rhs[k, i, rows, :] for k, m in enumerate(moves)]
        return here, moves, spread

    def fine_update(u, y_of, i, t):
        here, moves, spread = fine_terms(u, y_of, i, t)
        new = [0.4 * here[k] + moves[k] for k in range(3)]
        new.append(here[3] - 0.25 * (visc[i + 1, pl.ds(TOP + 8 * t, 8), :] * spread))
        return new

    def joined_ends(low_pack, high_pack):
        joined = [join(low_pack[n], high_pack[n]) for n in range(2)]
        return lambda k, i, t: y_shifts(k, i, t, ends(joined[k // 2], slot_of(k, i, t)))

    def exchange(u, make, sent, received):
        def plane(i, packs):
            packs = list(packs)
            for t in range(4):
                new = make(i, t)
                for k in range(4):
                    u[k, i + 1, pl.ds(TOP + 8 * t, 8), :] = new[k]
                    packs[k // 2] = put(packs[k // 2], new[k], slot_of(k, i, t))
            return tuple(packs)

        packs = plane(NX - 1, plane(0, (nil, nil)))
        x_start, x_wait = x_pair(u)
        x_start()
        packs = lax.fori_loop(1, NX - 1, plane, packs, unroll=3)
        sent[0], sent[1] = packs
        z_start, z_wait = z_pair(u)
        z_start()
        y_start, y_wait = y_pair(sent, received)
        y_start()

        def wait():
            x_wait()
            z_wait()
            y_wait()

        return wait

    ends0 = joined_ends(yrecv0.at[0], yrecv0.at[1])
    wait = exchange(u1, lambda i, t: fine_update(u0, ends0, i, t), ysend.at[0], yrecv.at[0])
    rotate(u1)
    drain(3)
    visc_start, visc_wait = deep_exchange(0, *visc_refs)
    visc_start(1, 2)
    wait()
    visc_start(3)
    ends1 = joined_ends(yrecv.at[0, 0], yrecv.at[0, 1])
    wait = exchange(u2, lambda i, t: fine_update(u1, ends1, i, t), ysend.at[1], yrecv.at[1])
    rotate(u2)
    visc_wait(1)
    near_unpack(hvisc, *visc_refs)
    lax.fori_loop(CX, 2 * CX, coarse_weights, 0, unroll=2)

    def flat(ref, pp, t):
        rows = pl.ds(DEEP + 8 * t, 8)
        a, b = ref[CX + 2 * pp - 1, rows, :], ref[CX + 2 * pp, rows, :]
        return jnp.where(first_half, a, roll(b, NY // 2))

    scales = [[flat(cscl, pp, t) for t in range(2)] for pp in range(2)]
    wait()


    ends2 = joined_ends(yrecv.at[1, 0], yrecv.at[1, 1])

    def restrict(i, _):
        for t in range(4):
            sums = None
            for h in range(2):
                here, moves, spread = fine_terms(u2, ends2, 2 * i + h, t)
                d = diag[2 * i + h, pl.ds(8 * t, 8), :]
                parts = [d * (moves[k] - 0.6 * here[k]) for k in range(3)] + [spread]
                sums = parts if sums is None else [a + b for a, b in zip(sums, parts)]
            for k in range(4):
                tmp[k, i, pl.ds(8 * t, 8), :] = sums[k]
        return 0

    lax.fori_loop(0, CX, restrict, 0, unroll=True)
    for k in range(4):
        for pp in range(2):
            for t in range(2):
                factor = scales[pp][t] if k < 3 else -0.03125 * vx[0, pp, pl.ds(8 * t, 8), :]
                cx[k, pp, pl.ds(8 * t, 8), :] = factor * squeeze(
                    z_pairs(tmp.at[k, 2 * pp], t), z_pairs(tmp.at[k, 2 * pp + 1], t)
                )
    deep_pack(cx, cy, 4)
    flow_start, flow_wait = deep_exchange(1, *flow_refs)
    flow_start(1, 2, 3)

    def insert_ends(i, _):
        for t in range(4):
            rows = pl.ds(8 * t, 8)
            for k in range(4):
                yprev[k, i, rows, :], ynext[k, i, rows, :] = ends2(k, i, t)
        return 0

    lax.fori_loop(0, NX, insert_ends, 0, unroll=2)
    visc_wait(2, 3)
    deep_unpack(hvisc, 1, *visc_refs)
    lax.fori_loop(1, HX - 1, coarse_weights, 0, unroll=2)
    drain(1)
    flow_wait(1, 2, 3)
    deep_unpack(c1, 4, *flow_refs)

    def coarse_sweep(old, new, start, stop):
        def plane(x, _):
            for t in range(3):
                r = TOP + 8 * t
                rows = pl.ds(8 * t, 8)
                here = [old[k, x, pl.ds(r, 8), :] for k in range(4)]
                around = (
                    [old[k, x - 1, pl.ds(r, 8), :] for k in range(4)],
                    [old[k, x + 1, pl.ds(r, 8), :] for k in range(4)],
                    [old[k, x, pl.ds(r - 1, 8), :] for k in range(4)],
                    [old[k, x, pl.ds(r + 1, 8), :] for k in range(4)],
                    [roll(h, 1) for h in here],
                    [roll(h, NY - 1) for h in here],
                )
                sides = [cwts[j, x - 1, rows, :] for j in range(6)]
                moves, spread = terms(here, around, sides, 2.0 * cscl[x - 1, rows, :])
                source = [c1[k, x, pl.ds(r, 8), :] for k in range(4)]
                for k in range(3):
                    new[k, x, pl.ds(r, 8), :] = 0.4 * here[k] + (moves[k] + source[k])
                new[3, x, pl.ds(r, 8), :] = here[3] + (
                    source[3] - 0.125 * (hvisc[0, x, pl.ds(r, 8), :] * spread)
                )
            return 0

        lax.fori_loop(start, stop, plane, 0, unroll=True)

    coarse_sweep(c1, c2, 1, HX - 1)
    coarse_sweep(c2, c3, 2, HX - 2)
    coarse_sweep(c3, c4, 3, HX - 3)


    parents = (couple, jnp.where(lane == 0, NY - 1, lax.div(lane + 1, 2) - 1), lax.div(lane + 1, 2))

    def widen(ref, start, value):
        ref[pl.ds(start, 8, stride=2), :] = value
        ref[pl.ds(start + 1, 8, stride=2), :] = value

    def prolong(x, _):
        for k in range(4):
            for t in range(2):
                widen(grown.at[k, x], TOP + 16 * t, pick(c4[k, x + 3, pl.ds(OWN + 8 * t, 8), :], parents[0]))
        return 0

    def prolong_sides(x, _):
        for k in range(4):
            above = pick(c4[k, x + 3, pl.ds(TOP, 8), :], parents[0])
            grown[k, x, TOP - 1 : TOP, :] = above[DEEP - 1 : DEEP]
            below = pick(c4[k, x + 3, pl.ds(OWN + CZ - DEEP, 8), :], parents[0])
            grown[k, x, TOP + NZ : TOP + NZ + 1, :] = below[DEEP : DEEP + 1]
            for t in range(2):
                value = c4[k, x + 3, pl.ds(OWN + 8 * t, 8), :]
                widen(gprev.at[k, x - 1], 16 * t, pick(value, parents[1]))
                widen(gnext.at[k, x - 1], 16 * t, pick(value, parents[2]))
        return 0

    lax.fori_loop(0, CX + 2, prolong, 0, unroll=True)
    lax.fori_loop(1, CX + 1, prolong_sides, 0, unroll=True)

    def correct(i, _):
        half = lax.div(i + 1, 2)
        for k in range(4):
            for t in range(4):
                rows = pl.ds(TOP + 8 * t, 8)
                u3[k, i, rows, :] = u2[k, i, rows, :] + grown[k, half, rows, :]
            for r in (TOP - 1, TOP + NZ):
                u3[k, i, r : r + 1, :] = u2[k, i, r : r + 1, :] + grown[k, half, r : r + 1, :]
        return 0

    lax.fori_loop(1, NX + 1, correct, 0, unroll=True)
    for i, x in ((0, 0), (NX + 1, CX + 1)):
        for k in range(4):
            for t in range(4):
                rows = pl.ds(TOP + 8 * t, 8)
                u3[k, i, rows, :] = u2[k, i, rows, :] + grown[k, x, rows, :]

    def ends3(k, i, t):
        rows = pl.ds(8 * t, 8)
        half = i // 2 if isinstance(i, int) else lax.div(i, 2)
        return yprev[k, i, rows, :] + gprev[k, half, rows, :], ynext[k, i, rows, :] + gnext[k, half, rows, :]


    wait = exchange(u4, lambda i, t: fine_update(u3, ends3, i, t), ysend.at[2], yrecv.at[2])
    rotate(u4)
    drain()
    wait()
    ends4 = joined_ends(yrecv.at[2, 0], yrecv.at[2, 1])

    def last(i, _):
        for t in range(4):
            new = fine_update(u4, ends4, i, t)
            for k in range(4):
                if k < 3:
                    vout[k, i, pl.ds(8 * t, 8), :] = new[k]
                else:
                    pout[i, pl.ds(8 * t, 8), :] = new[k]
        return 0

    lax.fori_loop(0, NX, last, 0, unroll=True)


def cycle(size, velocity, pressure, viscosity, body_force):
    field = pltpu.VMEM((4, NX + 2, NZ + 16, NY), F32)
    small = pltpu.VMEM((4, HX, HZ + 16, NY), F32)
    anywhere = pl.BlockSpec(memory_space=pl.ANY)

    def deep_buffers(nf):
        return [
            pltpu.VMEM((nf, 2, CZ, NY), F32),
            pltpu.VMEM(((nf + 1) // 2, 8, NY), F32),
            pltpu.VMEM((2, nf, 2, CZ, NY), F32),
            pltpu.VMEM((3, nf, 2, 8, NY), F32),
            pltpu.VMEM((3, 2, (nf + 1) // 2, 8, NY), F32),
            pltpu.VMEM((3, 2, (nf + 1) // 2, 8, NY), F32),
        ]

    out = pl.pallas_call(
        functools.partial(kernel, size),
        out_shape=(
            jax.ShapeDtypeStruct((3, NX, NZ, NY), F32),
            jax.ShapeDtypeStruct((NX, NZ, NY), F32),
        ),
        in_specs=[anywhere] * 4,
        out_specs=(pl.BlockSpec(memory_space=pltpu.VMEM),) * 2,
        scratch_shapes=[
            field, field, field, field, field,
            pltpu.VMEM((NX + 2, NZ + 16, NY), F32),
            pltpu.VMEM((3, NX, NZ, NY), F32),
            pltpu.VMEM((1, HX, HZ + 16, NY), F32),
            small, small, small, small,
            pltpu.VMEM((6, NX, NZ, NY), F32),
            pltpu.VMEM((NX, NZ, NY), F32),
            pltpu.VMEM((NX, NZ, NY), F32),
            pltpu.VMEM((3, NX, NZ, NY), F32),
            pltpu.VMEM((6, HX - 2, HZ, NY), F32),
            pltpu.VMEM((HX - 2, HZ, NY), F32),
            pltpu.VMEM((4, CX, NZ, NY), F32),
            pltpu.VMEM((4, CX + 2, NZ + 16, NY), F32),
            pltpu.VMEM((4, CX, NZ, NY), F32),
            pltpu.VMEM((4, CX, NZ, NY), F32),
            pltpu.VMEM((5, NX, NZ, NY), F32),
            pltpu.VMEM((5, NX, NZ, NY), F32),
            pltpu.VMEM((3, 8, NY), F32),
            pltpu.VMEM((2, 3, 8, NY), F32),
            pltpu.VMEM((3, 2, 8, NY), F32),
            pltpu.VMEM((3, 2, 2, 8, NY), F32),
            *deep_buffers(1),
            *deep_buffers(4),
            pltpu.SemaphoreType.DMA((FACES,)),
            pltpu.SemaphoreType.DMA((FACES,)),
            pltpu.SemaphoreType.DMA((2, len(AROUND))),
            pltpu.SemaphoreType.DMA((2, len(AROUND))),
            pltpu.SemaphoreType.DMA((4,)),
        ],
        compiler_params=pltpu.CompilerParams(collective_id=0, has_side_effects=True, vmem_limit_bytes=25165824),
        name="cycle",
    )(*[pltpu.with_memory_space_constraint(x, pltpu.HBM) for x in (velocity, pressure, viscosity, body_force)])
    return out[0], out[1]


def solution(mesh):
    return jax.shard_map(
        functools.partial(cycle, dict(mesh.shape)),
        mesh=mesh,
        in_specs=(
            P(None, "gx", "gz", "gy"),
            P("gx", "gz", "gy"),
            P("gx", "gz", "gy"),
            P(None, "gx", "gz", "gy"),
        ),
        out_specs=(P(None, "gx", "gz", "gy"), P("gx", "gz", "gy")),
        check_vma=False,
    )
```

```python
import functools
import itertools

import jax
import jax.numpy as jnp
from jax import lax
from jax.experimental import pallas as pl
from jax.experimental.pallas import tpu as pltpu
from jax.sharding import PartitionSpec as P

MESH = pl.DeviceIdType.MESH
F32 = jnp.float32
NX, NZ, NY = 8, 32, 128
CX, CZ = 4, 16
DEEP = 4
HX, HZ = CX + 2 * DEEP, CZ + 2 * DEEP
TOP = 8
OWN = TOP + DEEP
AXES = ("gx", "gy", "gz")
AROUND = sorted(
    (d for d in itertools.product((-1, 0, 1), repeat=3) if any(d)),
    key=lambda d: (d[1:] != (0, 0), -sum(map(abs, d))),
)
FACES = 2 * (2 + 2 + 1 + 3)


def kernel(
    size, vel, prs, vis, frc, vout, pout,
    u0, u1, u2, u3, u4, visc, force, hvisc, c1, c2, c3, c4,
    wts, scl, diag, rhs, cwts, cscl, tmp, grown, gprev, gnext, yprev, ynext,
    ysend0, yrecv0, ysend, yrecv,
    vx, vy, vxb, vzb, vyc, vyz, cx, cy, cxb, czb, cyc, cyz,
    send_sem, recv_sem, deep_send, deep_recv, load_sem,
):
    at = {axis: lax.axis_index(axis) for axis in AXES}
    has = {}
    for axis in AXES:
        has[axis, 1] = at[axis] < size[axis] - 1
        has[axis, -1] = at[axis] > 0
    lane = lax.broadcasted_iota(jnp.int32, (8, NY), 1)
    row = lax.broadcasted_iota(jnp.int32, (8, NY), 0)
    even = lax.rem(lane, 2) == 0
    couple = lax.div(lane, 2)
    nil = jnp.zeros((8, NY), F32)
    count = [0]
    pending = []

    def drain(keep=0):
        while len(pending) > keep:
            pending.pop(0)()

    def roll(value, shift):
        return pltpu.roll(value, shift % NY if isinstance(shift, int) else shift, 1)

    def pick(value, index):
        return jnp.take_along_axis(value, index, axis=1, mode="promise_in_bounds")

    def beside(axis, sign):
        return lax.rem(at[axis] + size[axis] + sign, size[axis])

    def exists(offset, sign=1):
        found = None
        for axis, d in zip(AXES, offset):
            if d:
                one = has[axis, sign * d]
                found = one if found is None else found & one
        return found


    def pair(axis, high_face, low_halo, low_face, high_halo):
        slot = count[0]
        count[0] += 2

        def make(k):
            src, dst, sign = ((high_face, low_halo, 1), (low_face, high_halo, -1))[k]
            return pltpu.make_async_remote_copy(
                src_ref=src, dst_ref=dst,
                send_sem=send_sem.at[slot + k], recv_sem=recv_sem.at[slot + k],
                device_id={axis: beside(axis, sign)}, device_id_type=MESH,
            )

        def each(sign, act):
            @pl.when(has[axis, sign])
            def _():
                act(make(0))

            @pl.when(has[axis, -sign])
            def _():
                act(make(1))

        pending.append(lambda: each(1, lambda c: c.wait_send()))
        return (lambda: each(1, lambda c: c.start())), (lambda: each(-1, lambda c: c.wait_recv()))

    def deep_parts(d, xs, ys, xb, zb, yc, yz):
        dx, dy, dz = d
        if dy == 0 and dz == 0:
            return xs, xb.at[0 if dx > 0 else 1]
        if dy == 0:
            if dz > 0:
                return xs.at[:, :, CZ - DEEP : CZ, :], zb.at[1 - dx, :, :, 0:DEEP, :]
            return xs.at[:, :, 0:DEEP, :], zb.at[1 - dx, :, :, DEEP : 2 * DEEP, :]
        side = 0 if dy > 0 else 1
        if dz == 0:
            return ys, yc.at[1 - dx, side]
        if dz > 0:
            return ys.at[:, DEEP : 2 * DEEP, :], yz.at[1 - dx, side, :, 0:DEEP, :]
        return ys.at[:, 0:DEEP, :], yz.at[1 - dx, side, :, DEEP : 2 * DEEP, :]

    def deep_exchange(which, *refs):
        def make(k):
            d = AROUND[k]
            src, dst = deep_parts(d, *refs)
            return pltpu.make_async_remote_copy(
                src_ref=src, dst_ref=dst,
                send_sem=deep_send.at[k], recv_sem=deep_recv.at[which, k],
                device_id={axis: beside(axis, s) for axis, s in zip(AXES, d) if s}, device_id_type=MESH,
            )

        def each(sign, act, hops=(1, 2, 3)):
            for k, d in enumerate(AROUND):
                if sum(map(abs, d)) in hops:
                    @pl.when(exists(d, sign))
                    def _():
                        act(make(k))

        def start(*hops):
            each(1, lambda c: c.start(), hops)

        pending.append(lambda: each(1, lambda c: c.wait_send()))
        return start, (lambda *hops: each(-1, lambda c: c.wait_recv(), hops))

    zs = pl.ds(TOP, NZ)
    planes = pl.ds(1, NX)

    def x_pair(u):
        return pair("gx", u.at[:, NX, zs, :], u.at[:, 0, zs, :], u.at[:, 1, zs, :], u.at[:, NX + 1, zs, :])

    def z_pair(u):
        return pair(
            "gz", u.at[:, planes, TOP + NZ - 1, :], u.at[:, planes, TOP - 1, :],
            u.at[:, planes, TOP, :], u.at[:, planes, TOP + NZ, :],
        )

    def y_pair(sent, received):
        return pair("gy", sent, received.at[0], sent, received.at[1])


    loads = [
        pltpu.make_async_copy(vel, u0.at[0:3, planes, zs, :], load_sem.at[0]),
        pltpu.make_async_copy(prs, u0.at[3, planes, zs, :], load_sem.at[1]),
        pltpu.make_async_copy(vis, visc.at[planes, zs, :], load_sem.at[2]),
        pltpu.make_async_copy(frc, force, load_sem.at[3]),
    ]
    for load in loads:
        load.start()

    barrier = pltpu.get_barrier_semaphore()
    total = jnp.int32(0)
    for axis in AXES:
        for sign in (1, -1):
            @pl.when(has[axis, sign])
            def _():
                pl.semaphore_signal(barrier, inc=1, device_id={axis: beside(axis, sign)}, device_id_type=MESH)
            total = total + has[axis, sign].astype(jnp.int32)

    def zero(ref):
        ref[...] = jnp.zeros(ref.shape, F32)

    fields = (u0, u1, u2, u4)
    low, high = TOP - 1, TOP + NZ

    def edges(axis, sign, refs):
        @pl.when(jnp.logical_not(has[axis, sign]))
        def _():
            for ref in refs:
                zero(ref)

    edges("gx", -1, [u.at[:, 0, zs, :] for u in fields] + [visc.at[0, zs, :]])
    edges("gx", 1, [u.at[:, NX + 1, zs, :] for u in fields] + [visc.at[NX + 1, zs, :]])
    edges("gz", -1, [u.at[:, planes, low : low + 1, :] for u in fields] + [visc.at[planes, low : low + 1, :]])
    edges("gz", 1, [u.at[:, planes, high : high + 1, :] for u in fields] + [visc.at[planes, high : high + 1, :]])
    edges("gy", -1, [yrecv0.at[0]] + [yrecv.at[s, 0] for s in range(3)])
    edges("gy", 1, [yrecv0.at[1]] + [yrecv.at[s, 1] for s in range(3)])

    for load in loads[:3]:
        load.wait()


    def slot_of(k, i, t):
        return (k % 2) * 32 + t * 8 + i

    def put(pack, value, slot):
        return jnp.where(couple == slot, roll(value, 2 * slot + 1), pack)

    def join(from_low, from_high):
        return jnp.where(even, roll(from_high, NY - 1), roll(from_low, 1))

    def ends(joined, slot):
        return roll(joined, NY - 1 - 2 * slot)

    def y_shifts(k, i, t, end):
        rows = pl.ds(8 * t, 8)
        return jnp.where(lane == 0, end, yprev[k, i, rows, :]), jnp.where(lane == NY - 1, end, ynext[k, i, rows, :])

    def rotate(u, more=None):
        def plane(i, _):
            for t in range(4):
                for k in range(4 if more is None else 5):
                    rows = pl.ds(TOP + 8 * t, 8)
                    value = u[k, i + 1, rows, :] if k < 4 else more[i + 1, rows, :]
                    yprev[k, i, pl.ds(8 * t, 8), :] = roll(value, 1)
                    ynext[k, i, pl.ds(8 * t, 8), :] = roll(value, NY - 1)
            return 0

        lax.fori_loop(0, NX, plane, 0, unroll=2)

    def first_pack(i, packs):
        a, b, c = packs
        for t in range(4):
            rows = pl.ds(TOP + 8 * t, 8)
            a = put(put(a, u0[0, i + 1, rows, :], slot_of(0, i, t)), u0[1, i + 1, rows, :], slot_of(1, i, t))
            b = put(put(b, u0[2, i + 1, rows, :], slot_of(2, i, t)), u0[3, i + 1, rows, :], slot_of(3, i, t))
            c = put(c, visc[i + 1, rows, :], slot_of(0, i, t))
        return a, b, c

    packs = lax.fori_loop(0, NX, first_pack, (nil, nil, nil), unroll=True)
    for n in range(3):
        ysend0[n] = packs[n]

    pl.semaphore_wait(barrier, total)
    first = [
        x_pair(u0),
        pair("gx", visc.at[NX, zs, :], visc.at[0, zs, :], visc.at[1, zs, :], visc.at[NX + 1, zs, :]),
        y_pair(ysend0, yrecv0),
        z_pair(u0),
        pair(
            "gz", visc.at[planes, TOP + NZ - 1, :], visc.at[planes, TOP - 1, :],
            visc.at[planes, TOP, :], visc.at[planes, TOP + NZ, :],
        ),
    ]
    for start, _ in first:
        start()


    doubled = jnp.bitwise_and(2 * lane, NY - 1)
    first_half = lane < NY // 2

    def z_pairs(ref, t):
        return ref[pl.ds(16 * t, 8, stride=2), :] + ref[pl.ds(16 * t + 1, 8, stride=2), :]

    def squeeze(a, b):
        a = a + roll(a, NY - 1)
        b = b + roll(b, NY - 1)
        return jnp.where(first_half, pick(a, doubled), pick(b, doubled))

    octet, fore = lax.div(lane, 2 * DEEP), lax.rem(lane, 2 * DEEP) < DEEP

    def deep_slot(f, pp, t):
        return (f % 2) * 4 + t * 2 + pp

    def deep_pack(xs, ys, nf):
        for n in range((nf + 1) // 2):
            pack = nil
            for f in range(2 * n, min(2 * n + 2, nf)):
                for pp in range(2):
                    for t in range(2):
                        s = deep_slot(f, pp, t)
                        first = fore & (lax.rem(octet, 8) == s)
                        last = jnp.logical_not(fore) & (lax.rem(octet + 1, 8) == s)
                        pack = jnp.where(first | last, roll(xs[f, pp, pl.ds(8 * t, 8), :], 8 * s), pack)
            ys[n] = pack

    def lay_own(value, odd):
        return roll(value, NY // 2) if odd else value

    def near_unpack(h, xs, ys, xb, zb, yc, yz):
        sides = jnp.where(fore, yc[1, 1, 0], yc[1, 0, 0])
        for i in range(CX):
            pp, odd = i // 2, i % 2
            for t in range(2):
                own = lay_own(xs[0, pp, pl.ds(8 * t, 8), :], odd)
                ends_here = roll(sides, NY // 2 - 8 * (deep_slot(0, pp, t) + 8 * odd))
                h[0, CX + i, pl.ds(OWN + 8 * t, 8), :] = jnp.where(first_half, own, ends_here)
            both = lay_own(zb[1, 0, pp], odd)
            h[0, CX + i, pl.ds(TOP, DEEP), :] = both[0:DEEP]
            h[0, CX + i, pl.ds(OWN + CZ, DEEP), :] = both[DEEP : 2 * DEEP]
        for t in range(2):
            rows = pl.ds(8 * t, 8)
            h[0, CX - 1, pl.ds(OWN + 8 * t, 8), :] = lay_own(xb[0, 0, 1, rows, :], 1)
            h[0, 2 * CX, pl.ds(OWN + 8 * t, 8), :] = lay_own(xb[1, 0, 0, rows, :], 0)

    def deep_unpack(h, nf, hops, xs, ys, xb, zb, yc, yz):
        for dx in range(3):
            far = 1 if dx == 1 else 2
            middle, corner = [], []
            for n in range((nf + 1) // 2):
                if far in hops:
                    middle.append(jnp.where(fore, yc[dx, 1, n], yc[dx, 0, n]))
                if far + 1 in hops:
                    value = jnp.where(fore, yz[dx, 1, n], yz[dx, 0, n])
                    corner.append(jnp.where(row < DEEP, roll(value, -4 * DEEP), value))
            block = xs if dx == 1 else xb.at[0 if dx == 0 else 1]

            def lay(value, odd, s, sides):
                return jnp.where(first_half, lay_own(value, odd), roll(sides, NY // 2 - 8 * (s + 8 * odd)))

            for f in range(nf):
                for i in range(CX):
                    pp, odd, x = i // 2, i % 2, dx * CX + i
                    if far in hops:
                        for t in range(2):
                            h[f, x, pl.ds(OWN + 8 * t, 8), :] = lay(
                                block[f, pp, pl.ds(8 * t, 8), :], odd, deep_slot(f, pp, t), middle[f // 2]
                            )
                    if far + 1 in hops:
                        both = lay(zb[dx, f, pp], odd, deep_slot(f, pp, 0), corner[f // 2])
                        h[f, x, pl.ds(TOP, DEEP), :] = both[0:DEEP]
                        h[f, x, pl.ds(OWN + CZ, DEEP), :] = both[DEEP : 2 * DEEP]

    def average(i, _):
        for t in range(4):
            rows = pl.ds(TOP + 8 * t, 8)
            tmp[0, i, pl.ds(8 * t, 8), :] = visc[2 * i + 1, rows, :] + visc[2 * i + 2, rows, :]
        return 0

    lax.fori_loop(0, CX, average, 0, unroll=True)
    for pp in range(2):
        for t in range(2):
            vx[0, pp, pl.ds(8 * t, 8), :] = 0.125 * squeeze(
                z_pairs(tmp.at[0, 2 * pp], t), z_pairs(tmp.at[0, 2 * pp + 1], t)
            )
    deep_pack(vx, vy, 1)
    visc_refs = (vx, vy, vxb, vzb, vyc, vyz)
    flow_refs = (cx, cy, cxb, czb, cyc, cyz)
    for refs in (visc_refs, flow_refs):
        for d in AROUND:
            @pl.when(jnp.logical_not(exists(d, -1)))
            def _():
                zero(deep_parts(d, *refs)[1])

    rotate(u0, visc)
    loads[3].wait()
    for _, wait in first:
        wait()


    def weights(i, _):
        joined = join(yrecv0[0, 2], yrecv0[1, 2])
        for t in range(4):
            r = TOP + 8 * t
            here = visc[i + 1, pl.ds(r, 8), :]
            before, after = y_shifts(4, i, t, ends(joined, slot_of(0, i, t)))
            sums = [here + other for other in (
                visc[i, pl.ds(r, 8), :], visc[i + 2, pl.ds(r, 8), :],
                visc[i + 1, pl.ds(r - 1, 8), :], visc[i + 1, pl.ds(r + 1, 8), :],
                before, after,
            )]
            twice = (sums[0] + sums[1]) + (sums[2] + sums[3]) + (sums[4] + sums[5])
            scale = 0.6 / twice
            rows = pl.ds(8 * t, 8)
            for j in range(6):
                wts[j, i, rows, :] = scale * sums[j]
            scl[i, rows, :] = scale
            diag[i, rows, :] = twice * (0.5 / 0.6)
            for k in range(3):
                rhs[k, i, rows, :] = (2.0 * scale) * force[k, i, rows, :]
        return 0

    lax.fori_loop(0, NX, weights, 0, unroll=True)

    def coarse_weights(x, _):
        for t in range(3):
            r = TOP + 8 * t
            here = hvisc[0, x, pl.ds(r, 8), :]
            sums = [here + other for other in (
                hvisc[0, x - 1, pl.ds(r, 8), :], hvisc[0, x + 1, pl.ds(r, 8), :],
                hvisc[0, x, pl.ds(r - 1, 8), :], hvisc[0, x, pl.ds(r + 1, 8), :],
                roll(here, 1), roll(here, NY - 1),
            )]
            twice = (sums[0] + sums[1]) + (sums[2] + sums[3]) + (sums[4] + sums[5])
            scale = jnp.where(here > 0.0, 0.6 / twice, 0.0)
            rows = pl.ds(8 * t, 8)
            for j in range(6):
                cwts[j, x - 1, rows, :] = scale * sums[j]
            cscl[x - 1, rows, :] = scale
        return 0


    def terms(here, around, sides, grad_scale):
        moves, spread = [], None
        for k in range(3):
            parts = [sides[j] * around[j][k] for j in range(6)]
            total = (parts[0] + parts[1]) + (parts[2] + parts[3]) + (parts[4] + parts[5])
            moves.append(total - grad_scale * (around[2 * k + 1][3] - around[2 * k][3]))
            d = around[2 * k + 1][k] - around[2 * k][k]
            spread = d if spread is None else spread + d
        return moves, spread

    def fine_terms(u, y_of, i, t):
        r = TOP + 8 * t
        rows = pl.ds(8 * t, 8)
        here = [u[k, i + 1, pl.ds(r, 8), :] for k in range(4)]
        ys = [y_of(k, i, t) for k in range(4)]
        around = (
            [u[k, i, pl.ds(r, 8), :] for k in range(4)],
            [u[k, i + 2, pl.ds(r, 8), :] for k in range(4)],
            [u[k, i + 1, pl.ds(r - 1, 8), :] for k in range(4)],
            [u[k, i + 1, pl.ds(r + 1, 8), :] for k in range(4)],
            [y[0] for y in ys],
            [y[1] for y in ys],
        )
        sides = [wts[j, i, rows, :] for j in range(6)]
        moves, spread = terms(here, around, sides, scl[i, rows, :])
        moves = [m + rhs[k, i, rows, :] for k, m in enumerate(moves)]
        return here, moves, spread

    def fine_update(u, y_of, i, t):
        here, moves, spread = fine_terms(u, y_of, i, t)
        new = [0.4 * here[k] + moves[k] for k in range(3)]
        new.append(here[3] - 0.25 * (visc[i + 1, pl.ds(TOP + 8 * t, 8), :] * spread))
        return new

    def joined_ends(low_pack, high_pack):
        joined = [join(low_pack[n], high_pack[n]) for n in range(2)]
        return lambda k, i, t: y_shifts(k, i, t, ends(joined[k // 2], slot_of(k, i, t)))

    def exchange(u, make, sent, received):
        def plane(i, packs):
            packs = list(packs)
            for t in range(4):
                new = make(i, t)
                for k in range(4):
                    u[k, i + 1, pl.ds(TOP + 8 * t, 8), :] = new[k]
                    packs[k // 2] = put(packs[k // 2], new[k], slot_of(k, i, t))
            return tuple(packs)

        packs = plane(NX - 1, plane(0, (nil, nil)))
        x_start, x_wait = x_pair(u)
        x_start()
        packs = lax.fori_loop(1, NX - 1, plane, packs, unroll=3)
        sent[0], sent[1] = packs
        z_start, z_wait = z_pair(u)
        z_start()
        y_start, y_wait = y_pair(sent, received)
        y_start()

        def wait():
            x_wait()
            z_wait()
            y_wait()

        return wait

    ends0 = joined_ends(yrecv0.at[0], yrecv0.at[1])
    wait = exchange(u1, lambda i, t: fine_update(u0, ends0, i, t), ysend.at[0], yrecv.at[0])
    rotate(u1)
    drain(3)
    visc_start, visc_wait = deep_exchange(0, *visc_refs)
    visc_start(1, 2)
    wait()
    visc_start(3)
    ends1 = joined_ends(yrecv.at[0, 0], yrecv.at[0, 1])
    count[0] = 0
    wait = exchange(u2, lambda i, t: fine_update(u1, ends1, i, t), ysend.at[1], yrecv.at[1])
    rotate(u2)
    drain(3)
    visc_wait(1)
    near_unpack(hvisc, *visc_refs)
    lax.fori_loop(CX, 2 * CX, coarse_weights, 0, unroll=2)

    def flat(ref, pp, t):
        rows = pl.ds(DEEP + 8 * t, 8)
        a, b = ref[CX + 2 * pp - 1, rows, :], ref[CX + 2 * pp, rows, :]
        return jnp.where(first_half, a, roll(b, NY // 2))

    scales = [[flat(cscl, pp, t) for t in range(2)] for pp in range(2)]
    wait()


    ends2 = joined_ends(yrecv.at[1, 0], yrecv.at[1, 1])

    def restrict(i, _):
        for t in range(4):
            sums = None
            for h in range(2):
                here, moves, spread = fine_terms(u2, ends2, 2 * i + h, t)
                d = diag[2 * i + h, pl.ds(8 * t, 8), :]
                parts = [d * (moves[k] - 0.6 * here[k]) for k in range(3)] + [spread]
                sums = parts if sums is None else [a + b for a, b in zip(sums, parts)]
            for k in range(4):
                tmp[k, i, pl.ds(8 * t, 8), :] = sums[k]
        return 0

    lax.fori_loop(0, CX, restrict, 0, unroll=True)
    for k in range(4):
        for pp in range(2):
            for t in range(2):
                factor = scales[pp][t] if k < 3 else -0.03125 * vx[0, pp, pl.ds(8 * t, 8), :]
                cx[k, pp, pl.ds(8 * t, 8), :] = factor * squeeze(
                    z_pairs(tmp.at[k, 2 * pp], t), z_pairs(tmp.at[k, 2 * pp + 1], t)
                )
    deep_pack(cx, cy, 4)
    flow_start, flow_wait = deep_exchange(1, *flow_refs)
    flow_start(1, 2, 3)

    def insert_ends(i, _):
        for t in range(4):
            rows = pl.ds(8 * t, 8)
            for k in range(4):
                yprev[k, i, rows, :], ynext[k, i, rows, :] = ends2(k, i, t)
        return 0

    lax.fori_loop(0, NX, insert_ends, 0, unroll=2)
    visc_wait(2, 3)
    deep_unpack(hvisc, 1, (1, 2, 3), *visc_refs)
    lax.fori_loop(1, HX - 1, coarse_weights, 0, unroll=2)
    drain(1)
    for hops in (1, 2, 3):
        flow_wait(hops)
        deep_unpack(c1, 4, (hops,), *flow_refs)

    def coarse_sweep(old, new, start, stop):
        def plane(x, _):
            for t in range(3):
                r = TOP + 8 * t
                rows = pl.ds(8 * t, 8)
                here = [old[k, x, pl.ds(r, 8), :] for k in range(4)]
                around = (
                    [old[k, x - 1, pl.ds(r, 8), :] for k in range(4)],
                    [old[k, x + 1, pl.ds(r, 8), :] for k in range(4)],
                    [old[k, x, pl.ds(r - 1, 8), :] for k in range(4)],
                    [old[k, x, pl.ds(r + 1, 8), :] for k in range(4)],
                    [roll(h, 1) for h in here],
                    [roll(h, NY - 1) for h in here],
                )
                sides = [cwts[j, x - 1, rows, :] for j in range(6)]
                moves, spread = terms(here, around, sides, 2.0 * cscl[x - 1, rows, :])
                source = [c1[k, x, pl.ds(r, 8), :] for k in range(4)]
                for k in range(3):
                    new[k, x, pl.ds(r, 8), :] = 0.4 * here[k] + (moves[k] + source[k])
                new[3, x, pl.ds(r, 8), :] = here[3] + (
                    source[3] - 0.125 * (hvisc[0, x, pl.ds(r, 8), :] * spread)
                )
            return 0

        lax.fori_loop(start, stop, plane, 0, unroll=True)

    coarse_sweep(c1, c2, 1, HX - 1)
    coarse_sweep(c2, c3, 2, HX - 2)
    coarse_sweep(c3, c4, 3, HX - 3)


    parents = (couple, jnp.where(lane == 0, NY - 1, lax.div(lane + 1, 2) - 1), lax.div(lane + 1, 2))

    def widen(ref, start, value):
        ref[pl.ds(start, 8, stride=2), :] = value
        ref[pl.ds(start + 1, 8, stride=2), :] = value

    def prolong(x, _):
        for k in range(4):
            for t in range(2):
                widen(grown.at[k, x], TOP + 16 * t, pick(c4[k, x + 3, pl.ds(OWN + 8 * t, 8), :], parents[0]))
        return 0

    def prolong_sides(x, _):
        for k in range(4):
            above = pick(c4[k, x + 3, pl.ds(TOP, 8), :], parents[0])
            grown[k, x, TOP - 1 : TOP, :] = above[DEEP - 1 : DEEP]
            below = pick(c4[k, x + 3, pl.ds(OWN + CZ - DEEP, 8), :], parents[0])
            grown[k, x, TOP + NZ : TOP + NZ + 1, :] = below[DEEP : DEEP + 1]
            for t in range(2):
                value = c4[k, x + 3, pl.ds(OWN + 8 * t, 8), :]
                widen(gprev.at[k, x - 1], 16 * t, pick(value, parents[1]))
                widen(gnext.at[k, x - 1], 16 * t, pick(value, parents[2]))
        return 0

    lax.fori_loop(0, CX + 2, prolong, 0, unroll=True)
    lax.fori_loop(1, CX + 1, prolong_sides, 0, unroll=True)

    def correct(i, _):
        half = lax.div(i + 1, 2)
        for k in range(4):
            for t in range(4):
                rows = pl.ds(TOP + 8 * t, 8)
                u3[k, i, rows, :] = u2[k, i, rows, :] + grown[k, half, rows, :]
            for r in (TOP - 1, TOP + NZ):
                u3[k, i, r : r + 1, :] = u2[k, i, r : r + 1, :] + grown[k, half, r : r + 1, :]
        return 0

    lax.fori_loop(1, NX + 1, correct, 0, unroll=True)
    for i, x in ((0, 0), (NX + 1, CX + 1)):
        for k in range(4):
            for t in range(4):
                rows = pl.ds(TOP + 8 * t, 8)
                u3[k, i, rows, :] = u2[k, i, rows, :] + grown[k, x, rows, :]

    def ends3(k, i, t):
        rows = pl.ds(8 * t, 8)
        half = i // 2 if isinstance(i, int) else lax.div(i, 2)
        return yprev[k, i, rows, :] + gprev[k, half, rows, :], ynext[k, i, rows, :] + gnext[k, half, rows, :]


    count[0] = FACES - 6
    wait = exchange(u4, lambda i, t: fine_update(u3, ends3, i, t), ysend.at[2], yrecv.at[2])
    rotate(u4)
    drain()
    wait()
    ends4 = joined_ends(yrecv.at[2, 0], yrecv.at[2, 1])

    def last(i, _):
        for t in range(4):
            new = fine_update(u4, ends4, i, t)
            for k in range(4):
                if k < 3:
                    vout[k, i, pl.ds(8 * t, 8), :] = new[k]
                else:
                    pout[i, pl.ds(8 * t, 8), :] = new[k]
        return 0

    lax.fori_loop(0, NX, last, 0, unroll=True)


def cycle(size, velocity, pressure, viscosity, body_force):
    field = pltpu.VMEM((4, NX + 2, NZ + 16, NY), F32)
    small = pltpu.VMEM((4, HX, HZ + 16, NY), F32)
    anywhere = pl.BlockSpec(memory_space=pl.ANY)

    def deep_buffers(nf):
        return [
            pltpu.VMEM((nf, 2, CZ, NY), F32),
            pltpu.VMEM(((nf + 1) // 2, 8, NY), F32),
            pltpu.VMEM((2, nf, 2, CZ, NY), F32),
            pltpu.VMEM((3, nf, 2, 8, NY), F32),
            pltpu.VMEM((3, 2, (nf + 1) // 2, 8, NY), F32),
            pltpu.VMEM((3, 2, (nf + 1) // 2, 8, NY), F32),
        ]

    out = pl.pallas_call(
        functools.partial(kernel, size),
        out_shape=(
            jax.ShapeDtypeStruct((3, NX, NZ, NY), F32),
            jax.ShapeDtypeStruct((NX, NZ, NY), F32),
        ),
        in_specs=[anywhere] * 4,
        out_specs=(pl.BlockSpec(memory_space=pltpu.VMEM),) * 2,
        scratch_shapes=[
            field, field, field, field, field,
            pltpu.VMEM((NX + 2, NZ + 16, NY), F32),
            pltpu.VMEM((3, NX, NZ, NY), F32),
            pltpu.VMEM((1, HX, HZ + 16, NY), F32),
            small, small, small, small,
            pltpu.VMEM((6, NX, NZ, NY), F32),
            pltpu.VMEM((NX, NZ, NY), F32),
            pltpu.VMEM((NX, NZ, NY), F32),
            pltpu.VMEM((3, NX, NZ, NY), F32),
            pltpu.VMEM((6, HX - 2, HZ, NY), F32),
            pltpu.VMEM((HX - 2, HZ, NY), F32),
            pltpu.VMEM((4, CX, NZ, NY), F32),
            pltpu.VMEM((4, CX + 2, NZ + 16, NY), F32),
            pltpu.VMEM((4, CX, NZ, NY), F32),
            pltpu.VMEM((4, CX, NZ, NY), F32),
            pltpu.VMEM((5, NX, NZ, NY), F32),
            pltpu.VMEM((5, NX, NZ, NY), F32),
            pltpu.VMEM((3, 8, NY), F32),
            pltpu.VMEM((2, 3, 8, NY), F32),
            pltpu.VMEM((3, 2, 8, NY), F32),
            pltpu.VMEM((3, 2, 2, 8, NY), F32),
            *deep_buffers(1),
            *deep_buffers(4),
            pltpu.SemaphoreType.DMA((FACES,)),
            pltpu.SemaphoreType.DMA((FACES,)),
            pltpu.SemaphoreType.DMA((len(AROUND),)),
            pltpu.SemaphoreType.DMA((2, len(AROUND))),
            pltpu.SemaphoreType.DMA((4,)),
        ],
        compiler_params=pltpu.CompilerParams(collective_id=0, has_side_effects=True, vmem_limit_bytes=25165824),
        name="cycle",
    )(*[pltpu.with_memory_space_constraint(x, pltpu.HBM) for x in (velocity, pressure, viscosity, body_force)])
    return out[0], out[1]


def solution(mesh):
    return jax.shard_map(
        functools.partial(cycle, dict(mesh.shape)),
        mesh=mesh,
        in_specs=(
            P(None, "gx", "gz", "gy"),
            P("gx", "gz", "gy"),
            P("gx", "gz", "gy"),
            P(None, "gx", "gz", "gy"),
        ),
        out_specs=(P(None, "gx", "gz", "gy"), P("gx", "gz", "gy")),
        check_vma=False,
    )
```
